32 devices in a mesh: fsdp: 8 (over z, y), dp: 4 (over x, core).
Axes of the slice: x: 2, y: 2, z: 4, core: 2. Of those that a mesh axis runs over, the one named last changes fastest.
Arguments:
- byte_ids: int32 [64, 1024], P(('fsdp', 'dp')), may hold values from 0 to 255
- doc_lengths: int32 [64, 8], P(('fsdp', 'dp')), may hold values from 1 to 512, 1024 in all within a row
- pad_mask: int32 [64, 1024], P(('fsdp', 'dp')), may hold values from 0 to 1, as said below
- embedding: bfloat16 [256, 768], P(None, 'fsdp'), may hold values from -6 to 6
- conv_weight: bfloat16 [5, 768, 768], P(None, 'fsdp'), may hold values from -0.09375 to 0.09375
- conv_bias: bfloat16 [768], P('fsdp'), may hold values from -3 to 3
- scorer: bfloat16 [768], P('fsdp'), may hold values from -0.3125 to 0.3125
- cotangent: bfloat16 [64, 512, 768], P(('fsdp', 'dp')), may hold values from -6 to 6
- aux_weight: float32 [], replicated, may hold values from 8192 to 16384
Outputs:
- blocks: bfloat16 [64, 512, 768], P(('fsdp', 'dp'))
- loss: float32 [], replicated
- emb_grad: float32 [256, 768], P(None, 'fsdp')
- conv_grad: float32 [5, 768, 768], P(None, 'fsdp')
- bias_grad: float32 [768], P('fsdp')
- score_grad: float32 [768], P('fsdp')
The draws below stay inside these ranges and needn't reach their ends.
Inputs may be any that keep to these rules, and one draw needn't show every extreme that they name: `doc_lengths`: each row's 8 document lengths sum to 1024; the longest document of a row is 512 long. `pad_mask`: in every row the real bytes come first and padding follows; every row holds 256 or more real bytes.
All inputs are finite; a program needn't handle non-finite values.
Results may differ from the reference program's by a relative error of at most 0.0046.
Values may be sent and summed in bfloat16 or wider, within the bound.
A program may use at most 320 MiB of HBM per device.

```python
import math
import jax
import jax.numpy as jnp
import numpy as np
from jax import lax

D = 768
V = 256
TAPS = 5
SIZES = 4
L = 1024
SEGS = 8
ROWS = 64
BLOCKS = 512


def draw_pad_mask(key, part):
    row_index = jnp.arange(ROWS, dtype=jnp.int32)[:, None]
    places = jnp.arange(L, dtype=jnp.int32)[None, :]
    base_count = L // 3 + (L - L // 3) * row_index // max(ROWS - 1, 1)
    cut_count = jax.random.randint(key, (ROWS, 1), 0, L // 16 + 1, dtype=jnp.int32)
    real_count = jnp.maximum(base_count - cut_count, L // 4)
    return (places < real_count).astype(jnp.int32)


def with_ends(drawn, own_key, low, largest):
    place = [jax.random.randint(jax.random.fold_in(own_key, axis), (), 0, length) for axis, length in enumerate(drawn.shape)]
    longest = drawn.shape.index(max(drawn.shape))
    next_to = place[:longest] + [(place[longest] + 1) % drawn.shape[longest]] + place[longest + 1:]
    return drawn.at[tuple(place)].set(low).at[tuple(next_to)].set(largest)


def block_levels(rng, shape, split, low, largest):
    factor_of = 1.0
    for axis_at, blocks in split:
        heights = jax.random.uniform(jax.random.fold_in(jax.random.fold_in(rng, 6), axis_at), (blocks,), jnp.float32, low / len(split), largest / len(split))
        factor_of = factor_of * jnp.repeat(jnp.exp(heights), shape[axis_at] // blocks).reshape((-1,) + (1,) * (len(shape) - 1 - axis_at))
    return factor_of


def cumulative_ranks(number_of, lean):
    loads = [(1 << 20) // math.isqrt(standing ** lean) + 1 for standing in range(1, number_of + 1)]
    spread = 1 + sum(loads) // (1 << 30)
    return np.cumsum(np.array([max(1, weight // spread) for weight in loads]))


def ranked(stream_key, shape, count, lean):
    table = cumulative_ranks(count, lean)
    ticket = jax.random.randint(jax.random.fold_in(stream_key, 1), shape, 0, int(table[count - 1]))
    rank = jnp.searchsorted(jnp.asarray(table, jnp.int32), ticket, side="right")
    return jax.random.permutation(jax.random.fold_in(stream_key, 2), count)[rank].astype(jnp.int32)


def length_profile(number_of, total, limit, skew):
    portions = [(1 << 20) // math.isqrt(standing ** skew) + 1 for standing in range(2, number_of + 1)]
    rest, given = total - limit - (number_of - 1), [1] * (number_of - 1)
    while rest > 0:
        movable = [i for i in range(number_of - 1) if given[i] < limit]
        pool, left = sum([portions[i] for i in movable]), rest
        for i in movable:
            more = min(limit - given[i], max(1, left * portions[i] // pool), rest)
            given[i] = given[i] + more
            rest = rest - more
    return np.array([limit] + given)


def ragged_sizes(rng, number_of, total, most, slope):
    if number_of == 2:
        one = jax.random.randint(rng, (), max(1, total - most), min(most, total - 1) + 1)
        return jnp.stack([one, total - one])
    sizes = jnp.asarray(length_profile(number_of, total, most, slope), jnp.int32)
    pairs = (number_of - 1) // 2
    source_of, sink = sizes[1:1 + 2 * pairs:2], sizes[2:2 + 2 * pairs:2]
    room = jnp.minimum(source_of - 1, most - sink)
    passed = jax.random.randint(jax.random.fold_in(rng, 1), (pairs,), 0, 1 << 20) % (room + 1)
    sizes = sizes.at[1:1 + 2 * pairs:2].set(source_of - passed).at[2:2 + 2 * pairs:2].set(sink + passed)
    return sizes[jax.random.permutation(jax.random.fold_in(rng, 2), number_of)]


def noise(stream_key, extent, scale, limit, split=(), kind=jnp.bfloat16):
    loudness = block_levels(stream_key, extent, split, -0.22, 0.18) if split else 1.0
    entries = jax.random.normal(stream_key, extent, jnp.float32) * scale * loudness
    return jnp.minimum(jnp.maximum(entries, -limit), limit).astype(kind)


def setup_inputs(seed: int = 0) -> dict:
    splits = jax.random.split(jax.random.key(seed), 10)
    byte_ids = with_ends(ranked(splits[0], (ROWS, L), V, 2), jax.random.fold_in(splits[0], 3), 0, V - 1).astype(jnp.int32)
    doc_lengths = jax.vmap(lambda own: ragged_sizes(own, SEGS, L, L // 2, 2))(jax.random.split(splits[1], ROWS)).reshape((ROWS, SEGS)).astype(jnp.int32)
    pad_mask = draw_pad_mask(jax.random.fold_in(splits[9], 71), 0)
    embedding = noise(splits[3], (V, D), 1.0, 6.0, ((1, 8),))
    conv_weight = noise(splits[4], (TAPS, D, D), (TAPS * D) ** -0.5, 0.09375, ((1, 8),))
    conv_bias = noise(splits[5], (D,), 0.5, 3.0, ((0, 8),))
    scorer = noise(splits[6], (D,), (D // 2) ** -0.5, 0.3125, ((0, 8),))
    cotangent = noise(splits[7], (ROWS, BLOCKS, D), 1.0, 6.0, ((0, 32),))
    aux_weight = jnp.clip(jax.random.uniform(splits[8], (), jnp.float32, 8192.0, 16384.0), 8192.0, 16384.0)
    return dict(byte_ids=byte_ids, doc_lengths=doc_lengths, pad_mask=pad_mask, embedding=embedding, conv_weight=conv_weight, conv_bias=conv_bias, scorer=scorer, cotangent=cotangent, aux_weight=aux_weight)


@jax.custom_vjp
def low(v):
    return lax.optimization_barrier(v.astype(jnp.bfloat16)).astype(jnp.float32)

@jax.custom_vjp
def low_back(v):
    return v

def low_keep(v):
    return (low(v), None)

def low_pass(kept, grad):
    return (grad,)

def back_keep(v):
    return (v, None)

def back_low(kept, grad):
    return (low(grad),)
low.defvjp(low_keep, low_pass)
low_back.defvjp(back_keep, back_low)

def segment_ids(length_row, length):
    ends = jnp.cumsum(length_row, axis=-1)
    places = jnp.arange(length, dtype=jnp.int32)
    return lax.optimization_barrier(jnp.sum((places[:, None] >= ends[None, :]).astype(jnp.int32), axis=1))

def partner_same(segment, offset):
    length = segment.shape[-1]
    places = jnp.arange(length, dtype=jnp.int32)
    inside = (places + offset >= 0) & (places + offset < length)
    return inside & (jnp.roll(segment, -offset, axis=-1) == segment)

def latent_row(hidden, scorer_input_rows, segment, real_mask):
    length = hidden.shape[0]
    places = jnp.arange(length, dtype=jnp.int32)
    mean_list = []
    for block_size in range(1, SIZES + 1):
        member_sum = jnp.zeros_like(hidden)
        member_count = jnp.zeros((length,), jnp.float32)
        for offset in range(1 - block_size, block_size):
            member = partner_same(segment, offset) & ((places + offset) // block_size == places // block_size)
            weight_here = member.astype(jnp.float32) * jnp.roll(real_mask, -offset)
            member_sum = member_sum + jnp.roll(hidden, -offset, axis=0) * weight_here[:, None]
            member_count = member_count + weight_here
        mean_list.append(member_sum / jnp.maximum(member_count, 1.0)[:, None])
    block_average_values = jnp.stack(mean_list)
    block_score_rows = jnp.einsum('agn,n->ga', block_average_values, scorer_input_rows, precision=lax.Precision.HIGHEST)
    similar = jnp.dot(block_score_rows, block_score_rows.T, precision=lax.Precision.HIGHEST)
    allowed = (segment[:, None] == segment[None, :]) & (real_mask[None, :] > 0.5) | (places[:, None] == places[None, :])
    similar = jnp.where(allowed, similar, -1000000000.0)
    top_similar = lax.optimization_barrier(jnp.max(similar, axis=1, keepdims=True))
    power_term = jnp.exp(similar - top_similar)
    attention = power_term / lax.optimization_barrier(jnp.sum(power_term, axis=1, keepdims=True))
    calibrated = jnp.dot(attention, block_score_rows, precision=lax.Precision.HIGHEST)
    log_weight = jax.nn.log_softmax(calibrated, axis=1)
    block_size_weight = jnp.exp(log_weight)
    entropy = -lax.optimization_barrier(jnp.sum(block_size_weight * log_weight, axis=1))
    hidden_state_rows = jnp.einsum('ue,euh->uh', block_size_weight, block_average_values, precision=lax.Precision.HIGHEST)
    uneven_location = places % 2 == 1
    pair_weight = real_mask * jnp.where(uneven_location, jnp.roll(segment, 1) == segment, True).astype(jnp.float32)
    pooled = (hidden_state_rows * pair_weight[:, None]).reshape(length // 2, 2, -1).sum(axis=1)
    pair_count = pair_weight.reshape(length // 2, 2).sum(axis=1)
    return (pooled / jnp.maximum(pair_count, 1.0)[:, None], jnp.sum(real_mask * entropy))

def row_forward(params, byte_row, length_row, mask_row):
    emb_table, conv_table, bias_vector, scorer_vector = params
    segment = segment_ids(length_row, L)
    real_mask = mask_row.astype(jnp.float32)
    inputs = low_back(emb_table[byte_row] * real_mask[:, None])
    tap_list = []
    for tap_index in range(TAPS):
        offset = tap_index - TAPS // 2
        keep = partner_same(segment, offset).astype(jnp.float32)
        tap_list.append(jnp.roll(inputs, -offset, axis=0) * keep[:, None])
    stacked = jnp.concatenate(tap_list, axis=1)
    hidden = jnp.dot(stacked, conv_table.reshape(TAPS * D, D), precision=lax.Precision.HIGHEST) + bias_vector
    hidden = low_back(hidden)
    return latent_row(hidden, scorer_vector, segment, real_mask)

def reference(byte_ids, doc_lengths, pad_mask, embedding, conv_weight, conv_bias, scorer, cotangent, aux_weight):
    params = (embedding.astype(jnp.float32), conv_weight.astype(jnp.float32), conv_bias.astype(jnp.float32), scorer.astype(jnp.float32))
    count = jnp.sum(pad_mask.astype(jnp.float32))
    checked_row = jax.checkpoint(row_forward)

    def forward(weights_in):

        def one_row(carry, row_inputs):
            pooled_row, entropy_row = checked_row(weights_in, row_inputs[0], row_inputs[1], row_inputs[2])
            return (carry + entropy_row, pooled_row)
        entropy_total, pooled = lax.scan(one_row, jnp.zeros((), jnp.float32), (byte_ids, doc_lengths, pad_mask))
        return (pooled, entropy_total)
    (pooled, entropy_total), pullback = jax.vjp(forward, params)
    grads = pullback((cotangent.astype(jnp.float32), aux_weight / count))[0]
    return (pooled.astype(jnp.bfloat16), entropy_total / count, grads[0], grads[1], grads[2], grads[3])
```

```python
import functools
import jax
import jax.numpy as jnp
from jax import lax
from jax.experimental import pallas as pl
from jax.experimental.pallas import tpu as pltpu
from jax.sharding import PartitionSpec as P

TAPS = 5
SIZES = 4
NEG = -1000000000.0
F32 = jnp.float32
BF16 = jnp.bfloat16
TILE = 256
EDGE = 16


def split2(x):
    high = x.astype(BF16).astype(F32)
    return high, x - high


def shift(x, offset):
    length = x.shape[1]
    return x if offset == 0 else pltpu.roll(x, (-offset) % length, 1)


def group_pair(x, step, lane_bit):
    size = x.shape[0]
    down = pltpu.roll(x, (size - step) % size, 0)
    up = pltpu.roll(x, step, 0)
    return jnp.where(lane_bit, up, down)


def group_all(x, op, bits):
    x = op(x, group_pair(x, 1, bits[0]))
    return op(x, group_pair(x, 2, bits[1]))


def spread(rows_list, length):
    return jnp.concatenate([jnp.broadcast_to(x, (SIZES, length)) for x in rows_list], axis=0)


def lane_rows(ref, at, r, length):
    return ref[at : at + 1, r * length : (r + 1) * length]


DELTA_EVEN = {-3: -2, -2: -1, -1: -1, 0: 0, 1: 0, 2: 1, 3: 1}
DELTA_ODD = {-3: -1, -2: -1, -1: 0, 0: 0, 1: 1, 2: 1, 3: 2}
OFFSETS = [o for o in range(1 - SIZES, SIZES) if o != 0]


def row_masks(rows, length, len_ref, ids_ref, mask_ref, taps_s):
    place1 = lax.broadcasted_iota(jnp.int32, (1, length), 1)
    seg_list, real_list = [], []
    for r in range(rows):
        end = len_ref[r, 0]
        segment = jnp.where(place1 >= end, 1.0, 0.0)
        for d in range(1, len_ref.shape[1]):
            end = end + len_ref[r, d]
            segment = segment + jnp.where(place1 >= end, 1.0, 0.0)
        seg_list.append(segment)
        real_list.append(mask_ref[r : r + 1, :].astype(F32))
        ids = ids_ref[r : r + 1, :].astype(F32)
        known = jnp.where(real_list[r] > 0.5, ids, -1.0)
        for k in range(TAPS):
            o = k - TAPS // 2
            inside = (place1 + o >= 0) & (place1 + o < length)
            keep = inside & (shift(segment, o) == segment)
            taps_s[k : k + 1, r * length : (r + 1) * length] = jnp.where(
                keep, shift(known, o), -1.0
            ).astype(jnp.int32)
    return seg_list, real_list


def fill_onehot(count, vocab, taps_s, onehot_s):
    symbol = lax.broadcasted_iota(jnp.int32, (vocab, TILE), 0)

    def step(t, carry):
        lanes = pl.ds(pl.multiple_of(t * TILE, TILE), TILE)
        for k in range(TAPS):
            here = taps_s[k : k + 1, lanes]
            onehot_s[k * vocab : (k + 1) * vocab, lanes] = jnp.where(symbol == here, 1.0, 0.0).astype(BF16)
        return carry

    lax.fori_loop(0, count, step, 0)


def members_of(rows, length, seg_list, real_list):
    shape = (rows * SIZES, length)
    place = lax.broadcasted_iota(jnp.int32, shape, 1)
    sub = lax.broadcasted_iota(jnp.int32, shape, 0)
    size = (sub & (SIZES - 1)) + 1
    third = jnp.floor((place.astype(F32) + 0.5) * (1.0 / 3.0)).astype(jnp.int32)
    within = jnp.where(
        size == 1, 0, jnp.where(size == 2, place & 1, jnp.where(size == 3, place - 3 * third, place & 3))
    )
    seg = spread(seg_list, length)
    real = spread(real_list, length)
    same = {}
    for o in range(1, SIZES):
        ahead = (within + o < size) & (place + o < length) & (shift(seg, o) == seg)
        behind = (within - o >= 0) & (shift(seg, -o) == seg)
        same[o] = jnp.where(ahead, 1.0, 0.0)
        same[-o] = jnp.where(behind, 1.0, 0.0)
    member = {o: same[o] * shift(real, o) for o in OFFSETS}
    members = real
    for o in OFFSETS:
        members = members + member[o]
    even = (place & 1) == 0
    pair = jnp.where(even | (shift(seg, -1) == seg), real, 0.0)
    partner = jnp.where(even, shift(pair, 1), shift(pair, -1))
    return dict(
        bits=((sub & 1) == 1, (sub & 2) == 2),
        first=size == 1,
        even=even,
        real=real,
        same=same,
        member=member,
        inverse=1.0 / jnp.maximum(members, 1.0),
        pair_weight=pair / jnp.maximum(pair + partner, 1.0),
    )


def block_scores(rows, length, m, q_s):
    q = spread([lane_rows(q_s, 0, r, length) for r in range(rows)], length)
    total = q * m["real"]
    for o in OFFSETS:
        total = total + m["member"][o] * shift(q, o)
    return total * m["inverse"]


def calibrate_row(r, length, scores, seg, real, similar_s, probs_s, between):
    s = scores[r * SIZES : (r + 1) * SIZES]
    a, rest = split2(s)
    b, c = split2(rest)
    key_seg = jnp.where(real > 0.5, seg, -1.0)
    zero = jnp.zeros((128 - 6 * SIZES - 1, length), F32)
    left = jnp.concatenate([a, a, b, b, a, c, key_seg, zero], axis=0).T
    right = jnp.concatenate([a, b, a, b, c, a, jnp.zeros_like(key_seg), zero], axis=0).astype(BF16)
    key_column = left[:, 6 * SIZES : 6 * SIZES + 1]
    left = left.astype(BF16)
    x = jnp.concatenate(
        [jnp.ones((1, length), F32), s, s[0:1] * s, s[1:2] * s[1:], s[2:3] * s[2:], s[3:4] * s[3:]]
        + [jnp.zeros((1, length), F32)],
        axis=0,
    )
    x_high, x_low = split2(x)
    features = jnp.concatenate([x_high, x_low], axis=0).astype(BF16)
    outs = []
    for t in range(length // TILE):
        lanes = slice(t * TILE, (t + 1) * TILE)
        query_seg = seg[:, lanes]
        top = None
        for j in range(length // 128):
            keys = slice(j * 128, (j + 1) * 128)
            sim = jnp.dot(left[keys], right[:, lanes], preferred_element_type=F32)
            allowed = key_column[keys] == query_seg
            if j * 128 // TILE == t:
                key_place = lax.broadcasted_iota(jnp.int32, (128, TILE), 0) + j * 128
                query_place = lax.broadcasted_iota(jnp.int32, (128, TILE), 1) + t * TILE
                allowed = allowed | (key_place == query_place)
            sim = jnp.where(allowed, sim, NEG)
            similar_s[keys, :] = sim
            here = jnp.max(sim, axis=0, keepdims=True)
            top = here if top is None else jnp.maximum(top, here)
        for j in range(length // 128):
            keys = slice(j * 128, (j + 1) * 128)
            probs_s[r, keys, lanes] = jnp.exp(similar_s[keys, :] - top).astype(BF16)
        outs.append(jnp.dot(features, probs_s[r, :, lanes], preferred_element_type=F32))
        between(r, t)
    moments = jnp.concatenate(outs, axis=1)
    moments = moments[0:16] + moments[16:32]
    norm = 1.0 / moments[0:1]
    return moments * norm, norm


def size_softmax(cal, bits):
    top = group_all(cal, jnp.maximum, bits)
    log_weight = (cal - top) - jnp.log(group_all(jnp.exp(cal - top), jnp.add, bits))
    weight = jnp.exp(log_weight)
    entropy = -group_all(weight * log_weight, jnp.add, bits)
    return weight, log_weight, entropy


def band_products(rows, length, cot_s, hidden_s, band_s, window):
    kl = lax.broadcasted_iota(jnp.int32, (window, TILE), 0)
    jl = lax.broadcasted_iota(jnp.int32, (window, TILE), 1) // 2 + EDGE
    diagonal = kl - jl
    for r in range(rows):
        for t in range(length // TILE):
            lanes = slice(r * length + t * TILE, r * length + (t + 1) * TILE)
            first = t * TILE // 2
            prod = jnp.dot(
                cot_s[r, first : first + window, :], hidden_s[:, lanes], preferred_element_type=F32
            )
            for d in range(-2, 3):
                band_s[d + 2 : d + 3, lanes] = jnp.sum(jnp.where(diagonal == d, prod, 0.0), axis=0, keepdims=True)
    return diagonal


def calibrate_back(r, length, scores, cal_grad, inner, moments, norm, probs_s):
    part = slice(r * SIZES, (r + 1) * SIZES)
    s, g, ri = scores[part], cal_grad[part], inner[r * SIZES : r * SIZES + 1]
    at = {}
    n = 1 + SIZES
    for a in range(SIZES):
        for b in range(a, SIZES):
            at[a, b] = at[b, a] = n
            n += 1
    query = []
    for a in range(SIZES):
        total = -moments[1 + a : 2 + a] * ri
        for b in range(SIZES):
            total = total + moments[at[a, b] : at[a, b] + 1] * g[b : b + 1]
        query.append(total)
    y = jnp.concatenate([g - s * ri] + [s[a : a + 1] * g for a in range(SIZES)], axis=0) * norm
    y = jnp.concatenate([y, jnp.zeros((4, length), F32)], axis=0)
    y_high, y_low = split2(y)
    features = jnp.concatenate([y_high, y_low], axis=0).astype(BF16)
    outs = []
    for t in range(length // TILE):
        keys = slice(t * TILE, (t + 1) * TILE)
        outs.append(
            lax.dot_general(features, probs_s[r, keys, :], (((1,), (1,)), ((), ())), preferred_element_type=F32)
        )
    back = jnp.concatenate(outs, axis=1)
    back = back[0:24] + back[24:48]
    key = []
    for a in range(SIZES):
        total = back[a : a + 1]
        for b in range(SIZES):
            n = SIZES + a * SIZES + b
            total = total + s[b : b + 1] * back[n : n + 1]
        key.append(total + query[a])
    return jnp.concatenate(key, axis=0)


def middle(dims, m, scores, seg_list, real_list, scale, scorer, refs, between):
    rows, length, width, vocab = dims
    half = length // 2
    tiles = length // TILE
    window = TILE // 2 + 2 * EDGE
    hidden_s, cot_s, band_s, pooled_s, hgrad_s, probs_s, similar_s, blocks_ref, part_ref, late_hidden = refs
    bits, real, same, member, inverse, pair_weight = (
        m[n] for n in ("bits", "real", "same", "member", "inverse", "pair_weight")
    )
    kept = [
        calibrate_row(r, length, scores, seg_list[r], real_list[r], similar_s, probs_s, between) for r in range(rows)
    ]
    cal = jnp.concatenate([moments[1 : 1 + SIZES] for moments, norm in kept], axis=0)
    weight, log_weight, entropy = size_softmax(cal, bits)
    entropy_sum = jnp.sum(
        jnp.sum(jnp.where(m["first"], entropy * real, 0.0), axis=1, keepdims=True), axis=0, keepdims=True
    )
    part_ref[...] = jnp.zeros_like(part_ref)
    part_ref[1:2, :] = jnp.broadcast_to(entropy_sum, (1, width))
    for r in range(rows):
        pooled_s[r] = jnp.zeros_like(pooled_s[r])

    late_hidden()
    diagonal = band_products(rows, length, cot_s, hidden_s, band_s, window)
    even1 = (lax.broadcasted_iota(jnp.int32, (1, length), 1) & 1) == 0
    band = [[lane_rows(band_s, d + 2, r, length) for d in range(-2, 3)] for r in range(rows)]

    def product(o):
        return spread(
            [jnp.where(even1, band[r][DELTA_EVEN[o] + 2], band[r][DELTA_ODD[o] + 2]) for r in range(rows)], length
        )

    gathered = real * product(0)
    for o in OFFSETS:
        gathered = gathered + member[o] * shift(product(-o), o)
    weight_grad = pair_weight * inverse * gathered
    cal_grad = weight * (weight_grad - group_all(weight * weight_grad, jnp.add, bits))
    cal_grad = cal_grad - scale() * real * weight * (log_weight + entropy)
    inner = group_all(cal * cal_grad, jnp.add, bits)
    score_grad = jnp.concatenate(
        [calibrate_back(r, length, scores, cal_grad, inner, kept[r][0], kept[r][1], probs_s) for r in range(rows)],
        axis=0,
    )
    score_grad = score_grad * inverse
    q_grad = score_grad
    for o in OFFSETS:
        q_grad = q_grad + same[o] * shift(score_grad, o)
    q_grad = group_all(q_grad * real, jnp.add, bits)

    use = pair_weight * weight * inverse
    moved = {o: (use if o == 0 else same[o] * shift(use, o)) for o in range(1 - SIZES, SIZES)}
    mix = []
    for d in range(-2, 3):
        odd_sum = sum([moved[o] for o in moved if DELTA_ODD[o] == d], jnp.zeros_like(use))
        even_sum = sum([moved[o] for o in moved if DELTA_EVEN[o] == d], jnp.zeros_like(use))
        mix.append(group_all(jnp.where(m["even"], even_sum, odd_sum) * real, jnp.add, bits))

    scorer16 = jnp.concatenate([scorer, scorer, jnp.zeros((EDGE - 2, width), BF16)], axis=0)
    for r in range(rows):
        at = r * SIZES
        q_high, q_low = split2(q_grad[at : at + 1])
        for t in range(tiles):
            lanes = slice(t * TILE, (t + 1) * TILE)
            all_lanes = slice(r * length + t * TILE, r * length + (t + 1) * TILE)
            first = t * TILE // 2
            matrix = jnp.zeros((window, TILE), F32)
            for d in range(-2, 3):
                matrix = jnp.where(diagonal == d, mix[d + 2][at : at + 1, lanes], matrix)
            high, low = split2(matrix)
            matrix = jnp.concatenate(
                [high, low, q_high[:, lanes], q_low[:, lanes], jnp.zeros((EDGE - 2, TILE), F32)], axis=0
            ).astype(BF16)
            out = lax.dot_general(
                matrix, hidden_s[:, all_lanes], (((1,), (1,)), ((), ())), preferred_element_type=F32
            )
            pooled_s[r, first : first + window, :] += out[:window] + out[window : 2 * window]
            part_ref[0:1, :] += out[2 * window : 2 * window + 1] + out[2 * window + 1 : 2 * window + 2]
            here = cot_s[r, first : first + window, :]
            given = jnp.concatenate([here, here, scorer16], axis=0)
            hgrad_s[all_lanes, :] = lax.dot_general(
                matrix, given, (((0,), (0,)), ((), ())), preferred_element_type=F32
            ).astype(BF16)
        blocks_ref[r] = pooled_s[r, EDGE : EDGE + half, :].astype(BF16)


def fill_cotangent(rows, half, width, cot_ref, cot_s):
    cot_s[:, 0:EDGE, :] = jnp.zeros((rows, EDGE, width), BF16)
    cot_s[:, EDGE + half :, :] = jnp.zeros((rows, EDGE, width), BF16)
    for r in range(rows):
        cot_s[r, EDGE : EDGE + half, :] = cot_ref[r]


def fill_q(count, tq16, const, onehot_s, q_s):
    def step(t, carry):
        lanes = pl.ds(pl.multiple_of(t * TILE, TILE), TILE)
        got = jnp.dot(tq16, onehot_s[:, lanes], preferred_element_type=F32)
        q_s[0:1, lanes] = got[0:1] + got[1:2] + got[2:3] + const
        return carry

    lax.fori_loop(0, count, step, 0)


def fill_hidden(count, table, bias_column, onehot_s, hidden_s):
    def step(t, carry):
        lanes = pl.ds(pl.multiple_of(t * TILE, TILE), TILE)
        got = jnp.dot(table(), onehot_s[:, lanes], preferred_element_type=F32)
        hidden_s[:, lanes] = (got + bias_column).astype(BF16)
        return carry

    lax.fori_loop(0, count, step, 0)


def local_scratch(rows, length, width, vocab):
    half = length // 2
    return [
        pltpu.VMEM((8, rows * length), jnp.int32),
        pltpu.VMEM((TAPS * vocab, rows * length), BF16),
        pltpu.VMEM((width, rows * length), BF16),
        pltpu.VMEM((8, rows * length), F32),
        pltpu.VMEM((rows, length, length), BF16),
        pltpu.VMEM((length, TILE), F32),
        pltpu.VMEM((rows, half + 2 * EDGE, width), BF16),
        pltpu.VMEM((8, rows * length), F32),
        pltpu.VMEM((rows, half + 2 * EDGE, width), F32),
        pltpu.VMEM((rows * length, width), BF16),
    ]


def main_kernel(
    dims, len_ref, aux_ref, small_ref, ids_ref, mask_ref, table_ref, tq_ref, bias_ref, scorer_ref, cot_ref,
    blocks_ref, grad_ref, part_ref,
    taps_s, onehot_s, hidden_s, q_s, probs_s, similar_s, cot_s, band_s, pooled_s, hgrad_s,
):
    rows, length, width, vocab = dims
    count = rows * (length // TILE)
    seg_list, real_list = row_masks(rows, length, len_ref, ids_ref, mask_ref, taps_s)
    fill_cotangent(rows, length // 2, width, cot_ref, cot_s)
    fill_onehot(count, vocab, taps_s, onehot_s)
    m = members_of(rows, length, seg_list, real_list)
    fill_q(count, tq_ref[...], small_ref[1:2, 0:1], onehot_s, q_s)
    scores = block_scores(rows, length, m, q_s)

    def late_hidden():
        fill_hidden(count, lambda: table_ref[...], bias_ref[...], onehot_s, hidden_s)

    def scale():
        return aux_ref[0, 0] / small_ref[0:1, 0:1]

    refs = (hidden_s, cot_s, band_s, pooled_s, hgrad_s, probs_s, similar_s, blocks_ref, part_ref, late_hidden)
    middle(dims, m, scores, seg_list, real_list, scale, scorer_ref[...], refs, lambda r, t: None)

    def grad_step(k, carry):
        symbols = pl.ds(pl.multiple_of(k * vocab, vocab), vocab)
        for c in range(width // TILE):
            cols = slice(c * TILE, (c + 1) * TILE)
            grad_ref[symbols, cols] = jnp.dot(
                onehot_s[symbols, :], hgrad_s[:, cols], preferred_element_type=F32
            )
        return carry

    lax.fori_loop(0, TAPS, grad_step, 0)


def main_call(lengths, aux, small, ids, mask, table, tq, bias, scorer, cot):
    rows, length = ids.shape
    width = cot.shape[2]
    vocab = table.shape[1] // TAPS
    dims = (rows, length, width, vocab)
    vmem = pl.BlockSpec(memory_space=pltpu.VMEM)
    smem = pl.BlockSpec(memory_space=pltpu.SMEM)
    half = length // 2
    return pl.pallas_call(
        functools.partial(main_kernel, dims),
        out_shape=(
            jax.ShapeDtypeStruct((rows, half, width), BF16),
            jax.ShapeDtypeStruct((TAPS * vocab, width), F32),
            jax.ShapeDtypeStruct((8, width), F32),
        ),
        in_specs=[smem, smem] + [vmem] * 8,
        out_specs=(vmem, vmem, vmem),
        scratch_shapes=local_scratch(rows, length, width, vocab),
        compiler_params=pltpu.CompilerParams(vmem_limit_bytes=60 * 1024 * 1024),
        name="latent",
    )(lengths, aux, small, ids, mask, table, tq, bias, scorer, cot)


MESH = pl.DeviceIdType.MESH
ALL = slice(None)


def split3(x):
    a = x.astype(BF16).astype(F32)
    b = (x - a).astype(BF16).astype(F32)
    return a, b, x - a - b


def remote(src, dst, send, recv, device):
    return pltpu.make_async_remote_copy(
        src_ref=src, dst_ref=dst, send_sem=send, recv_sem=recv, device_id=device, device_id_type=MESH
    )


def device_at(c, x, y, z):
    return (z * 2 + y, x * 2 + c)


class Gather:
    def __init__(self, buf, me, send, recv):
        self.buf, self.me, self.send, self.recv = buf, me, send, recv
        self.rows = buf.shape[4] // 2
        self.copies = {}

    def part(self, c, x, y, z, half):
        return self.buf.at[c, x, y, z, pl.ds(half * self.rows, self.rows)]

    def go(self, n, ref, device):
        copy = remote(ref, ref, self.send.at[n], self.recv.at[n], device)
        copy.start()
        self.copies[n] = copy

    def along_z(self):
        c, x, y, z = self.me
        for half in range(2):
            for i in range(1, 4):
                self.go(half * 3 + i - 1, self.part(c, x, y, z, half), device_at(c, x, y, lax.rem(z + i, 4)))

    def across(self, half, step):
        c, x, y, z = self.me
        if step == 0:
            for i in range(3):
                self.copies[half * 3 + i].wait_recv()
            mine = got = self.part(c, x, y, ALL, half)
        elif step == 1:
            self.copies[6 + half].wait_recv()
            mine = self.part(c, ALL, y, ALL, half) if half == 0 else self.part(c, x, ALL, ALL, half)
            got = self.part(c, 1 - x, y, ALL, half) if half == 0 else self.part(c, x, 1 - y, ALL, half)
        else:
            self.copies[8 + half].wait_recv()
            got = self.part(c, ALL, 1 - y, ALL, half) if half == 0 else self.part(c, 1 - x, ALL, ALL, half)
        if step < 2:
            over_x = (half == 0) == (step == 0)
            to = device_at(c, 1 - x, y, z) if over_x else device_at(c, x, 1 - y, z)
            self.go(6 + 2 * step + half, mine, to)
        self.go(10 + 2 * step + half, got, device_at(1 - c, x, y, z))

    def steps(self):
        return [functools.partial(self.across, half, step) for step in range(3) for half in range(2)]

    def finish(self):
        for n in range(10, 16):
            self.copies[n].wait_recv()
        for copy in self.copies.values():
            copy.wait_send()


def place_of(slot, taps, per_tap):
    slot = jnp.minimum(slot, taps * per_tap - 1)
    tap = slot // per_tap
    return tap, slot - tap * per_tap


def static_place(tap, column, per_tap):
    slot = tap * per_tap + column
    return slot // 16, slot // 8 % 2, slot // 4 % 2, slot % 4


def step_kernel(
    dims,
    len_ref, aux_ref, ids_ref, mask_ref, emb_ref, conv_ref, bias_ref, scorer_ref, cot_ref,
    blocks_ref, loss_ref, embg_ref, convg_ref, biasg_ref, scoreg_ref,
    taps_s, onehot_s, hidden_s, q_s, probs_s, similar_s, cot_s, band_s, pooled_s, hgrad_s,
    blocks_s, part_s, conv_s, emb_s, convg_s,
    small_s, smalls_s, wcol_s, emball_s, tq_s, tqs_s, count_s, table_s,
    give_s, take_s, own_s, pass_s, came_s, zgive_s, zown_s, zcame_s, final_s, sums_s, sumr_s,
    local_sem, start_send, start_recv, half_sem, gather_send, gather_recv,
    core_send, core_recv, quad_send, quad_recv, line_send, line_recv, sum_send, sum_recv,
):
    rows, length, width, vocab, size, fs = dims
    half = length // 2
    count = rows * (length // TILE)
    per_tap = width // 128
    f, d = lax.axis_index("fsdp"), lax.axis_index("dp")
    z, y = f // 2, lax.rem(f, 2)
    x, c = d // 2, lax.rem(d, 2)
    me = (c, x, y, z)
    core = device_at(1 - c, x, y, z)

    barrier = pltpu.get_barrier_semaphore()
    peers = [(lax.rem(f + i, fs), d) for i in range(1, fs)]
    others = [core, device_at(c, 1 - x, y, z), device_at(c, 1 - x, 1 - y, z)]
    for peer in peers + others:
        pl.semaphore_signal(barrier, inc=1, device_id=peer, device_id_type=MESH)

    mid = vocab // 2
    my_half = pl.ds(pl.multiple_of(c * mid, mid), mid)
    my_tap, my_column = place_of(((c * 2 + x) * 2 + y) * 4 + z, TAPS, per_tap)
    local = [
        pltpu.make_async_copy(conv_ref, conv_s, local_sem.at[0]),
        pltpu.make_async_copy(emb_ref, emb_s, local_sem.at[1]),
        pltpu.make_async_copy(
            conv_ref.at[my_tap, :, pl.ds(pl.multiple_of(my_column * 128, 128), 128)], wcol_s.at[f], local_sem.at[2]
        ),
        pltpu.make_async_copy(emb_ref.at[my_half], emball_s.at[f, my_half], local_sem.at[3]),
    ]
    for r in range(rows):
        local.append(pltpu.make_async_copy(cot_ref.at[r], cot_s.at[r, pl.ds(EDGE, half)], local_sem.at[4 + r]))
    for copy in local:
        copy.start()
    real_here = jnp.sum(jnp.sum(mask_ref[...].astype(F32), axis=1, keepdims=True), axis=0, keepdims=True)
    small_s[...] = jnp.zeros_like(small_s)
    small_s[0:1, 0:size] = bias_ref[...].astype(F32)
    small_s[1:2, 0:size] = scorer_ref[...].astype(F32)
    small_s[2:3, :] = jnp.broadcast_to(real_here, (1, 128))
    smalls_s[f] = small_s[...]
    seg_list, real_list = row_masks(rows, length, len_ref, ids_ref, mask_ref, taps_s)

    pl.semaphore_wait(barrier, fs - 1 + 3)
    starts = []
    for i, peer in enumerate(peers):
        starts.append(remote(small_s, smalls_s.at[f], start_send.at[0, i], start_recv.at[0, i], peer))
        starts[-1].start()
    for i, peer in enumerate(peers):
        tap, column = place_of(((c * 2 + x) * 2 + lax.rem(peer[0], 2)) * 4 + peer[0] // 2, TAPS, per_tap)
        starts.append(
            remote(emb_ref.at[my_half], emball_s.at[f, my_half], start_send.at[1, i], start_recv.at[1, i], peer)
        )
        starts[-1].start()
        starts.append(
            remote(
                conv_ref.at[tap, :, pl.ds(pl.multiple_of(column * 128, 128), 128)],
                wcol_s.at[f],
                start_send.at[2, i],
                start_recv.at[2, i],
                peer,
            )
        )
        starts[-1].start()

    fill_onehot(count, vocab, taps_s, onehot_s)
    cot_s[:, 0:EDGE, :] = jnp.zeros((rows, EDGE, width), BF16)
    cot_s[:, EDGE + half :, :] = jnp.zeros((rows, EDGE, width), BF16)

    for i in range(fs - 1):
        starts[i].wait_recv()
    line = jnp.zeros((16, width), F32)
    real_sum = jnp.zeros((1, 1), F32)
    lane = lax.broadcasted_iota(jnp.int32, (128, width), 0)
    at = lax.broadcasted_iota(jnp.int32, (128, width), 1)
    for g in range(fs):
        pick = jnp.where((at == lane + g * size) & (lane < size), 1.0, 0.0).astype(BF16)
        both = jnp.concatenate([smalls_s[g], jnp.zeros((8, 128), F32)], axis=0)
        keep = lax.broadcasted_iota(jnp.int32, (16, 128), 0) < 2
        line = line + jnp.dot(jnp.where(keep, both, 0.0).astype(BF16), pick, preferred_element_type=F32)
        real_sum = real_sum + smalls_s[g][2:3, 0:1]
    count_s[0] = jnp.broadcast_to(real_sum, (8, 128))
    count_x = remote(
        count_s.at[0], count_s.at[1], half_sem.at[0], half_sem.at[1], device_at(c, 1 - x, y, z)
    )
    count_x.start()
    line16 = line.astype(BF16)
    bias_column = jnp.concatenate([line, jnp.zeros((112, width), F32)], axis=0).T[:, 0:1]
    const = jnp.sum(line[0:1] * line[1:2], axis=1, keepdims=True)
    scorer = line16[1:2]
    local[0].wait()
    local[1].wait()
    across = (((1,), (1,)), ((), ()))
    u = jnp.concatenate(
        [
            lax.dot_general(line16, conv_s[k], across, preferred_element_type=F32)[1:2]
            for k in range(TAPS)
        ],
        axis=0,
    )
    u = jnp.concatenate(list(split3(u)) + [jnp.zeros((1, size), F32)], axis=0).astype(BF16)
    tq = lax.dot_general(u, emb_s[...], across, preferred_element_type=F32)
    tq_s[...] = jnp.zeros_like(tq_s)
    tq_s[0:TAPS, :] = tq[0:TAPS] + tq[TAPS : 2 * TAPS] + tq[2 * TAPS : 3 * TAPS]
    tqs_s[f] = tq_s[...]
    tq_copies = []
    for i, peer in enumerate(peers):
        copy = remote(tq_s, tqs_s.at[f], start_send.at[3, i], start_recv.at[3, i], peer)
        copy.start()
        tq_copies.append(copy)

    for copy in local[2:4]:
        copy.wait()
    for i in range(fs - 1):
        starts[fs - 1 + 2 * i].wait_recv()
    emb_core = remote(
        emball_s.at[:, my_half], emball_s.at[:, my_half], half_sem.at[2], half_sem.at[3], core
    )
    emb_core.start()
    for i in range(fs - 1):
        starts[fs + 2 * i].wait_recv()
    emb_core.wait_recv()
    block = None
    for g in range(fs):
        term = lax.dot_general(wcol_s[g], emball_s[g], (((0,), (1,)), ((), ())), preferred_element_type=F32)
        block = term if block is None else block + term
    table_s[c, x, y, z] = block.astype(BF16)
    tables = Gather(table_s, me, gather_send.at[0], gather_recv.at[0])
    tables.along_z()

    count_x.wait_recv()
    count_s[2] = count_s[0] + count_s[1]
    count_c = remote(count_s.at[2], count_s.at[3], half_sem.at[4], half_sem.at[5], core)
    count_c.start()

    m = members_of(rows, length, seg_list, real_list)
    for copy in tq_copies:
        copy.wait_recv()
    tq = tqs_s[0]
    for g in range(1, fs):
        tq = tq + tqs_s[g]
    tq16 = jnp.concatenate(
        [
            jnp.concatenate(list(split3(tq[k : k + 1])) + [jnp.zeros((13, vocab), F32)], axis=0)
            for k in range(TAPS)
        ],
        axis=1,
    ).astype(BF16)
    fill_q(count, tq16, const, onehot_s, q_s)
    scores = block_scores(rows, length, m, q_s)

    steps = tables.steps()

    def between(r, t):
        if steps and (r, t) != (0, 0):
            steps.pop(0)()

    def whole(k):
        return jnp.concatenate(
            [table_s[static_place(k, j, per_tap)] for j in range(per_tap)], axis=0
        )

    def late_hidden():
        while steps:
            steps.pop(0)()
        tables.finish()
        fill_hidden(
            count, lambda: jnp.concatenate([whole(k) for k in range(TAPS)], axis=1), bias_column, onehot_s, hidden_s
        )
        for copy in local[4:]:
            copy.wait()
        count_c.wait_recv()

    def scale():
        return aux_ref[0, 0] / (count_s[2][0:1, 0:1] + count_s[3][0:1, 0:1])

    refs = (hidden_s, cot_s, band_s, pooled_s, hgrad_s, probs_s, similar_s, blocks_s, part_s, late_hidden)
    middle(dims[:4], m, scores, seg_list, real_list, scale, scorer, refs, between)
    blocks_out = pltpu.make_async_copy(blocks_s, blocks_ref, local_sem.at[0])
    blocks_out.start()

    sums_s[0] = part_s[...]
    sum_copies = [remote(sums_s.at[0], sumr_s.at[0], sum_send.at[0], sum_recv.at[0], core)]
    sum_copies[0].start()

    def product(slot):
        tap, column = place_of(jnp.minimum(slot, TAPS * per_tap - 2), TAPS, per_tap)
        symbols = pl.ds(pl.multiple_of(tap * vocab, vocab), vocab)
        lanes = pl.ds(pl.multiple_of(column * 128, 256), 256)
        return jnp.dot(onehot_s[symbols, :], hgrad_s[:, lanes], preferred_element_type=F32)

    def core_copy(p):
        return remote(give_s.at[p], take_s.at[p], core_send.at[p], core_recv.at[p], core)

    def give(p, carry):
        give_s[p] = product((1 - c) * 16 + 2 * p)
        core_copy(p).start()
        return carry

    lax.fori_loop(0, 8, give, 0)

    sum_copies[0].wait_recv()
    sums_s[1] = sums_s[0] + sumr_s[0]
    quad = [device_at(c, lax.rem(x + q // 2, 2), lax.rem(y + q % 2, 2), z) for q in range(4)]
    for q in range(1, 4):
        sum_copies.append(remote(sums_s.at[1], sumr_s.at[q], sum_send.at[q], sum_recv.at[q], quad[q]))
        sum_copies[-1].start()

    def quad_copy(t):
        q = 3 - t // 2
        to = device_at(c, lax.rem(x + q // 2, 2), lax.rem(y + lax.rem(q, 2), 2), z)
        return remote(pass_s.at[t], came_s.at[t], quad_send.at[t], quad_recv.at[t], to)

    def forward(t, carry):
        q = 3 - t // 2
        p = lax.rem(x + q // 2, 2) * 4 + lax.rem(y + lax.rem(q, 2), 2) * 2 + lax.rem(t, 2)
        got = product(c * 16 + 2 * p)
        core_copy(p).wait_recv()
        pass_s[t] = (got + take_s[p]).astype(BF16)
        quad_copy(t).start()
        return carry

    lax.fori_loop(0, 6, forward, 0)
    for t in range(2):
        p = x * 4 + y * 2 + t
        got = product(c * 16 + 2 * p)
        core_copy(p).wait_recv()
        own_s[t] = got + take_s[p]

    for q in range(1, 4):
        sum_copies[q].wait_recv()
    sums_s[2] = (sums_s[1] + sumr_s[1]) + (sumr_s[2] + sumr_s[3])
    for i in range(1, 4):
        to = device_at(c, x, y, lax.rem(z + i, 4))
        sum_copies.append(remote(sums_s.at[2], sumr_s.at[3 + i], sum_send.at[3 + i], sum_recv.at[3 + i], to))
        sum_copies[-1].start()

    for t in range(2):
        for q in range(1, 4):
            quad_copy(6 - 2 * q + t).wait_recv()
        total = own_s[t]
        for q in range(1, 4):
            total = total + came_s[6 - 2 * q + t].astype(F32)
        for j in range(2):
            zown_s[2 * t + j] = total[:, j * 128 : (j + 1) * 128]
            zgive_s[2 * t + j] = total[:, j * 128 : (j + 1) * 128].astype(BF16)
    line_copies = []
    for i in range(1, 4):
        to = lax.rem(z + i, 4)
        copy = remote(
            zgive_s.at[to], zcame_s.at[i - 1], line_send.at[i - 1], line_recv.at[i - 1], device_at(c, x, y, to)
        )
        copy.start()
        line_copies.append(copy)
    total = zown_s[z]
    for i, copy in enumerate(line_copies):
        copy.wait_recv()
        total = total + zcame_s[i].astype(F32)
    final_s[c, x, y, z] = total.astype(BF16)
    grads = Gather(final_s, me, gather_send.at[1], gather_recv.at[1])
    grads.along_z()

    for i in range(4, 7):
        sum_copies[i].wait_recv()
    sums = (sums_s[2] + sumr_s[4]) + (sumr_s[5] + sumr_s[6])
    loss_ref[...] = sums[1:2, 0:1] / (count_s[2][0:1, 0:1] + count_s[3][0:1, 0:1])

    for step in grads.steps():
        step()
    grads.finish()
    emb_total = None
    out_copies = []
    for k in range(TAPS):
        grad = jnp.concatenate([final_s[static_place(k, j, per_tap)] for j in range(per_tap)], axis=1)
        convg_s[k] = lax.dot_general(emb_s[...], grad, (((0,), (0,)), ((), ())), preferred_element_type=F32)
        out_copies.append(pltpu.make_async_copy(convg_s.at[k], convg_ref.at[k], local_sem.at[1 + k]))
        out_copies[-1].start()
        term = lax.dot_general(grad, conv_s[k], across, preferred_element_type=F32)
        emb_total = term if emb_total is None else emb_total + term
        if k == TAPS // 2:
            bias_line = jnp.sum(grad.astype(F32), axis=0, keepdims=True)
    embg_ref[...] = emb_total
    pick = jnp.where((at == lane + f * size) & (lane < size), 1.0, 0.0).astype(BF16)
    lines = jnp.concatenate(
        list(split3(bias_line)) + list(split3(sums[0:1])) + [jnp.zeros((10, width), F32)], axis=0
    ).astype(BF16)
    mine = lax.dot_general(lines, pick, across, preferred_element_type=F32)
    biasg_ref[...] = (mine[0:1] + mine[1:2] + mine[2:3])[:, :size]
    scoreg_ref[...] = (mine[3:4] + mine[4:5] + mine[5:6])[:, :size]

    for copy in starts + tq_copies + sum_copies + line_copies + [count_x, count_c, emb_core]:
        copy.wait_send()
    for p in range(8):
        core_copy(p).wait_send()
    for t in range(6):
        quad_copy(t).wait_send()
    for copy in out_copies + [blocks_out]:
        copy.wait()


def step_shards(byte_ids, doc_lengths, pad_mask, embedding, conv_weight, conv_bias, scorer, cotangent, aux_weight):
    rows, length = byte_ids.shape
    vocab, size = embedding.shape
    width = conv_weight.shape[2]
    half = length // 2
    fs = width // size
    dims = (rows, length, width, vocab, size, fs)
    vmem = pl.BlockSpec(memory_space=pltpu.VMEM)
    smem = pl.BlockSpec(memory_space=pltpu.SMEM)
    hbm = pl.BlockSpec(memory_space=pl.ANY)
    dma = pltpu.SemaphoreType.DMA
    blocks, loss, emb_grad, conv_grad, bias_grad, score_grad = pl.pallas_call(
        functools.partial(step_kernel, dims),
        out_shape=(
            jax.ShapeDtypeStruct((rows, half, width), BF16),
            jax.ShapeDtypeStruct((1, 1), F32),
            jax.ShapeDtypeStruct((vocab, size), F32),
            jax.ShapeDtypeStruct((TAPS, size, width), F32),
            jax.ShapeDtypeStruct((1, size), F32),
            jax.ShapeDtypeStruct((1, size), F32),
        ),
        in_specs=[smem, smem, vmem, vmem, hbm, hbm, vmem, vmem, hbm],
        out_specs=(hbm, vmem, vmem, hbm, vmem, vmem),
        scratch_shapes=local_scratch(rows, length, width, vocab)
        + [
            pltpu.VMEM((rows, half, width), BF16),
            pltpu.VMEM((8, width), F32),
            pltpu.VMEM((TAPS, size, width), BF16),
            pltpu.VMEM((vocab, size), BF16),
            pltpu.VMEM((TAPS, size, width), F32),
            pltpu.VMEM((8, 128), F32),
            pltpu.VMEM((fs, 8, 128), F32),
            pltpu.VMEM((fs, size, 128), BF16),
            pltpu.VMEM((fs, vocab, size), BF16),
            pltpu.VMEM((8, vocab), F32),
            pltpu.VMEM((fs, 8, vocab), F32),
            pltpu.VMEM((4, 8, 128), F32),
            pltpu.VMEM((2, 2, 2, 4, 128, vocab), BF16),
            pltpu.VMEM((8, vocab, 256), F32),
            pltpu.VMEM((8, vocab, 256), F32),
            pltpu.VMEM((2, vocab, 256), F32),
            pltpu.VMEM((6, vocab, 256), BF16),
            pltpu.VMEM((6, vocab, 256), BF16),
            pltpu.VMEM((4, vocab, 128), BF16),
            pltpu.VMEM((4, vocab, 128), F32),
            pltpu.VMEM((3, vocab, 128), BF16),
            pltpu.VMEM((2, 2, 2, 4, vocab, 128), BF16),
            pltpu.VMEM((3, 8, width), F32),
            pltpu.VMEM((7, 8, width), F32),
            dma((4 + max(rows, 2),)),
            dma((4, fs - 1)),
            dma((4, fs - 1)),
            dma((6,)),
            dma((2, 16)),
            dma((2, 16)),
            dma((8,)),
            dma((8,)),
            dma((6,)),
            dma((6,)),
            dma((3,)),
            dma((3,)),
            dma((7,)),
            dma((7,)),
        ],
        compiler_params=pltpu.CompilerParams(
            collective_id=0, has_side_effects=True, vmem_limit_bytes=62 * 1024 * 1024
        ),
        name="step",
    )(
        doc_lengths,
        aux_weight.reshape(1, 1),
        byte_ids,
        pad_mask,
        embedding,
        conv_weight,
        conv_bias.reshape(1, size),
        scorer.reshape(1, size),
        cotangent,
    )
    return blocks, loss.reshape(()), emb_grad, conv_grad, bias_grad.reshape(size), score_grad.reshape(size)


def split3_rows(x):
    a = lax.reduce_precision(x, 8, 7)
    b = lax.reduce_precision(x - a, 8, 7)
    return jnp.concatenate([a, b, x - a - b], axis=0).astype(BF16)


def gathered_shards(byte_ids, doc_lengths, pad_mask, embedding, conv_weight, conv_bias, scorer, cotangent, aux_weight):
    emb = lax.all_gather(embedding, "fsdp", axis=1, tiled=True)
    conv = lax.all_gather(conv_weight, "fsdp", axis=1, tiled=True)
    bias = lax.all_gather(conv_bias, "fsdp", axis=0, tiled=True)
    score = lax.all_gather(scorer, "fsdp", axis=0, tiled=True)
    vocab, width = emb.shape
    count = lax.psum(jnp.sum(pad_mask.astype(F32)), ("fsdp", "dp"))
    table = jnp.einsum("kcd,vc->dkv", conv, emb, preferred_element_type=F32).reshape(width, TAPS * vocab)
    score32 = score.astype(F32)
    q_table = jnp.sum(table * score32[:, None], axis=0, keepdims=True)
    tq = jnp.concatenate([split3_rows(q_table), jnp.zeros((13, TAPS * vocab), BF16)], axis=0)
    bias32 = bias.astype(F32)
    small = jnp.stack([jnp.full((128,), count), jnp.full((128,), jnp.sum(bias32 * score32))])
    small = jnp.concatenate([small, jnp.zeros((6, 128), F32)], axis=0)
    blocks, grad, part = main_call(
        doc_lengths, aux_weight.reshape(1, 1), small, byte_ids, pad_mask, table.astype(BF16), tq, bias32[:, None], score[None, :], cotangent
    )
    grad = lax.psum(grad, ("fsdp", "dp")).reshape(TAPS, vocab, width)
    score_grad = lax.psum(part[0], ("fsdp", "dp"))
    loss = lax.psum(part[1, 0], ("fsdp", "dp")) / count
    size = embedding.shape[1]
    at = lax.axis_index("fsdp") * size
    bias_grad = lax.dynamic_slice_in_dim(jnp.sum(grad[TAPS // 2], axis=0), at, size, 0)
    score_grad = lax.dynamic_slice_in_dim(score_grad, at, size, 0)
    conv_grad = jnp.einsum("vc,kvd->kcd", embedding.astype(F32), grad, precision=lax.Precision.HIGHEST)
    emb_grad = jnp.einsum("kvd,kcd->vc", grad, conv_weight.astype(F32), precision=lax.Precision.HIGHEST)
    return blocks, loss, emb_grad, conv_grad, bias_grad, score_grad


def solution(mesh):
    small = mesh.shape["fsdp"] == 8 and mesh.shape["dp"] == 4
    return jax.shard_map(
        step_shards if small else gathered_shards,
        mesh=mesh,
        in_specs=(
            P(("fsdp", "dp"), None),
            P(("fsdp", "dp"), None),
            P(("fsdp", "dp"), None),
            P(None, "fsdp"),
            P(None, "fsdp", None),
            P("fsdp"),
            P("fsdp"),
            P(("fsdp", "dp"), None, None),
            P(),
        ),
        out_specs=(
            P(("fsdp", "dp"), None, None),
            P(),
            P(None, "fsdp"),
            P(None, "fsdp", None),
            P("fsdp"),
            P("fsdp"),
        ),
        check_vma=False,
    )
```

```python
import functools
import jax
import jax.numpy as jnp
from jax import lax
from jax.experimental import pallas as pl
from jax.experimental.pallas import tpu as pltpu
from jax.sharding import PartitionSpec as P

TAPS = 5
SIZES = 4
NEG = -1000000000.0
F32 = jnp.float32
BF16 = jnp.bfloat16
TILE = 256
EDGE = 16
TABLE_CHUNKS = 2
GRAD_CHUNKS = 2


def split2(x):
    high = x.astype(BF16).astype(F32)
    return high, x - high


def shift(x, offset):
    length = x.shape[1]
    return x if offset == 0 else pltpu.roll(x, (-offset) % length, 1)


def group_pair(x, step, lane_bit):
    size = x.shape[0]
    down = pltpu.roll(x, (size - step) % size, 0)
    up = pltpu.roll(x, step, 0)
    return jnp.where(lane_bit, up, down)


def group_all(x, op, bits):
    x = op(x, group_pair(x, 1, bits[0]))
    return op(x, group_pair(x, 2, bits[1]))


def spread(rows_list, length):
    return jnp.concatenate([jnp.broadcast_to(x, (SIZES, length)) for x in rows_list], axis=0)


def lane_rows(ref, at, r, length):
    return ref[at : at + 1, r * length : (r + 1) * length]


DELTA_EVEN = {-3: -2, -2: -1, -1: -1, 0: 0, 1: 0, 2: 1, 3: 1}
DELTA_ODD = {-3: -1, -2: -1, -1: 0, 0: 0, 1: 1, 2: 1, 3: 2}
OFFSETS = [o for o in range(1 - SIZES, SIZES) if o != 0]


def row_masks(rows, length, len_ref, ids_ref, mask_ref, taps_s):
    place1 = lax.broadcasted_iota(jnp.int32, (1, length), 1)
    seg_list, real_list = [], []
    for r in range(rows):
        end = len_ref[r, 0]
        segment = jnp.where(place1 >= end, 1.0, 0.0)
        for d in range(1, len_ref.shape[1]):
            end = end + len_ref[r, d]
            segment = segment + jnp.where(place1 >= end, 1.0, 0.0)
        seg_list.append(segment)
        real_list.append(mask_ref[r : r + 1, :].astype(F32))
        ids = ids_ref[r : r + 1, :].astype(F32)
        known = jnp.where(real_list[r] > 0.5, ids, -1.0)
        for k in range(TAPS):
            o = k - TAPS // 2
            inside = (place1 + o >= 0) & (place1 + o < length)
            keep = inside & (shift(segment, o) == segment)
            taps_s[k : k + 1, r * length : (r + 1) * length] = jnp.where(
                keep, shift(known, o), -1.0
            ).astype(jnp.int32)
    return seg_list, real_list


def fill_onehot(count, vocab, taps_s, onehot_s):
    symbol = lax.broadcasted_iota(jnp.int32, (vocab, TILE), 0)

    def step(t, carry):
        lanes = pl.ds(pl.multiple_of(t * TILE, TILE), TILE)
        for k in range(TAPS):
            here = taps_s[k : k + 1, lanes]
            onehot_s[k * vocab : (k + 1) * vocab, lanes] = jnp.where(symbol == here, 1.0, 0.0).astype(BF16)
        return carry

    lax.fori_loop(0, count, step, 0)


def members_of(rows, length, seg_list, real_list):
    shape = (rows * SIZES, length)
    place = lax.broadcasted_iota(jnp.int32, shape, 1)
    sub = lax.broadcasted_iota(jnp.int32, shape, 0)
    size = (sub & (SIZES - 1)) + 1
    third = jnp.floor((place.astype(F32) + 0.5) * (1.0 / 3.0)).astype(jnp.int32)
    within = jnp.where(
        size == 1, 0, jnp.where(size == 2, place & 1, jnp.where(size == 3, place - 3 * third, place & 3))
    )
    seg = spread(seg_list, length)
    real = spread(real_list, length)
    same = {}
    for o in range(1, SIZES):
        ahead = (within + o < size) & (place + o < length) & (shift(seg, o) == seg)
        behind = (within - o >= 0) & (shift(seg, -o) == seg)
        same[o] = jnp.where(ahead, 1.0, 0.0)
        same[-o] = jnp.where(behind, 1.0, 0.0)
    member = {o: same[o] * shift(real, o) for o in OFFSETS}
    members = real
    for o in OFFSETS:
        members = members + member[o]
    even = (place & 1) == 0
    pair = jnp.where(even | (shift(seg, -1) == seg), real, 0.0)
    partner = jnp.where(even, shift(pair, 1), shift(pair, -1))
    return dict(
        bits=((sub & 1) == 1, (sub & 2) == 2),
        first=size == 1,
        even=even,
        real=real,
        same=same,
        member=member,
        inverse=1.0 / jnp.maximum(members, 1.0),
        pair_weight=pair / jnp.maximum(pair + partner, 1.0),
    )


def block_scores(rows, length, m, q_s):
    q = spread([lane_rows(q_s, 0, r, length) for r in range(rows)], length)
    total = q * m["real"]
    for o in OFFSETS:
        total = total + m["member"][o] * shift(q, o)
    return total * m["inverse"]


def calibrate_row(r, length, scores, seg, real, similar_s, probs_s, between):
    s = scores[r * SIZES : (r + 1) * SIZES]
    a, rest = split2(s)
    b, c = split2(rest)
    key_seg = jnp.where(real > 0.5, seg, -1.0)
    zero = jnp.zeros((128 - 6 * SIZES - 1, length), F32)
    left = jnp.concatenate([a, a, b, b, a, c, key_seg, zero], axis=0).T
    right = jnp.concatenate([a, b, a, b, c, a, jnp.zeros_like(key_seg), zero], axis=0).astype(BF16)
    key_column = left[:, 6 * SIZES : 6 * SIZES + 1]
    left = left.astype(BF16)
    x = jnp.concatenate(
        [jnp.ones((1, length), F32), s, s[0:1] * s, s[1:2] * s[1:], s[2:3] * s[2:], s[3:4] * s[3:]]
        + [jnp.zeros((1, length), F32)],
        axis=0,
    )
    x_high, x_low = split2(x)
    features = jnp.concatenate([x_high, x_low], axis=0).astype(BF16)
    outs = []
    for t in range(length // TILE):
        lanes = slice(t * TILE, (t + 1) * TILE)
        query_seg = seg[:, lanes]
        top = None
        for j in range(length // 128):
            keys = slice(j * 128, (j + 1) * 128)
            sim = jnp.dot(left[keys], right[:, lanes], preferred_element_type=F32)
            allowed = key_column[keys] == query_seg
            if j * 128 // TILE == t:
                key_place = lax.broadcasted_iota(jnp.int32, (128, TILE), 0) + j * 128
                query_place = lax.broadcasted_iota(jnp.int32, (128, TILE), 1) + t * TILE
                allowed = allowed | (key_place == query_place)
            sim = jnp.where(allowed, sim, NEG)
            similar_s[keys, :] = sim
            here = jnp.max(sim, axis=0, keepdims=True)
            top = here if top is None else jnp.maximum(top, here)
        for j in range(length // 128):
            keys = slice(j * 128, (j + 1) * 128)
            probs_s[r, keys, lanes] = jnp.exp(similar_s[keys, :] - top).astype(BF16)
        outs.append(jnp.dot(features, probs_s[r, :, lanes], preferred_element_type=F32))
        between(r, t)
    moments = jnp.concatenate(outs, axis=1)
    moments = moments[0:16] + moments[16:32]
    norm = 1.0 / moments[0:1]
    return moments * norm, norm


def size_softmax(cal, bits):
    top = group_all(cal, jnp.maximum, bits)
    log_weight = (cal - top) - jnp.log(group_all(jnp.exp(cal - top), jnp.add, bits))
    weight = jnp.exp(log_weight)
    entropy = -group_all(weight * log_weight, jnp.add, bits)
    return weight, log_weight, entropy


def band_products(rows, length, cot_s, hidden_s, band_s, window):
    kl = lax.broadcasted_iota(jnp.int32, (window, TILE), 0)
    jl = lax.broadcasted_iota(jnp.int32, (window, TILE), 1) // 2 + EDGE
    diagonal = kl - jl
    for r in range(rows):
        for t in range(length // TILE):
            lanes = slice(r * length + t * TILE, r * length + (t + 1) * TILE)
            first = t * TILE // 2
            prod = jnp.dot(
                cot_s[r, first : first + window, :], hidden_s[:, lanes], preferred_element_type=F32
            )
            for d in range(-2, 3):
                band_s[d + 2 : d + 3, lanes] = jnp.sum(jnp.where(diagonal == d, prod, 0.0), axis=0, keepdims=True)
    return diagonal


def calibrate_back(r, length, scores, cal_grad, inner, moments, norm, probs_s):
    part = slice(r * SIZES, (r + 1) * SIZES)
    s, g, ri = scores[part], cal_grad[part], inner[r * SIZES : r * SIZES + 1]
    at = {}
    n = 1 + SIZES
    for a in range(SIZES):
        for b in range(a, SIZES):
            at[a, b] = at[b, a] = n
            n += 1
    query = []
    for a in range(SIZES):
        total = -moments[1 + a : 2 + a] * ri
        for b in range(SIZES):
            total = total + moments[at[a, b] : at[a, b] + 1] * g[b : b + 1]
        query.append(total)
    y = jnp.concatenate([g - s * ri] + [s[a : a + 1] * g for a in range(SIZES)], axis=0) * norm
    y = jnp.concatenate([y, jnp.zeros((4, length), F32)], axis=0)
    y_high, y_low = split2(y)
    features = jnp.concatenate([y_high, y_low], axis=0).astype(BF16)
    outs = []
    for t in range(length // TILE):
        keys = slice(t * TILE, (t + 1) * TILE)
        outs.append(
            lax.dot_general(features, probs_s[r, keys, :], (((1,), (1,)), ((), ())), preferred_element_type=F32)
        )
    back = jnp.concatenate(outs, axis=1)
    back = back[0:24] + back[24:48]
    key = []
    for a in range(SIZES):
        total = back[a : a + 1]
        for b in range(SIZES):
            n = SIZES + a * SIZES + b
            total = total + s[b : b + 1] * back[n : n + 1]
        key.append(total + query[a])
    return jnp.concatenate(key, axis=0)


def middle(dims, m, scores, seg_list, real_list, scale, scorer, refs, between):
    rows, length, width, vocab = dims
    half = length // 2
    tiles = length // TILE
    window = TILE // 2 + 2 * EDGE
    hidden_s, cot_s, band_s, pooled_s, hgrad_s, probs_s, similar_s, blocks_ref, part_ref, matrix_s, late_hidden = refs
    bits, real, same, member, inverse, pair_weight = (
        m[n] for n in ("bits", "real", "same", "member", "inverse", "pair_weight")
    )
    kept = [
        calibrate_row(r, length, scores, seg_list[r], real_list[r], similar_s, probs_s, between) for r in range(rows)
    ]
    cal = jnp.concatenate([moments[1 : 1 + SIZES] for moments, norm in kept], axis=0)
    weight, log_weight, entropy = size_softmax(cal, bits)
    entropy_sum = jnp.sum(
        jnp.sum(jnp.where(m["first"], entropy * real, 0.0), axis=1, keepdims=True), axis=0, keepdims=True
    )
    part_ref[...] = jnp.zeros_like(part_ref)
    part_ref[1:2, :] = jnp.broadcast_to(entropy_sum, (1, width))
    for r in range(rows):
        pooled_s[r] = jnp.zeros_like(pooled_s[r])

    late_hidden()
    diagonal = band_products(rows, length, cot_s, hidden_s, band_s, window)
    even1 = (lax.broadcasted_iota(jnp.int32, (1, length), 1) & 1) == 0
    band = [[lane_rows(band_s, d + 2, r, length) for d in range(-2, 3)] for r in range(rows)]

    def product(o):
        return spread(
            [jnp.where(even1, band[r][DELTA_EVEN[o] + 2], band[r][DELTA_ODD[o] + 2]) for r in range(rows)], length
        )

    gathered = real * product(0)
    for o in OFFSETS:
        gathered = gathered + member[o] * shift(product(-o), o)
    weight_grad = pair_weight * inverse * gathered
    cal_grad = weight * (weight_grad - group_all(weight * weight_grad, jnp.add, bits))
    cal_grad = cal_grad - scale() * real * weight * (log_weight + entropy)
    inner = group_all(cal * cal_grad, jnp.add, bits)
    score_grad = jnp.concatenate(
        [calibrate_back(r, length, scores, cal_grad, inner, kept[r][0], kept[r][1], probs_s) for r in range(rows)],
        axis=0,
    )
    score_grad = score_grad * inverse
    q_grad = score_grad
    for o in OFFSETS:
        q_grad = q_grad + same[o] * shift(score_grad, o)
    q_grad = group_all(q_grad * real, jnp.add, bits)

    use = pair_weight * weight * inverse
    moved = {o: (use if o == 0 else same[o] * shift(use, o)) for o in range(1 - SIZES, SIZES)}
    mix = []
    for d in range(-2, 3):
        odd_sum = sum([moved[o] for o in moved if DELTA_ODD[o] == d], jnp.zeros_like(use))
        even_sum = sum([moved[o] for o in moved if DELTA_EVEN[o] == d], jnp.zeros_like(use))
        mix.append(group_all(jnp.where(m["even"], even_sum, odd_sum) * real, jnp.add, bits))

    scorer16 = jnp.concatenate([scorer, scorer, jnp.zeros((EDGE - 2, width), BF16)], axis=0)
    for r in range(rows):
        at = r * SIZES
        q_high, q_low = split2(q_grad[at : at + 1])
        for t in range(tiles):
            lanes = slice(t * TILE, (t + 1) * TILE)
            all_lanes = slice(r * length + t * TILE, r * length + (t + 1) * TILE)
            first = t * TILE // 2
            matrix = jnp.zeros((window, TILE), F32)
            for d in range(-2, 3):
                matrix = jnp.where(diagonal == d, mix[d + 2][at : at + 1, lanes], matrix)
            high, low = split2(matrix)
            matrix = jnp.concatenate(
                [high, low, q_high[:, lanes], q_low[:, lanes], jnp.zeros((EDGE - 2, TILE), F32)], axis=0
            ).astype(BF16)
            matrix_s[r * tiles + t] = matrix
            here = cot_s[r, first : first + window, :]
            given = jnp.concatenate([here, here, scorer16], axis=0)
            hgrad_s[all_lanes, :] = lax.dot_general(
                matrix, given, (((0,), (0,)), ((), ())), preferred_element_type=F32
            ).astype(BF16)

    def pool():
        for r in range(rows):
            for t in range(tiles):
                first = t * TILE // 2
                out = lax.dot_general(
                    matrix_s[r * tiles + t],
                    hidden_s[:, r * length + t * TILE : r * length + (t + 1) * TILE],
                    (((1,), (1,)), ((), ())),
                    preferred_element_type=F32,
                )
                pooled_s[r, first : first + window, :] += out[:window] + out[window : 2 * window]
                part_ref[0:1, :] += out[2 * window : 2 * window + 1] + out[2 * window + 1 : 2 * window + 2]
            blocks_ref[r] = pooled_s[r, EDGE : EDGE + half, :].astype(BF16)

    return pool


def fill_cotangent(rows, half, width, cot_ref, cot_s):
    cot_s[:, 0:EDGE, :] = jnp.zeros((rows, EDGE, width), BF16)
    cot_s[:, EDGE + half :, :] = jnp.zeros((rows, EDGE, width), BF16)
    for r in range(rows):
        cot_s[r, EDGE : EDGE + half, :] = cot_ref[r]


def fill_q(count, tq16, const, onehot_s, q_s):
    def step(t, carry):
        lanes = pl.ds(pl.multiple_of(t * TILE, TILE), TILE)
        got = jnp.dot(tq16, onehot_s[:, lanes], preferred_element_type=F32)
        q_s[0:1, lanes] = got[0:1] + got[1:2] + got[2:3] + const
        return carry

    lax.fori_loop(0, count, step, 0)


def fill_hidden(count, table, bias_column, onehot_s, hidden_s):
    def step(t, carry):
        lanes = pl.ds(pl.multiple_of(t * TILE, TILE), TILE)
        got = jnp.dot(table(), onehot_s[:, lanes], preferred_element_type=F32)
        hidden_s[:, lanes] = (got + bias_column).astype(BF16)
        return carry

    lax.fori_loop(0, count, step, 0)


def local_scratch(rows, length, width, vocab):
    half = length // 2
    return [
        pltpu.VMEM((8, rows * length), jnp.int32),
        pltpu.VMEM((TAPS * vocab, rows * length), BF16),
        pltpu.VMEM((width, rows * length), BF16),
        pltpu.VMEM((8, rows * length), F32),
        pltpu.VMEM((rows, length, length), BF16),
        pltpu.VMEM((length, TILE), F32),
        pltpu.VMEM((rows, half + 2 * EDGE, width), BF16),
        pltpu.VMEM((8, rows * length), F32),
        pltpu.VMEM((rows, half + 2 * EDGE, width), F32),
        pltpu.VMEM((rows * length, width), BF16),
        pltpu.VMEM((rows * (length // TILE), TILE + 5 * EDGE, TILE), BF16),
    ]


def main_kernel(
    dims, len_ref, aux_ref, small_ref, ids_ref, mask_ref, table_ref, tq_ref, bias_ref, scorer_ref, cot_ref,
    blocks_ref, grad_ref, part_ref,
    taps_s, onehot_s, hidden_s, q_s, probs_s, similar_s, cot_s, band_s, pooled_s, hgrad_s, matrix_s,
):
    rows, length, width, vocab = dims
    count = rows * (length // TILE)
    seg_list, real_list = row_masks(rows, length, len_ref, ids_ref, mask_ref, taps_s)
    fill_cotangent(rows, length // 2, width, cot_ref, cot_s)
    fill_onehot(count, vocab, taps_s, onehot_s)
    m = members_of(rows, length, seg_list, real_list)
    fill_q(count, tq_ref[...], small_ref[1:2, 0:1], onehot_s, q_s)
    scores = block_scores(rows, length, m, q_s)

    def late_hidden():
        fill_hidden(count, lambda: table_ref[...], bias_ref[...], onehot_s, hidden_s)

    def scale():
        return aux_ref[0, 0] / small_ref[0:1, 0:1]

    refs = (hidden_s, cot_s, band_s, pooled_s, hgrad_s, probs_s, similar_s, blocks_ref, part_ref, matrix_s, late_hidden)
    pool = middle(dims, m, scores, seg_list, real_list, scale, scorer_ref[...], refs, lambda r, t: None)
    pool()

    def grad_step(k, carry):
        symbols = pl.ds(pl.multiple_of(k * vocab, vocab), vocab)
        for c in range(width // TILE):
            cols = slice(c * TILE, (c + 1) * TILE)
            grad_ref[symbols, cols] = jnp.dot(
                onehot_s[symbols, :], hgrad_s[:, cols], preferred_element_type=F32
            )
        return carry

    lax.fori_loop(0, TAPS, grad_step, 0)


def main_call(lengths, aux, small, ids, mask, table, tq, bias, scorer, cot):
    rows, length = ids.shape
    width = cot.shape[2]
    vocab = table.shape[1] // TAPS
    dims = (rows, length, width, vocab)
    vmem = pl.BlockSpec(memory_space=pltpu.VMEM)
    smem = pl.BlockSpec(memory_space=pltpu.SMEM)
    half = length // 2
    return pl.pallas_call(
        functools.partial(main_kernel, dims),
        out_shape=(
            jax.ShapeDtypeStruct((rows, half, width), BF16),
            jax.ShapeDtypeStruct((TAPS * vocab, width), F32),
            jax.ShapeDtypeStruct((8, width), F32),
        ),
        in_specs=[smem, smem] + [vmem] * 8,
        out_specs=(vmem, vmem, vmem),
        scratch_shapes=local_scratch(rows, length, width, vocab),
        compiler_params=pltpu.CompilerParams(vmem_limit_bytes=60 * 1024 * 1024),
        name="latent",
    )(lengths, aux, small, ids, mask, table, tq, bias, scorer, cot)


MESH = pl.DeviceIdType.MESH
ALL = slice(None)


def split3(x):
    a = x.astype(BF16).astype(F32)
    b = (x - a).astype(BF16).astype(F32)
    return a, b, x - a - b


def remote(src, dst, send, recv, device):
    return pltpu.make_async_remote_copy(
        src_ref=src, dst_ref=dst, send_sem=send, recv_sem=recv, device_id=device, device_id_type=MESH
    )


def device_at(c, x, y, z):
    return (z * 2 + y, x * 2 + c)


class Gather:
    def __init__(self, buf, me, send, recv, chunks):
        self.buf, self.me, self.send, self.recv, self.chunks = buf, me, send, recv, chunks
        self.rows = buf.shape[4] // chunks
        self.copies = {}

    def part(self, c, x, y, z, chunk, half=None):
        if half is None:
            return self.buf.at[c, x, y, z, pl.ds(chunk * self.rows, self.rows)]
        return self.buf.at[c, x, y, z, pl.ds(chunk * self.rows + half * (self.rows // 2), self.rows // 2)]

    def go(self, chunk, n, ref, device):
        at = chunk * 11 + n
        copy = remote(ref, ref, self.send.at[at], self.recv.at[at], device)
        copy.start()
        self.copies[chunk, n] = copy

    def along_z(self, chunk):
        c, x, y, z = self.me
        for i in range(1, 4):
            self.go(chunk, i - 1, self.part(c, x, y, z, chunk), device_at(c, x, y, lax.rem(z + i, 4)))

    def across(self, chunk, step):
        c, x, y, z = self.me
        copies = self.copies
        core, over_x, over_y = device_at(1 - c, x, y, z), device_at(c, 1 - x, y, z), device_at(c, x, 1 - y, z)
        if step == 0:
            for n in range(3):
                copies[chunk, n].wait_recv()
            mine = self.part(c, x, y, ALL, chunk)
            self.go(chunk, 3, mine, over_x)
            self.go(chunk, 4, mine, over_y)
            self.go(chunk, 5, mine, core)
        elif step == 1:
            copies[chunk, 3].wait_recv()
            self.go(chunk, 6, self.part(c, 1 - x, y, ALL, chunk, 0), over_y)
            self.go(chunk, 7, self.part(c, 1 - x, y, ALL, chunk), core)
            copies[chunk, 4].wait_recv()
            self.go(chunk, 8, self.part(c, x, 1 - y, ALL, chunk, 1), over_x)
            self.go(chunk, 9, self.part(c, x, 1 - y, ALL, chunk), core)
        else:
            copies[chunk, 6].wait_recv()
            copies[chunk, 8].wait_recv()
            self.go(chunk, 10, self.part(c, 1 - x, 1 - y, ALL, chunk), core)

    def arrived(self, chunk):
        for n in (5, 7, 9, 10):
            self.copies[chunk, n].wait_recv()

    def drain(self):
        for copy in self.copies.values():
            copy.wait_send()


def place_of(slot, taps, per_tap):
    slot = jnp.minimum(slot, taps * per_tap - 1)
    tap = slot // per_tap
    return tap, slot - tap * per_tap


def static_place(tap, column, per_tap):
    slot = tap * per_tap + column
    return slot // 16, slot // 8 % 2, slot // 4 % 2, slot % 4


def step_kernel(
    dims,
    len_ref, aux_ref, ids_ref, mask_ref, emb_ref, conv_ref, bias_ref, scorer_ref, cot_ref,
    blocks_ref, final_ref, sums_ref,
    taps_s, onehot_s, hidden_s, q_s, probs_s, similar_s, cot_s, band_s, pooled_s, hgrad_s, matrix_s,
    blocks_s, part_s, conv_s, emb_s,
    small_s, smalls_s, wcol_s, emball_s, tq_s, tqs_s, count_s, table_s,
    give_s, take_s, own_s, pass_s, came_s, zgive_s, zown_s, zcame_s, final_s, sums_s, sumr_s,
    local_sem, start_send, start_recv, half_sem, gather_send, gather_recv,
    core_send, core_recv, quad_send, quad_recv, line_send, line_recv, sum_send, sum_recv,
):
    rows, length, width, vocab, size, fs = dims
    half = length // 2
    count = rows * (length // TILE)
    per_tap = width // 128
    f, d = lax.axis_index("fsdp"), lax.axis_index("dp")
    z, y = f // 2, lax.rem(f, 2)
    x, c = d // 2, lax.rem(d, 2)
    me = (c, x, y, z)
    core = device_at(1 - c, x, y, z)

    barrier = pltpu.get_barrier_semaphore()
    peers = [(lax.rem(f + i, fs), d) for i in range(1, fs)]
    others = [core, device_at(c, 1 - x, y, z), device_at(c, 1 - x, 1 - y, z)]
    for peer in peers + others:
        pl.semaphore_signal(barrier, inc=1, device_id=peer, device_id_type=MESH)

    mid = vocab // 2
    my_half = pl.ds(pl.multiple_of(c * mid, mid), mid)
    my_rows = pl.ds(pl.multiple_of(x * (size // 2), size // 2), size // 2)
    my_tap, my_column = place_of(((c * 2 + x) * 2 + y) * 4 + z, TAPS, per_tap)
    local = [
        pltpu.make_async_copy(conv_ref, conv_s, local_sem.at[0]),
        pltpu.make_async_copy(emb_ref, emb_s, local_sem.at[1]),
        pltpu.make_async_copy(
            conv_ref.at[my_tap, :, pl.ds(pl.multiple_of(my_column * 128, 128), 128)], wcol_s.at[f], local_sem.at[2]
        ),
        pltpu.make_async_copy(emb_ref.at[my_rows, my_half], emball_s.at[f, my_rows, my_half], local_sem.at[3]),
    ]
    for r in range(rows):
        local.append(pltpu.make_async_copy(cot_ref.at[r], cot_s.at[r, pl.ds(EDGE, half)], local_sem.at[4 + r]))
    for copy in local:
        copy.start()
    real_here = jnp.sum(jnp.sum(mask_ref[...].astype(F32), axis=1, keepdims=True), axis=0, keepdims=True)
    small_s[...] = jnp.zeros_like(small_s)
    small_s[0:1, 0:size] = bias_ref[...].astype(F32)
    small_s[1:2, 0:size] = scorer_ref[...].astype(F32)
    small_s[2:3, :] = jnp.broadcast_to(real_here, (1, 128))
    smalls_s[f] = small_s[...]
    seg_list, real_list = row_masks(rows, length, len_ref, ids_ref, mask_ref, taps_s)

    pl.semaphore_wait(barrier, fs - 1 + 3)
    starts = []
    for i, peer in enumerate(peers):
        starts.append(remote(small_s, smalls_s.at[f], start_send.at[0, i], start_recv.at[0, i], peer))
        starts[-1].start()
    for i, peer in enumerate(peers):
        mine = emb_ref.at[my_rows, my_half]
        starts.append(
            remote(mine, emball_s.at[f, my_rows, my_half], start_send.at[1, i], start_recv.at[1, i], peer)
        )
        starts[-1].start()
    for i, peer in enumerate(peers):
        tap, column = place_of(((c * 2 + x) * 2 + lax.rem(peer[0], 2)) * 4 + peer[0] // 2, TAPS, per_tap)
        mine = conv_ref.at[tap, :, pl.ds(pl.multiple_of(column * 128, 128), 128)]
        starts.append(remote(mine, wcol_s.at[f], start_send.at[2, i], start_recv.at[2, i], peer))
        starts[-1].start()

    fill_onehot(count, vocab, taps_s, onehot_s)
    cot_s[:, 0:EDGE, :] = jnp.zeros((rows, EDGE, width), BF16)
    cot_s[:, EDGE + half :, :] = jnp.zeros((rows, EDGE, width), BF16)

    for i in range(fs - 1):
        starts[i].wait_recv()
    line = jnp.zeros((16, width), F32)
    real_sum = jnp.zeros((1, 1), F32)
    lane = lax.broadcasted_iota(jnp.int32, (128, width), 0)
    at = lax.broadcasted_iota(jnp.int32, (128, width), 1)
    for g in range(fs):
        pick = jnp.where((at == lane + g * size) & (lane < size), 1.0, 0.0).astype(BF16)
        both = jnp.concatenate([smalls_s[g], jnp.zeros((8, 128), F32)], axis=0)
        keep = lax.broadcasted_iota(jnp.int32, (16, 128), 0) < 2
        line = line + jnp.dot(jnp.where(keep, both, 0.0).astype(BF16), pick, preferred_element_type=F32)
        real_sum = real_sum + smalls_s[g][2:3, 0:1]
    count_s[0] = jnp.broadcast_to(real_sum, (8, 128))
    count_x = remote(
        count_s.at[0], count_s.at[1], half_sem.at[0], half_sem.at[1], device_at(c, 1 - x, y, z)
    )
    count_x.start()
    line16 = line.astype(BF16)
    bias_column = jnp.concatenate([line, jnp.zeros((112, width), F32)], axis=0).T[:, 0:1]
    const = jnp.sum(line[0:1] * line[1:2], axis=1, keepdims=True)
    scorer = line16[1:2]
    local[0].wait()
    local[1].wait()
    across = (((1,), (1,)), ((), ()))
    u = jnp.concatenate(
        [
            lax.dot_general(line16, conv_s[k], across, preferred_element_type=F32)[1:2]
            for k in range(TAPS)
        ],
        axis=0,
    )
    u = jnp.concatenate(list(split3(u)) + [jnp.zeros((1, size), F32)], axis=0).astype(BF16)
    tq = jnp.dot(u, emb_s[...], preferred_element_type=F32)
    tq_s[...] = jnp.zeros_like(tq_s)
    tq_s[0:TAPS, :] = tq[0:TAPS] + tq[TAPS : 2 * TAPS] + tq[2 * TAPS : 3 * TAPS]
    tqs_s[f] = tq_s[...]
    tq_copies = []
    for i, peer in enumerate(peers):
        copy = remote(tq_s, tqs_s.at[f], start_send.at[3, i], start_recv.at[3, i], peer)
        copy.start()
        tq_copies.append(copy)

    for copy in local[2:4]:
        copy.wait()
    for i in range(fs - 1):
        starts[fs - 1 + i].wait_recv()
    mine = emball_s.at[:, my_rows, my_half]
    emb_x = remote(mine, mine, half_sem.at[6], half_sem.at[7], device_at(c, 1 - x, y, z))
    emb_x.start()
    emb_x.wait_recv()
    mine = emball_s.at[:, :, my_half]
    emb_core = remote(mine, mine, half_sem.at[2], half_sem.at[3], core)
    emb_core.start()
    for i in range(fs - 1):
        starts[2 * (fs - 1) + i].wait_recv()
    emb_core.wait_recv()
    block = lax.dot_general(
        wcol_s[...].reshape(fs * size, 128),
        emball_s[...].reshape(fs * size, vocab),
        (((0,), (0,)), ((), ())),
        preferred_element_type=F32,
    )
    table_s[c, x, y, z] = block.astype(BF16)
    tables = Gather(table_s, me, gather_send.at[0], gather_recv.at[0], TABLE_CHUNKS)
    for chunk in range(TABLE_CHUNKS):
        tables.along_z(chunk)

    count_x.wait_recv()
    count_s[2] = count_s[0] + count_s[1]
    count_c = remote(count_s.at[2], count_s.at[3], half_sem.at[4], half_sem.at[5], core)
    count_c.start()

    m = members_of(rows, length, seg_list, real_list)
    for copy in tq_copies:
        copy.wait_recv()
    tq = tqs_s[0]
    for g in range(1, fs):
        tq = tq + tqs_s[g]
    tq16 = jnp.concatenate(
        [
            jnp.concatenate(list(split3(tq[k : k + 1])) + [jnp.zeros((13, vocab), F32)], axis=0)
            for k in range(TAPS)
        ],
        axis=1,
    ).astype(BF16)
    fill_q(count, tq16, const, onehot_s, q_s)
    scores = block_scores(rows, length, m, q_s)

    part = 128 // TABLE_CHUNKS

    def table_rows(chunk):
        return jnp.concatenate(
            [
                jnp.concatenate(
                    [
                        table_s[(*static_place(k, j, per_tap), slice(chunk * part, (chunk + 1) * part))]
                        for j in range(per_tap)
                    ],
                    axis=0,
                )
                for k in range(TAPS)
            ],
            axis=1,
        )

    def hidden_part(chunk, low, high):
        if low == 0:
            tables.arrived(chunk)
        bias_part = jnp.concatenate(
            [bias_column[j * 128 + chunk * part : j * 128 + (chunk + 1) * part] for j in range(per_tap)], axis=0
        )

        def step(t, carry):
            lanes = pl.ds(pl.multiple_of(t * TILE, TILE), TILE)
            got = jnp.dot(table_rows(chunk), onehot_s[:, lanes], preferred_element_type=F32)
            got = (got + bias_part).astype(BF16)
            for j in range(per_tap):
                hidden_s[j * 128 + chunk * part : j * 128 + (chunk + 1) * part, lanes] = got[
                    j * part : (j + 1) * part
                ]
            return carry

        lax.fori_loop(count * low // 4, count * high // 4, step, 0)

    order = [(0, 0), (1, 0), (0, 1), (1, 1), (0, 2), (0, 0, 2), (1, 2), (0, 2, 4), (1, 0, 4)]
    steps = [
        functools.partial(tables.across if len(n) == 2 else hidden_part, *n) for n in order
    ]
    turns = {(0, 1): 1, (0, 3): 1, (1, 1): 1, (1, 3): 1}

    def between(r, t):
        for _ in range(turns.get((r, t), 0)):
            steps.pop(0)()

    def late_hidden():
        while steps:
            steps.pop(0)()
        tables.drain()
        for copy in local[4:]:
            copy.wait()
        count_c.wait_recv()

    def scale():
        return aux_ref[0, 0] / (count_s[2][0:1, 0:1] + count_s[3][0:1, 0:1])

    refs = (hidden_s, cot_s, band_s, pooled_s, hgrad_s, probs_s, similar_s, blocks_s, part_s, matrix_s, late_hidden)
    pool = middle(dims[:4], m, scores, seg_list, real_list, scale, scorer, refs, between)
    def product(slot):
        tap, column = place_of(jnp.minimum(slot, TAPS * per_tap - 2), TAPS, per_tap)
        symbols = pl.ds(pl.multiple_of(tap * vocab, vocab), vocab)
        lanes = pl.ds(pl.multiple_of(column * 128, 256), 256)
        return jnp.dot(onehot_s[symbols, :], hgrad_s[:, lanes], preferred_element_type=F32)

    def core_copy(p):
        return remote(give_s.at[p], take_s.at[p], core_send.at[p], core_recv.at[p], core)

    def quad_of(t):
        q = 3 - t // 2
        qx, qy = lax.rem(x + q // 2, 2), lax.rem(y + lax.rem(q, 2), 2)
        return qx, qy, qx * 4 + qy * 2 + lax.rem(t, 2)

    def give(t):
        p = quad_of(t)[2]
        give_s[p] = product((1 - c) * 16 + 2 * p)
        core_copy(p).start()

    def keep(t):
        p = quad_of(t)[2]
        got = product(c * 16 + 2 * p)
        core_copy(p).wait_recv()
        return got + take_s[p]

    gap = vocab // GRAD_CHUNKS

    def quad_copy(t, chunk):
        qx, qy, _ = quad_of(t)
        at = chunk * 6 + t
        ref = t, pl.ds(chunk * gap, gap)
        return remote(pass_s.at[ref], came_s.at[ref], quad_send.at[at], quad_recv.at[at], device_at(c, qx, qy, z))

    def pass_on(t):
        pass_s[t] = keep(t).astype(BF16)
        for chunk in range(GRAD_CHUNKS):
            quad_copy(t, chunk).start()

    def forward(t, carry):
        pass_on(t)
        give(t + 2)
        return carry

    give(jnp.int32(0))
    give(jnp.int32(1))
    lax.fori_loop(0, 6, forward, 0)
    own_s[0] = keep(jnp.int32(6))
    own_s[1] = keep(jnp.int32(7))

    pool()
    blocks_out = pltpu.make_async_copy(blocks_s, blocks_ref, local_sem.at[0])
    blocks_out.start()
    sums_s[0] = part_s[...]
    sum_copies = [remote(sums_s.at[0], sumr_s.at[0], sum_send.at[0], sum_recv.at[0], core)]
    sum_copies[0].start()

    def sums_quad():
        sum_copies[0].wait_recv()
        sums_s[1] = sums_s[0] + sumr_s[0]
        quad = [device_at(c, lax.rem(x + q // 2, 2), lax.rem(y + q % 2, 2), z) for q in range(4)]
        for q in range(1, 4):
            sum_copies.append(remote(sums_s.at[1], sumr_s.at[q], sum_send.at[q], sum_recv.at[q], quad[q]))
            sum_copies[-1].start()

    def sums_line():
        for q in range(1, 4):
            sum_copies[q].wait_recv()
        sums_s[2] = (sums_s[1] + sumr_s[1]) + (sumr_s[2] + sumr_s[3])
        for i in range(1, 4):
            to = device_at(c, x, y, lax.rem(z + i, 4))
            sum_copies.append(remote(sums_s.at[2], sumr_s.at[3 + i], sum_send.at[3 + i], sum_recv.at[3 + i], to))
            sum_copies[-1].start()

    grads = Gather(final_s, me, gather_send.at[1], gather_recv.at[1], GRAD_CHUNKS)
    line_copies = {}

    def to_line(chunk):
        part = slice(chunk * gap, (chunk + 1) * gap)
        for t in range(6):
            quad_copy(jnp.int32(t), chunk).wait_recv()
        for t in range(2):
            total = own_s[t, part]
            for q in range(1, 4):
                total = total + came_s[6 - 2 * q + t, part].astype(F32)
            for j in range(2):
                zown_s[2 * t + j, part] = total[:, j * 128 : (j + 1) * 128]
                zgive_s[2 * t + j, part] = total[:, j * 128 : (j + 1) * 128].astype(BF16)
        for i in range(1, 4):
            to = lax.rem(z + i, 4)
            at = chunk * 3 + i - 1
            part = pl.ds(chunk * gap, gap)
            copy = remote(
                zgive_s.at[to, part],
                zcame_s.at[i - 1, part],
                line_send.at[at],
                line_recv.at[at],
                device_at(c, x, y, to),
            )
            copy.start()
            line_copies[chunk, i] = copy

    def from_line(chunk):
        part = slice(chunk * gap, (chunk + 1) * gap)
        total = zown_s[z, part]
        for i in range(1, 4):
            line_copies[chunk, i].wait_recv()
            total = total + zcame_s[i - 1, part].astype(F32)
        final_s[c, x, y, z, part] = total.astype(BF16)
        grads.along_z(chunk)

    def put(chunk):
        part = pl.ds(chunk * gap, gap)
        ref = ALL, ALL, ALL, ALL, part
        out_copies.append(pltpu.make_async_copy(final_s.at[ref], final_ref.at[ref], local_sem.at[1 + chunk]))
        out_copies[-1].start()

    out_copies = []
    to_line(0)
    sums_quad()
    to_line(1)
    from_line(0)
    sums_line()
    from_line(1)
    grads.across(0, 0)
    grads.across(1, 0)
    grads.across(0, 1)
    grads.across(1, 1)
    grads.across(0, 2)
    grads.across(1, 2)
    grads.arrived(0)
    put(0)
    grads.arrived(1)
    put(1)
    grads.drain()

    for i in range(4, 7):
        sum_copies[i].wait_recv()
    sums = (sums_s[2] + sumr_s[4]) + (sumr_s[5] + sumr_s[6])
    total_count = count_s[2][0:1, 0:1] + count_s[3][0:1, 0:1]
    sums_ref[...] = jnp.concatenate([sums[0:1], sums[1:2] / total_count, sums[2:8]], axis=0)

    for copy in starts + tq_copies + sum_copies + list(line_copies.values()) + [count_x, count_c, emb_x, emb_core]:
        copy.wait_send()
    for p in range(8):
        core_copy(p).wait_send()
    for chunk in range(GRAD_CHUNKS):
        for t in range(6):
            quad_copy(jnp.int32(t), chunk).wait_send()
    for copy in out_copies + [blocks_out]:
        copy.wait()


def last_kernel(
    dims, blocks_ref, final_ref, sums_ref, emb_ref, conv_ref,
    out_ref, loss_ref, embg_ref, convg_ref, biasg_ref, scoreg_ref,
    blocks_s, final_s, emb_s, conv_s, convg_s, in_sem, out_sem,
):
    rows, length, width, vocab, size, fs = dims
    per_tap = width // 128
    copies = [
        pltpu.make_async_copy(emb_ref, emb_s, in_sem.at[0]),
        pltpu.make_async_copy(conv_ref, conv_s, in_sem.at[1]),
    ]
    for n in range(4):
        copies.append(
            pltpu.make_async_copy(final_ref.at[n // 2, n % 2], final_s.at[n // 2, n % 2], in_sem.at[2 + n])
        )
    blocks = [pltpu.make_async_copy(blocks_ref.at[r], blocks_s.at[r], in_sem.at[6 + r]) for r in range(rows)]
    for copy in copies + blocks:
        copy.start()
    outs = []
    have = 0
    copies[0].wait()
    copies[1].wait()
    emb_total = None
    for k in range(TAPS):
        while have * 8 < (k + 1) * per_tap:
            copies[2 + have].wait()
            have += 1
        grad = jnp.concatenate([final_s[static_place(k, j, per_tap)] for j in range(per_tap)], axis=1)
        convg_s[k] = jnp.dot(emb_s[...], grad, preferred_element_type=F32)
        outs.append(pltpu.make_async_copy(convg_s.at[k], convg_ref.at[k], out_sem.at[k]))
        outs[-1].start()
        term = lax.dot_general(conv_s[k], grad, (((1,), (1,)), ((), ())), preferred_element_type=F32)
        emb_total = term if emb_total is None else emb_total + term
        if k == TAPS // 2:
            bias_line = jnp.sum(grad.astype(F32), axis=0, keepdims=True)
        if k < rows:
            blocks[k].wait()
            outs.append(pltpu.make_async_copy(blocks_s.at[k], out_ref.at[k], out_sem.at[TAPS + k]))
            outs[-1].start()
    embg_ref[...] = emb_total
    f = lax.axis_index("fsdp")
    lane = lax.broadcasted_iota(jnp.int32, (128, width), 0)
    at = lax.broadcasted_iota(jnp.int32, (128, width), 1)
    pick = jnp.where((at == lane + f * size) & (lane < size), 1.0, 0.0).astype(BF16)
    lines = jnp.concatenate(
        list(split3(bias_line)) + list(split3(sums_ref[0:1])) + [jnp.zeros((10, width), F32)], axis=0
    ).astype(BF16)
    mine = lax.dot_general(lines, pick, (((1,), (1,)), ((), ())), preferred_element_type=F32)
    biasg_ref[...] = (mine[0:1] + mine[1:2] + mine[2:3])[:, :size]
    scoreg_ref[...] = (mine[3:4] + mine[4:5] + mine[5:6])[:, :size]
    loss_ref[...] = sums_ref[1:2, 0:1]
    while have < 4:
        copies[2 + have].wait()
        have += 1
    for copy in outs:
        copy.wait()


def step_shards(byte_ids, doc_lengths, pad_mask, embedding, conv_weight, conv_bias, scorer, cotangent, aux_weight):
    rows, length = byte_ids.shape
    vocab, size = embedding.shape
    width = conv_weight.shape[2]
    half = length // 2
    fs = width // size
    dims = (rows, length, width, vocab, size, fs)
    vmem = pl.BlockSpec(memory_space=pltpu.VMEM)
    smem = pl.BlockSpec(memory_space=pltpu.SMEM)
    hbm = pl.BlockSpec(memory_space=pl.ANY)
    dma = pltpu.SemaphoreType.DMA
    blocks, final, sums = pl.pallas_call(
        functools.partial(step_kernel, dims),
        out_shape=(
            jax.ShapeDtypeStruct((rows, half, width), BF16),
            jax.ShapeDtypeStruct((2, 2, 2, 4, vocab, 128), BF16),
            jax.ShapeDtypeStruct((8, width), F32),
        ),
        in_specs=[smem, smem, vmem, vmem, hbm, hbm, vmem, vmem, hbm],
        out_specs=(hbm, hbm, vmem),
        scratch_shapes=local_scratch(rows, length, width, vocab)
        + [
            pltpu.VMEM((rows, half, width), BF16),
            pltpu.VMEM((8, width), F32),
            pltpu.VMEM((TAPS, size, width), BF16),
            pltpu.VMEM((size, vocab), BF16),
            pltpu.VMEM((8, 128), F32),
            pltpu.VMEM((fs, 8, 128), F32),
            pltpu.VMEM((fs, size, 128), BF16),
            pltpu.VMEM((fs, size, vocab), BF16),
            pltpu.VMEM((8, vocab), F32),
            pltpu.VMEM((fs, 8, vocab), F32),
            pltpu.VMEM((4, 8, 128), F32),
            pltpu.VMEM((2, 2, 2, 4, 128, vocab), BF16),
            pltpu.VMEM((8, vocab, 256), F32),
            pltpu.VMEM((8, vocab, 256), F32),
            pltpu.VMEM((2, vocab, 256), F32),
            pltpu.VMEM((6, vocab, 256), BF16),
            pltpu.VMEM((6, vocab, 256), BF16),
            pltpu.VMEM((4, vocab, 128), BF16),
            pltpu.VMEM((4, vocab, 128), F32),
            pltpu.VMEM((3, vocab, 128), BF16),
            pltpu.VMEM((2, 2, 2, 4, vocab, 128), BF16),
            pltpu.VMEM((3, 8, width), F32),
            pltpu.VMEM((7, 8, width), F32),
            dma((4 + max(rows, 2),)),
            dma((4, fs - 1)),
            dma((4, fs - 1)),
            dma((8,)),
            dma((2, 11 * max(TABLE_CHUNKS, GRAD_CHUNKS))),
            dma((2, 11 * max(TABLE_CHUNKS, GRAD_CHUNKS))),
            dma((8,)),
            dma((8,)),
            dma((6 * GRAD_CHUNKS,)),
            dma((6 * GRAD_CHUNKS,)),
            dma((3 * GRAD_CHUNKS,)),
            dma((3 * GRAD_CHUNKS,)),
            dma((7,)),
            dma((7,)),
        ],
        compiler_params=pltpu.CompilerParams(
            collective_id=0, has_side_effects=True, vmem_limit_bytes=62 * 1024 * 1024
        ),
        name="step",
    )(
        doc_lengths,
        aux_weight.reshape(1, 1),
        byte_ids,
        pad_mask,
        embedding.T,
        conv_weight,
        conv_bias.reshape(1, size),
        scorer.reshape(1, size),
        cotangent,
    )
    blocks, loss, emb_grad, conv_grad, bias_grad, score_grad = pl.pallas_call(
        functools.partial(last_kernel, dims),
        out_shape=(
            jax.ShapeDtypeStruct((rows, half, width), BF16),
            jax.ShapeDtypeStruct((1, 1), F32),
            jax.ShapeDtypeStruct((size, vocab), F32),
            jax.ShapeDtypeStruct((TAPS, size, width), F32),
            jax.ShapeDtypeStruct((1, size), F32),
            jax.ShapeDtypeStruct((1, size), F32),
        ),
        in_specs=[hbm, hbm, vmem, hbm, hbm],
        out_specs=(hbm, vmem, vmem, hbm, vmem, vmem),
        scratch_shapes=[
            pltpu.VMEM((rows, half, width), BF16),
            pltpu.VMEM((2, 2, 2, 4, vocab, 128), BF16),
            pltpu.VMEM((size, vocab), BF16),
            pltpu.VMEM((TAPS, size, width), BF16),
            pltpu.VMEM((TAPS, size, width), F32),
            dma((6 + rows,)),
            dma((rows + TAPS,)),
        ],
        compiler_params=pltpu.CompilerParams(vmem_limit_bytes=62 * 1024 * 1024),
        name="last",
    )(blocks, final, sums, embedding.T, conv_weight)
    return blocks, loss.reshape(()), emb_grad.T, conv_grad, bias_grad.reshape(size), score_grad.reshape(size)


def split3_rows(x):
    a = lax.reduce_precision(x, 8, 7)
    b = lax.reduce_precision(x - a, 8, 7)
    return jnp.concatenate([a, b, x - a - b], axis=0).astype(BF16)


def gathered_shards(byte_ids, doc_lengths, pad_mask, embedding, conv_weight, conv_bias, scorer, cotangent, aux_weight):
    emb = lax.all_gather(embedding, "fsdp", axis=1, tiled=True)
    conv = lax.all_gather(conv_weight, "fsdp", axis=1, tiled=True)
    bias = lax.all_gather(conv_bias, "fsdp", axis=0, tiled=True)
    score = lax.all_gather(scorer, "fsdp", axis=0, tiled=True)
    vocab, width = emb.shape
    count = lax.psum(jnp.sum(pad_mask.astype(F32)), ("fsdp", "dp"))
    table = jnp.einsum("kcd,vc->dkv", conv, emb, preferred_element_type=F32).reshape(width, TAPS * vocab)
    score32 = score.astype(F32)
    q_table = jnp.sum(table * score32[:, None], axis=0, keepdims=True)
    tq = jnp.concatenate([split3_rows(q_table), jnp.zeros((13, TAPS * vocab), BF16)], axis=0)
    bias32 = bias.astype(F32)
    small = jnp.stack([jnp.full((128,), count), jnp.full((128,), jnp.sum(bias32 * score32))])
    small = jnp.concatenate([small, jnp.zeros((6, 128), F32)], axis=0)
    blocks, grad, part = main_call(
        doc_lengths, aux_weight.reshape(1, 1), small, byte_ids, pad_mask, table.astype(BF16), tq, bias32[:, None], score[None, :], cotangent
    )
    grad = lax.psum(grad, ("fsdp", "dp")).reshape(TAPS, vocab, width)
    score_grad = lax.psum(part[0], ("fsdp", "dp"))
    loss = lax.psum(part[1, 0], ("fsdp", "dp")) / count
    size = embedding.shape[1]
    at = lax.axis_index("fsdp") * size
    bias_grad = lax.dynamic_slice_in_dim(jnp.sum(grad[TAPS // 2], axis=0), at, size, 0)
    score_grad = lax.dynamic_slice_in_dim(score_grad, at, size, 0)
    conv_grad = jnp.einsum("vc,kvd->kcd", embedding.astype(F32), grad, precision=lax.Precision.HIGHEST)
    emb_grad = jnp.einsum("kvd,kcd->vc", grad, conv_weight.astype(F32), precision=lax.Precision.HIGHEST)
    return blocks, loss, emb_grad, conv_grad, bias_grad, score_grad


def solution(mesh):
    small = mesh.shape["fsdp"] == 8 and mesh.shape["dp"] == 4
    return jax.shard_map(
        step_shards if small else gathered_shards,
        mesh=mesh,
        in_specs=(
            P(("fsdp", "dp"), None),
            P(("fsdp", "dp"), None),
            P(("fsdp", "dp"), None),
            P(None, "fsdp"),
            P(None, "fsdp", None),
            P("fsdp"),
            P("fsdp"),
            P(("fsdp", "dp"), None, None),
            P(),
        ),
        out_specs=(
            P(("fsdp", "dp"), None, None),
            P(),
            P(None, "fsdp"),
            P(None, "fsdp", None),
            P("fsdp"),
            P("fsdp"),
        ),
        check_vma=False,
    )
```

```python
import functools
import jax
import jax.numpy as jnp
from jax import lax
from jax.experimental import pallas as pl
from jax.experimental.pallas import tpu as pltpu
from jax.sharding import PartitionSpec as P

TAPS = 5
SIZES = 4
NEG = -1000000000.0
F32 = jnp.float32
BF16 = jnp.bfloat16
TILE = 256
EDGE = 16
TABLE_CHUNKS = 2
GRAD_CHUNKS = 2


def split2(x):
    high = x.astype(BF16).astype(F32)
    return high, x - high


def shift(x, offset):
    length = x.shape[1]
    return x if offset == 0 else pltpu.roll(x, (-offset) % length, 1)


def group_pair(x, step, lane_bit):
    size = x.shape[0]
    down = pltpu.roll(x, (size - step) % size, 0)
    up = pltpu.roll(x, step, 0)
    return jnp.where(lane_bit, up, down)


def group_all(x, op, bits):
    x = op(x, group_pair(x, 1, bits[0]))
    return op(x, group_pair(x, 2, bits[1]))


def spread(rows_list, length):
    return jnp.concatenate([jnp.broadcast_to(x, (SIZES, length)) for x in rows_list], axis=0)


def lane_rows(ref, at, r, length):
    return ref[at : at + 1, r * length : (r + 1) * length]


DELTA_EVEN = {-3: -2, -2: -1, -1: -1, 0: 0, 1: 0, 2: 1, 3: 1}
DELTA_ODD = {-3: -1, -2: -1, -1: 0, 0: 0, 1: 1, 2: 1, 3: 2}
OFFSETS = [o for o in range(1 - SIZES, SIZES) if o != 0]


def row_masks(rows, length, len_ref, ids_ref, mask_ref, taps_s):
    place1 = lax.broadcasted_iota(jnp.int32, (1, length), 1)
    seg_list, real_list = [], []
    for r in range(rows):
        end = len_ref[r, 0]
        segment = jnp.where(place1 >= end, 1.0, 0.0)
        for d in range(1, len_ref.shape[1]):
            end = end + len_ref[r, d]
            segment = segment + jnp.where(place1 >= end, 1.0, 0.0)
        seg_list.append(segment)
        real_list.append(mask_ref[r : r + 1, :].astype(F32))
        ids = ids_ref[r : r + 1, :].astype(F32)
        known = jnp.where(real_list[r] > 0.5, ids, -1.0)
        for k in range(TAPS):
            o = k - TAPS // 2
            inside = (place1 + o >= 0) & (place1 + o < length)
            keep = inside & (shift(segment, o) == segment)
            taps_s[k : k + 1, r * length : (r + 1) * length] = jnp.where(
                keep, shift(known, o), -1.0
            ).astype(jnp.int32)
    return seg_list, real_list


def fill_onehot(count, vocab, taps_s, onehot_s):
    symbol = lax.broadcasted_iota(jnp.int32, (vocab, TILE), 0)

    def step(t, carry):
        lanes = pl.ds(pl.multiple_of(t * TILE, TILE), TILE)
        for k in range(TAPS):
            here = taps_s[k : k + 1, lanes]
            onehot_s[k * vocab : (k + 1) * vocab, lanes] = jnp.where(symbol == here, 1.0, 0.0).astype(BF16)
        return carry

    lax.fori_loop(0, count, step, 0)


def members_of(rows, length, seg_list, real_list):
    shape = (rows * SIZES, length)
    place = lax.broadcasted_iota(jnp.int32, shape, 1)
    sub = lax.broadcasted_iota(jnp.int32, shape, 0)
    size = (sub & (SIZES - 1)) + 1
    third = jnp.floor((place.astype(F32) + 0.5) * (1.0 / 3.0)).astype(jnp.int32)
    within = jnp.where(
        size == 1, 0, jnp.where(size == 2, place & 1, jnp.where(size == 3, place - 3 * third, place & 3))
    )
    seg = spread(seg_list, length)
    real = spread(real_list, length)
    same = {}
    for o in range(1, SIZES):
        ahead = (within + o < size) & (place + o < length) & (shift(seg, o) == seg)
        behind = (within - o >= 0) & (shift(seg, -o) == seg)
        same[o] = jnp.where(ahead, 1.0, 0.0)
        same[-o] = jnp.where(behind, 1.0, 0.0)
    member = {o: same[o] * shift(real, o) for o in OFFSETS}
    members = real
    for o in OFFSETS:
        members = members + member[o]
    even = (place & 1) == 0
    pair = jnp.where(even | (shift(seg, -1) == seg), real, 0.0)
    partner = jnp.where(even, shift(pair, 1), shift(pair, -1))
    return dict(
        bits=((sub & 1) == 1, (sub & 2) == 2),
        first=size == 1,
        even=even,
        real=real,
        same=same,
        member=member,
        inverse=1.0 / jnp.maximum(members, 1.0),
        pair_weight=pair / jnp.maximum(pair + partner, 1.0),
    )


def block_scores(rows, length, m, q_s):
    q = spread([lane_rows(q_s, 0, r, length) for r in range(rows)], length)
    total = q * m["real"]
    for o in OFFSETS:
        total = total + m["member"][o] * shift(q, o)
    return total * m["inverse"]


def calibrate_row(r, length, scores, seg, real, similar_s, probs_s, between):
    s = scores[r * SIZES : (r + 1) * SIZES]
    a, rest = split2(s)
    b, c = split2(rest)
    key_seg = jnp.where(real > 0.5, seg, -1.0)
    zero = jnp.zeros((128 - 6 * SIZES - 1, length), F32)
    left = jnp.concatenate([a, a, b, b, a, c, key_seg, zero], axis=0).T
    right = jnp.concatenate([a, b, a, b, c, a, jnp.zeros_like(key_seg), zero], axis=0).astype(BF16)
    key_column = left[:, 6 * SIZES : 6 * SIZES + 1]
    left = left.astype(BF16)
    x = jnp.concatenate(
        [jnp.ones((1, length), F32), s, s[0:1] * s, s[1:2] * s[1:], s[2:3] * s[2:], s[3:4] * s[3:]]
        + [jnp.zeros((1, length), F32)],
        axis=0,
    )
    x_high, x_low = split2(x)
    features = jnp.concatenate([x_high, x_low], axis=0).astype(BF16)
    outs = []
    for t in range(length // TILE):
        lanes = slice(t * TILE, (t + 1) * TILE)
        query_seg = seg[:, lanes]
        top = None
        for j in range(length // 128):
            keys = slice(j * 128, (j + 1) * 128)
            sim = jnp.dot(left[keys], right[:, lanes], preferred_element_type=F32)
            allowed = key_column[keys] == query_seg
            if j * 128 // TILE == t:
                key_place = lax.broadcasted_iota(jnp.int32, (128, TILE), 0) + j * 128
                query_place = lax.broadcasted_iota(jnp.int32, (128, TILE), 1) + t * TILE
                allowed = allowed | (key_place == query_place)
            sim = jnp.where(allowed, sim, NEG)
            similar_s[keys, :] = sim
            here = jnp.max(sim, axis=0, keepdims=True)
            top = here if top is None else jnp.maximum(top, here)
        for j in range(length // 128):
            keys = slice(j * 128, (j + 1) * 128)
            probs_s[r, keys, lanes] = jnp.exp(similar_s[keys, :] - top).astype(BF16)
        outs.append(jnp.dot(features, probs_s[r, :, lanes], preferred_element_type=F32))
        between(r, t)
    moments = jnp.concatenate(outs, axis=1)
    moments = moments[0:16] + moments[16:32]
    norm = 1.0 / moments[0:1]
    return moments * norm, norm


def size_softmax(cal, bits):
    top = group_all(cal, jnp.maximum, bits)
    log_weight = (cal - top) - jnp.log(group_all(jnp.exp(cal - top), jnp.add, bits))
    weight = jnp.exp(log_weight)
    entropy = -group_all(weight * log_weight, jnp.add, bits)
    return weight, log_weight, entropy


def band_products(rows, length, cot_s, hidden_s, band_s, window, diagonal):
    for r in range(rows):
        for t in range(length // TILE):
            lanes = slice(r * length + t * TILE, r * length + (t + 1) * TILE)
            first = t * TILE // 2
            prod = jnp.dot(
                cot_s[r, first : first + window, :], hidden_s[:, lanes], preferred_element_type=F32
            )
            for d in range(-2, 3):
                band_s[d + 2 : d + 3, lanes] = jnp.sum(jnp.where(diagonal == d, prod, 0.0), axis=0, keepdims=True)


def calibrate_back(r, length, scores, cal_grad, inner, moments, norm, probs_s):
    part = slice(r * SIZES, (r + 1) * SIZES)
    s, g, ri = scores[part], cal_grad[part], inner[r * SIZES : r * SIZES + 1]
    at = {}
    n = 1 + SIZES
    for a in range(SIZES):
        for b in range(a, SIZES):
            at[a, b] = at[b, a] = n
            n += 1
    query = []
    for a in range(SIZES):
        total = -moments[1 + a : 2 + a] * ri
        for b in range(SIZES):
            total = total + moments[at[a, b] : at[a, b] + 1] * g[b : b + 1]
        query.append(total)
    y = jnp.concatenate([g - s * ri] + [s[a : a + 1] * g for a in range(SIZES)], axis=0) * norm
    y = jnp.concatenate([y, jnp.zeros((4, length), F32)], axis=0)
    y_high, y_low = split2(y)
    features = jnp.concatenate([y_high, y_low], axis=0).astype(BF16)
    outs = []
    for t in range(length // TILE):
        keys = slice(t * TILE, (t + 1) * TILE)
        outs.append(
            lax.dot_general(features, probs_s[r, keys, :], (((1,), (1,)), ((), ())), preferred_element_type=F32)
        )
    back = jnp.concatenate(outs, axis=1)
    back = back[0:24] + back[24:48]
    key = []
    for a in range(SIZES):
        total = back[a : a + 1]
        for b in range(SIZES):
            n = SIZES + a * SIZES + b
            total = total + s[b : b + 1] * back[n : n + 1]
        key.append(total + query[a])
    return jnp.concatenate(key, axis=0)


def middle(dims, m, scores, seg_list, real_list, scale, scorer, refs, between):
    rows, length, width, vocab = dims
    half = length // 2
    tiles = length // TILE
    window = TILE // 2 + 2 * EDGE
    hidden_s, cot_s, band_s, pooled_s, hgrad_s, probs_s, similar_s, blocks_ref, part_ref, matrix_s, late_hidden = refs
    bits, real, same, member, inverse, pair_weight = (
        m[n] for n in ("bits", "real", "same", "member", "inverse", "pair_weight")
    )
    kept = [
        calibrate_row(r, length, scores, seg_list[r], real_list[r], similar_s, probs_s, between) for r in range(rows)
    ]
    cal = jnp.concatenate([moments[1 : 1 + SIZES] for moments, norm in kept], axis=0)
    weight, log_weight, entropy = size_softmax(cal, bits)
    entropy_sum = jnp.sum(
        jnp.sum(jnp.where(m["first"], entropy * real, 0.0), axis=1, keepdims=True), axis=0, keepdims=True
    )
    part_ref[...] = jnp.zeros_like(part_ref)
    part_ref[1:2, :] = jnp.broadcast_to(entropy_sum, (1, width))
    for r in range(rows):
        pooled_s[r] = jnp.zeros_like(pooled_s[r])

    use = pair_weight * weight * inverse
    moved = {o: (use if o == 0 else same[o] * shift(use, o)) for o in range(1 - SIZES, SIZES)}
    mix = []
    for d in range(-2, 3):
        odd_sum = sum([moved[o] for o in moved if DELTA_ODD[o] == d], jnp.zeros_like(use))
        even_sum = sum([moved[o] for o in moved if DELTA_EVEN[o] == d], jnp.zeros_like(use))
        mix.append(group_all(jnp.where(m["even"], even_sum, odd_sum) * real, jnp.add, bits))

    kl = lax.broadcasted_iota(jnp.int32, (window, TILE), 0)
    diagonal = kl - (lax.broadcasted_iota(jnp.int32, (window, TILE), 1) // 2 + EDGE)
    for r in range(rows):
        at = r * SIZES
        for t in range(tiles):
            lanes = slice(t * TILE, (t + 1) * TILE)
            matrix = jnp.zeros((window, TILE), F32)
            for d in range(-2, 3):
                matrix = jnp.where(diagonal == d, mix[d + 2][at : at + 1, lanes], matrix)
            high, low = split2(matrix)
            matrix_s[r * tiles + t, 0:window] = high.astype(BF16)
            matrix_s[r * tiles + t, window : 2 * window] = low.astype(BF16)

    late_hidden()
    band_products(rows, length, cot_s, hidden_s, band_s, window, diagonal)
    even1 = (lax.broadcasted_iota(jnp.int32, (1, length), 1) & 1) == 0
    band = [[lane_rows(band_s, d + 2, r, length) for d in range(-2, 3)] for r in range(rows)]

    def product(o):
        return spread(
            [jnp.where(even1, band[r][DELTA_EVEN[o] + 2], band[r][DELTA_ODD[o] + 2]) for r in range(rows)], length
        )

    gathered = real * product(0)
    for o in OFFSETS:
        gathered = gathered + member[o] * shift(product(-o), o)
    weight_grad = pair_weight * inverse * gathered
    cal_grad = weight * (weight_grad - group_all(weight * weight_grad, jnp.add, bits))
    cal_grad = cal_grad - scale() * real * weight * (log_weight + entropy)
    inner = group_all(cal * cal_grad, jnp.add, bits)
    score_grad = jnp.concatenate(
        [calibrate_back(r, length, scores, cal_grad, inner, kept[r][0], kept[r][1], probs_s) for r in range(rows)],
        axis=0,
    )
    score_grad = score_grad * inverse
    q_grad = score_grad
    for o in OFFSETS:
        q_grad = q_grad + same[o] * shift(score_grad, o)
    q_grad = group_all(q_grad * real, jnp.add, bits)

    scorer16 = jnp.concatenate([scorer, scorer, jnp.zeros((EDGE - 2, width), BF16)], axis=0)
    for r in range(rows):
        at = r * SIZES
        q_high, q_low = split2(q_grad[at : at + 1])
        for t in range(tiles):
            lanes = slice(t * TILE, (t + 1) * TILE)
            all_lanes = slice(r * length + t * TILE, r * length + (t + 1) * TILE)
            first = t * TILE // 2
            matrix_s[r * tiles + t, 2 * window :] = jnp.concatenate(
                [q_high[:, lanes], q_low[:, lanes], jnp.zeros((EDGE - 2, TILE), F32)], axis=0
            ).astype(BF16)
            here = cot_s[r, first : first + window, :]
            given = jnp.concatenate([here, here, scorer16], axis=0)
            hgrad_s[all_lanes, :] = lax.dot_general(
                matrix_s[r * tiles + t], given, (((0,), (0,)), ((), ())), preferred_element_type=F32
            ).astype(BF16)

    def pool():
        for r in range(rows):
            for t in range(tiles):
                first = t * TILE // 2
                out = lax.dot_general(
                    matrix_s[r * tiles + t],
                    hidden_s[:, r * length + t * TILE : r * length + (t + 1) * TILE],
                    (((1,), (1,)), ((), ())),
                    preferred_element_type=F32,
                )
                pooled_s[r, first : first + window, :] += out[:window] + out[window : 2 * window]
                part_ref[0:1, :] += out[2 * window : 2 * window + 1] + out[2 * window + 1 : 2 * window + 2]
            blocks_ref[r] = pooled_s[r, EDGE : EDGE + half, :].astype(BF16)

    return pool


def fill_cotangent(rows, half, width, cot_ref, cot_s):
    cot_s[:, 0:EDGE, :] = jnp.zeros((rows, EDGE, width), BF16)
    cot_s[:, EDGE + half :, :] = jnp.zeros((rows, EDGE, width), BF16)
    for r in range(rows):
        cot_s[r, EDGE : EDGE + half, :] = cot_ref[r]


def fill_q(count, tq16, const, onehot_s, q_s):
    def step(t, carry):
        lanes = pl.ds(pl.multiple_of(t * TILE, TILE), TILE)
        got = jnp.dot(tq16, onehot_s[:, lanes], preferred_element_type=F32)
        q_s[0:1, lanes] = got[0:1] + got[1:2] + got[2:3] + const
        return carry

    lax.fori_loop(0, count, step, 0)


def fill_hidden(count, table, bias_column, onehot_s, hidden_s):
    def step(t, carry):
        lanes = pl.ds(pl.multiple_of(t * TILE, TILE), TILE)
        got = jnp.dot(table(), onehot_s[:, lanes], preferred_element_type=F32)
        hidden_s[:, lanes] = (got + bias_column).astype(BF16)
        return carry

    lax.fori_loop(0, count, step, 0)


def local_scratch(rows, length, width, vocab):
    half = length // 2
    return [
        pltpu.VMEM((8, rows * length), jnp.int32),
        pltpu.VMEM((TAPS * vocab, rows * length), BF16),
        pltpu.VMEM((width, rows * length), BF16),
        pltpu.VMEM((8, rows * length), F32),
        pltpu.VMEM((rows, length, length), BF16),
        pltpu.VMEM((length, TILE), F32),
        pltpu.VMEM((rows, half + 2 * EDGE, width), BF16),
        pltpu.VMEM((8, rows * length), F32),
        pltpu.VMEM((rows, half + 2 * EDGE, width), F32),
        pltpu.VMEM((rows * length, width), BF16),
        pltpu.VMEM((rows * (length // TILE), TILE + 5 * EDGE, TILE), BF16),
    ]


def main_kernel(
    dims, len_ref, aux_ref, small_ref, ids_ref, mask_ref, table_ref, tq_ref, bias_ref, scorer_ref, cot_ref,
    blocks_ref, grad_ref, part_ref,
    taps_s, onehot_s, hidden_s, q_s, probs_s, similar_s, cot_s, band_s, pooled_s, hgrad_s, matrix_s,
):
    rows, length, width, vocab = dims
    count = rows * (length // TILE)
    seg_list, real_list = row_masks(rows, length, len_ref, ids_ref, mask_ref, taps_s)
    fill_cotangent(rows, length // 2, width, cot_ref, cot_s)
    fill_onehot(count, vocab, taps_s, onehot_s)
    m = members_of(rows, length, seg_list, real_list)
    fill_q(count, tq_ref[...], small_ref[1:2, 0:1], onehot_s, q_s)
    scores = block_scores(rows, length, m, q_s)

    def late_hidden():
        fill_hidden(count, lambda: table_ref[...], bias_ref[...], onehot_s, hidden_s)

    def scale():
        return aux_ref[0, 0] / small_ref[0:1, 0:1]

    refs = (hidden_s, cot_s, band_s, pooled_s, hgrad_s, probs_s, similar_s, blocks_ref, part_ref, matrix_s, late_hidden)
    pool = middle(dims, m, scores, seg_list, real_list, scale, scorer_ref[...], refs, lambda r, t: None)
    pool()

    def grad_step(k, carry):
        symbols = pl.ds(pl.multiple_of(k * vocab, vocab), vocab)
        for c in range(width // TILE):
            cols = slice(c * TILE, (c + 1) * TILE)
            grad_ref[symbols, cols] = jnp.dot(
                onehot_s[symbols, :], hgrad_s[:, cols], preferred_element_type=F32
            )
        return carry

    lax.fori_loop(0, TAPS, grad_step, 0)


def main_call(lengths, aux, small, ids, mask, table, tq, bias, scorer, cot):
    rows, length = ids.shape
    width = cot.shape[2]
    vocab = table.shape[1] // TAPS
    dims = (rows, length, width, vocab)
    vmem = pl.BlockSpec(memory_space=pltpu.VMEM)
    smem = pl.BlockSpec(memory_space=pltpu.SMEM)
    half = length // 2
    return pl.pallas_call(
        functools.partial(main_kernel, dims),
        out_shape=(
            jax.ShapeDtypeStruct((rows, half, width), BF16),
            jax.ShapeDtypeStruct((TAPS * vocab, width), F32),
            jax.ShapeDtypeStruct((8, width), F32),
        ),
        in_specs=[smem, smem] + [vmem] * 8,
        out_specs=(vmem, vmem, vmem),
        scratch_shapes=local_scratch(rows, length, width, vocab),
        compiler_params=pltpu.CompilerParams(vmem_limit_bytes=60 * 1024 * 1024),
        name="latent",
    )(lengths, aux, small, ids, mask, table, tq, bias, scorer, cot)


MESH = pl.DeviceIdType.MESH
ALL = slice(None)


def split3(x):
    a = x.astype(BF16).astype(F32)
    b = (x - a).astype(BF16).astype(F32)
    return a, b, x - a - b


def remote(src, dst, send, recv, device):
    return pltpu.make_async_remote_copy(
        src_ref=src, dst_ref=dst, send_sem=send, recv_sem=recv, device_id=device, device_id_type=MESH
    )


def device_at(c, x, y, z):
    return (z * 2 + y, x * 2 + c)


class Gather:
    def __init__(self, buf, me, send, recv, chunks):
        self.buf, self.me, self.send, self.recv, self.chunks = buf, me, send, recv, chunks
        self.rows = buf.shape[4] // chunks
        self.copies = {}

    def part(self, c, x, y, z, chunk, half=None):
        if half is None:
            return self.buf.at[c, x, y, z, pl.ds(chunk * self.rows, self.rows)]
        return self.buf.at[c, x, y, z, pl.ds(chunk * self.rows + half * (self.rows // 2), self.rows // 2)]

    def go(self, chunk, n, ref, device):
        at = chunk * 11 + n
        copy = remote(ref, ref, self.send.at[at], self.recv.at[at], device)
        copy.start()
        self.copies[chunk, n] = copy

    def along_z(self, chunk):
        c, x, y, z = self.me
        for i in range(1, 4):
            self.go(chunk, i - 1, self.part(c, x, y, z, chunk), device_at(c, x, y, lax.rem(z + i, 4)))

    def across(self, chunk, step):
        c, x, y, z = self.me
        copies = self.copies
        core, over_x, over_y = device_at(1 - c, x, y, z), device_at(c, 1 - x, y, z), device_at(c, x, 1 - y, z)
        if step == 0:
            for n in range(3):
                copies[chunk, n].wait_recv()
            mine = self.part(c, x, y, ALL, chunk)
            self.go(chunk, 3, mine, over_x)
            self.go(chunk, 4, mine, over_y)
            self.go(chunk, 5, mine, core)
        elif step == 1:
            copies[chunk, 3].wait_recv()
            self.go(chunk, 6, self.part(c, 1 - x, y, ALL, chunk, 0), over_y)
            self.go(chunk, 7, self.part(c, 1 - x, y, ALL, chunk), core)
            copies[chunk, 4].wait_recv()
            self.go(chunk, 8, self.part(c, x, 1 - y, ALL, chunk, 1), over_x)
            self.go(chunk, 9, self.part(c, x, 1 - y, ALL, chunk), core)
        else:
            copies[chunk, 6].wait_recv()
            copies[chunk, 8].wait_recv()
            self.go(chunk, 10, self.part(c, 1 - x, 1 - y, ALL, chunk), core)

    def arrived(self, chunk):
        for n in (5, 7, 9, 10):
            self.copies[chunk, n].wait_recv()

    def drain(self):
        for copy in self.copies.values():
            copy.wait_send()


def place_of(slot, taps, per_tap):
    slot = jnp.minimum(slot, taps * per_tap - 1)
    tap = slot // per_tap
    return tap, slot - tap * per_tap


def static_place(tap, column, per_tap):
    slot = tap * per_tap + column
    return slot // 16, slot // 8 % 2, slot // 4 % 2, slot % 4


def step_kernel(
    dims,
    len_in, aux_in, ids_in, mask_in, emb_ref, conv_ref, bias_in, scorer_in, cot_ref,
    blocks_ref, final_ref, sums_out,
    taps_s, onehot_s, hidden_s, q_s, probs_s, similar_s, cot_s, band_s, pooled_s, hgrad_s, matrix_s,
    blocks_s, part_s, conv_s, emb_s,
    small_s, smalls_s, wcol_s, emball_s, tq_s, tqs_s, count_s, table_s,
    give_s, take_s, own_s, pass_s, came_s, zgive_s, zown_s, zcame_s, final_s, sums_s, sumr_s,
    local_sem, start_send, start_recv, half_sem, gather_send, gather_recv,
    core_send, core_recv, quad_send, quad_recv, line_send, line_recv, sum_send, sum_recv,
    len_ref, aux_ref, ids_ref, mask_ref, bias_ref, scorer_ref, sums_ref, in_sem,
):
    rows, length, width, vocab, size, fs = dims
    half = length // 2
    count = rows * (length // TILE)
    per_tap = width // 128
    f, d = lax.axis_index("fsdp"), lax.axis_index("dp")
    z, y = f // 2, lax.rem(f, 2)
    x, c = d // 2, lax.rem(d, 2)
    me = (c, x, y, z)
    core = device_at(1 - c, x, y, z)

    barrier = pltpu.get_barrier_semaphore()
    peers = [(lax.rem(f + i, fs), d) for i in range(1, fs)]
    others = [core, device_at(c, 1 - x, y, z), device_at(c, 1 - x, 1 - y, z)]
    for peer in peers + others:
        pl.semaphore_signal(barrier, inc=1, device_id=peer, device_id_type=MESH)

    inputs = [
        pltpu.make_async_copy(source, target, in_sem.at[n])
        for n, (source, target) in enumerate(
            [
                (len_in, len_ref),
                (ids_in, ids_ref),
                (mask_in, mask_ref),
                (bias_in, bias_ref),
                (scorer_in, scorer_ref),
                (aux_in, aux_ref),
            ]
        )
    ]
    for copy in inputs:
        copy.start()
    mid = vocab // 2
    my_half = pl.ds(pl.multiple_of(c * mid, mid), mid)
    my_rows = pl.ds(pl.multiple_of(x * (size // 2), size // 2), size // 2)
    my_tap, my_column = place_of(((c * 2 + x) * 2 + y) * 4 + z, TAPS, per_tap)
    local = [
        pltpu.make_async_copy(conv_ref, conv_s, local_sem.at[0]),
        pltpu.make_async_copy(emb_ref, emb_s, local_sem.at[1]),
        pltpu.make_async_copy(
            conv_ref.at[my_tap, :, pl.ds(pl.multiple_of(my_column * 128, 128), 128)], wcol_s.at[f], local_sem.at[2]
        ),
        pltpu.make_async_copy(emb_ref.at[my_rows, my_half], emball_s.at[f, my_rows, my_half], local_sem.at[3]),
    ]
    for r in range(rows):
        local.append(pltpu.make_async_copy(cot_ref.at[r], cot_s.at[r, pl.ds(EDGE, half)], local_sem.at[4 + r]))
    for copy in local:
        copy.start()
    for copy in inputs:
        copy.wait()
    real_here = jnp.sum(jnp.sum(mask_ref[...].astype(F32), axis=1, keepdims=True), axis=0, keepdims=True)
    small_s[...] = jnp.zeros_like(small_s)
    small_s[0:1, 0:size] = bias_ref[...].astype(F32)
    small_s[1:2, 0:size] = scorer_ref[...].astype(F32)
    small_s[2:3, :] = jnp.broadcast_to(real_here, (1, 128))
    smalls_s[f] = small_s[...]
    seg_list, real_list = row_masks(rows, length, len_ref, ids_ref, mask_ref, taps_s)

    pl.semaphore_wait(barrier, fs - 1 + 3)
    starts = []
    for i, peer in enumerate(peers):
        starts.append(remote(small_s, smalls_s.at[f], start_send.at[0, i], start_recv.at[0, i], peer))
        starts[-1].start()
    for i, peer in enumerate(peers):
        mine = emb_ref.at[my_rows, my_half]
        starts.append(
            remote(mine, emball_s.at[f, my_rows, my_half], start_send.at[1, i], start_recv.at[1, i], peer)
        )
        starts[-1].start()
    for i, peer in enumerate(peers):
        tap, column = place_of(((c * 2 + x) * 2 + lax.rem(peer[0], 2)) * 4 + peer[0] // 2, TAPS, per_tap)
        mine = conv_ref.at[tap, :, pl.ds(pl.multiple_of(column * 128, 128), 128)]
        starts.append(remote(mine, wcol_s.at[f], start_send.at[2, i], start_recv.at[2, i], peer))
        starts[-1].start()

    fill_onehot(count, vocab, taps_s, onehot_s)
    cot_s[:, 0:EDGE, :] = jnp.zeros((rows, EDGE, width), BF16)
    cot_s[:, EDGE + half :, :] = jnp.zeros((rows, EDGE, width), BF16)

    for i in range(fs - 1):
        starts[i].wait_recv()
    line = jnp.zeros((16, width), F32)
    real_sum = jnp.zeros((1, 1), F32)
    lane = lax.broadcasted_iota(jnp.int32, (128, width), 0)
    at = lax.broadcasted_iota(jnp.int32, (128, width), 1)
    for g in range(fs):
        pick = jnp.where((at == lane + g * size) & (lane < size), 1.0, 0.0).astype(BF16)
        both = jnp.concatenate([smalls_s[g], jnp.zeros((8, 128), F32)], axis=0)
        keep = lax.broadcasted_iota(jnp.int32, (16, 128), 0) < 2
        line = line + jnp.dot(jnp.where(keep, both, 0.0).astype(BF16), pick, preferred_element_type=F32)
        real_sum = real_sum + smalls_s[g][2:3, 0:1]
    count_s[0] = jnp.broadcast_to(real_sum, (8, 128))
    count_x = remote(
        count_s.at[0], count_s.at[1], half_sem.at[0], half_sem.at[1], device_at(c, 1 - x, y, z)
    )
    count_x.start()
    line16 = line.astype(BF16)
    bias_column = jnp.concatenate([line, jnp.zeros((112, width), F32)], axis=0).T[:, 0:1]
    const = jnp.sum(line[0:1] * line[1:2], axis=1, keepdims=True)
    scorer = line16[1:2]
    local[0].wait()
    local[1].wait()
    across = (((1,), (1,)), ((), ()))
    u = jnp.concatenate(
        [
            lax.dot_general(line16, conv_s[k], across, preferred_element_type=F32)[1:2]
            for k in range(TAPS)
        ],
        axis=0,
    )
    u = jnp.concatenate(list(split3(u)) + [jnp.zeros((1, size), F32)], axis=0).astype(BF16)
    tq = jnp.dot(u, emb_s[...], preferred_element_type=F32)
    tq_s[...] = jnp.zeros_like(tq_s)
    tq_s[0:TAPS, :] = tq[0:TAPS] + tq[TAPS : 2 * TAPS] + tq[2 * TAPS : 3 * TAPS]
    tqs_s[f] = tq_s[...]
    tq_copies = []
    for i, peer in enumerate(peers):
        copy = remote(tq_s, tqs_s.at[f], start_send.at[3, i], start_recv.at[3, i], peer)
        copy.start()
        tq_copies.append(copy)

    for copy in local[2:4]:
        copy.wait()
    for i in range(fs - 1):
        starts[fs - 1 + i].wait_recv()
    mine = emball_s.at[:, my_rows, my_half]
    emb_x = remote(mine, mine, half_sem.at[6], half_sem.at[7], device_at(c, 1 - x, y, z))
    emb_x.start()
    emb_x.wait_recv()
    mine = emball_s.at[:, :, my_half]
    emb_core = remote(mine, mine, half_sem.at[2], half_sem.at[3], core)
    emb_core.start()
    for i in range(fs - 1):
        starts[2 * (fs - 1) + i].wait_recv()
    emb_core.wait_recv()
    block = lax.dot_general(
        wcol_s[...].reshape(fs * size, 128),
        emball_s[...].reshape(fs * size, vocab),
        (((0,), (0,)), ((), ())),
        preferred_element_type=F32,
    )
    table_s[c, x, y, z] = block.astype(BF16)
    tables = Gather(table_s, me, gather_send.at[0], gather_recv.at[0], TABLE_CHUNKS)
    for chunk in range(TABLE_CHUNKS):
        tables.along_z(chunk)

    count_x.wait_recv()
    count_s[2] = count_s[0] + count_s[1]
    count_c = remote(count_s.at[2], count_s.at[3], half_sem.at[4], half_sem.at[5], core)
    count_c.start()

    m = members_of(rows, length, seg_list, real_list)
    for copy in tq_copies:
        copy.wait_recv()
    tq = tqs_s[0]
    for g in range(1, fs):
        tq = tq + tqs_s[g]
    tq16 = jnp.concatenate(
        [
            jnp.concatenate(list(split3(tq[k : k + 1])) + [jnp.zeros((13, vocab), F32)], axis=0)
            for k in range(TAPS)
        ],
        axis=1,
    ).astype(BF16)
    fill_q(count, tq16, const, onehot_s, q_s)
    scores = block_scores(rows, length, m, q_s)

    part = 128 // TABLE_CHUNKS

    def table_rows(chunk):
        return jnp.concatenate(
            [
                jnp.concatenate(
                    [
                        table_s[(*static_place(k, j, per_tap), slice(chunk * part, (chunk + 1) * part))]
                        for j in range(per_tap)
                    ],
                    axis=0,
                )
                for k in range(TAPS)
            ],
            axis=1,
        )

    def hidden_part(chunk, low, high):
        if low == 0:
            tables.arrived(chunk)
        bias_part = jnp.concatenate(
            [bias_column[j * 128 + chunk * part : j * 128 + (chunk + 1) * part] for j in range(per_tap)], axis=0
        )

        def step(t, carry):
            lanes = pl.ds(pl.multiple_of(t * TILE, TILE), TILE)
            got = jnp.dot(table_rows(chunk), onehot_s[:, lanes], preferred_element_type=F32)
            got = (got + bias_part).astype(BF16)
            for j in range(per_tap):
                hidden_s[j * 128 + chunk * part : j * 128 + (chunk + 1) * part, lanes] = got[
                    j * part : (j + 1) * part
                ]
            return carry

        lax.fori_loop(count * low // 4, count * high // 4, step, 0)

    order = [(0, 0), (1, 0), (0, 1), (1, 1), (0, 2), (0, 0, 2), (1, 2), (0, 2, 4), (1, 0, 4)]
    steps = [
        functools.partial(tables.across if len(n) == 2 else hidden_part, *n) for n in order
    ]
    turns = {(0, 1): 1, (0, 3): 1, (1, 1): 1, (1, 3): 1}

    def between(r, t):
        for _ in range(turns.get((r, t), 0)):
            steps.pop(0)()

    def late_hidden():
        while steps:
            steps.pop(0)()
        tables.drain()
        for copy in local[4:]:
            copy.wait()
        count_c.wait_recv()

    def scale():
        return aux_ref[0, 0] / (count_s[2][0:1, 0:1] + count_s[3][0:1, 0:1])

    refs = (hidden_s, cot_s, band_s, pooled_s, hgrad_s, probs_s, similar_s, blocks_s, part_s, matrix_s, late_hidden)
    pool = middle(dims[:4], m, scores, seg_list, real_list, scale, scorer, refs, between)
    def product(slot):
        tap, column = place_of(jnp.minimum(slot, TAPS * per_tap - 2), TAPS, per_tap)
        symbols = pl.ds(pl.multiple_of(tap * vocab, vocab), vocab)
        lanes = pl.ds(pl.multiple_of(column * 128, 256), 256)
        return jnp.dot(onehot_s[symbols, :], hgrad_s[:, lanes], preferred_element_type=F32)

    def core_copy(p):
        return remote(give_s.at[p], take_s.at[p], core_send.at[p], core_recv.at[p], core)

    def quad_of(t):
        q = 3 - t // 2
        qx, qy = lax.rem(x + q // 2, 2), lax.rem(y + lax.rem(q, 2), 2)
        return qx, qy, qx * 4 + qy * 2 + lax.rem(t, 2)

    def give(t):
        p = quad_of(t)[2]
        give_s[p] = product((1 - c) * 16 + 2 * p)
        core_copy(p).start()

    def keep(t):
        p = quad_of(t)[2]
        got = product(c * 16 + 2 * p)
        core_copy(p).wait_recv()
        return got + take_s[p]

    gap = vocab // GRAD_CHUNKS

    def quad_copy(t, chunk):
        qx, qy, _ = quad_of(t)
        at = chunk * 6 + t
        ref = t, pl.ds(chunk * gap, gap)
        return remote(pass_s.at[ref], came_s.at[ref], quad_send.at[at], quad_recv.at[at], device_at(c, qx, qy, z))

    def pass_on(t):
        pass_s[t] = keep(t).astype(BF16)
        for chunk in range(GRAD_CHUNKS):
            quad_copy(t, chunk).start()

    def forward(t, carry):
        pass_on(t)
        give(t + 2)
        return carry

    give(jnp.int32(0))
    give(jnp.int32(1))
    lax.fori_loop(0, 6, forward, 0)
    own_s[0] = keep(jnp.int32(6))
    own_s[1] = keep(jnp.int32(7))

    pool()
    blocks_out = pltpu.make_async_copy(blocks_s, blocks_ref, local_sem.at[0])
    blocks_out.start()
    sums_s[0] = part_s[...]
    sum_copies = [remote(sums_s.at[0], sumr_s.at[0], sum_send.at[0], sum_recv.at[0], core)]
    sum_copies[0].start()

    def sums_quad():
        sum_copies[0].wait_recv()
        sums_s[1] = sums_s[0] + sumr_s[0]
        quad = [device_at(c, lax.rem(x + q // 2, 2), lax.rem(y + q % 2, 2), z) for q in range(4)]
        for q in range(1, 4):
            sum_copies.append(remote(sums_s.at[1], sumr_s.at[q], sum_send.at[q], sum_recv.at[q], quad[q]))
            sum_copies[-1].start()

    def sums_line():
        for q in range(1, 4):
            sum_copies[q].wait_recv()
        sums_s[2] = (sums_s[1] + sumr_s[1]) + (sumr_s[2] + sumr_s[3])
        for i in range(1, 4):
            to = device_at(c, x, y, lax.rem(z + i, 4))
            sum_copies.append(remote(sums_s.at[2], sumr_s.at[3 + i], sum_send.at[3 + i], sum_recv.at[3 + i], to))
            sum_copies[-1].start()

    grads = Gather(final_s, me, gather_send.at[1], gather_recv.at[1], GRAD_CHUNKS)
    line_copies = {}

    def to_line(chunk):
        part = slice(chunk * gap, (chunk + 1) * gap)
        for t in range(6):
            quad_copy(jnp.int32(t), chunk).wait_recv()
        for t in range(2):
            total = own_s[t, part]
            for q in range(1, 4):
                total = total + came_s[6 - 2 * q + t, part].astype(F32)
            for j in range(2):
                zown_s[2 * t + j, part] = total[:, j * 128 : (j + 1) * 128]
                zgive_s[2 * t + j, part] = total[:, j * 128 : (j + 1) * 128].astype(BF16)
        for i in range(1, 4):
            to = lax.rem(z + i, 4)
            at = chunk * 3 + i - 1
            part = pl.ds(chunk * gap, gap)
            copy = remote(
                zgive_s.at[to, part],
                zcame_s.at[i - 1, part],
                line_send.at[at],
                line_recv.at[at],
                device_at(c, x, y, to),
            )
            copy.start()
            line_copies[chunk, i] = copy

    def from_line(chunk):
        part = slice(chunk * gap, (chunk + 1) * gap)
        total = zown_s[z, part]
        for i in range(1, 4):
            line_copies[chunk, i].wait_recv()
            total = total + zcame_s[i - 1, part].astype(F32)
        final_s[c, x, y, z, part] = total.astype(BF16)
        grads.along_z(chunk)

    def put(chunk):
        part = pl.ds(chunk * gap, gap)
        ref = ALL, ALL, ALL, ALL, part
        out_copies.append(pltpu.make_async_copy(final_s.at[ref], final_ref.at[ref], local_sem.at[1 + chunk]))
        out_copies[-1].start()

    out_copies = []
    to_line(0)
    sums_quad()
    to_line(1)
    from_line(0)
    sums_line()
    from_line(1)
    grads.across(0, 0)
    grads.across(1, 0)
    grads.across(0, 1)
    grads.across(1, 1)
    grads.across(0, 2)
    grads.across(1, 2)
    grads.arrived(0)
    put(0)
    grads.arrived(1)
    put(1)
    grads.drain()

    for i in range(4, 7):
        sum_copies[i].wait_recv()
    sums = (sums_s[2] + sumr_s[4]) + (sumr_s[5] + sumr_s[6])
    total_count = count_s[2][0:1, 0:1] + count_s[3][0:1, 0:1]
    sums_ref[...] = jnp.concatenate([sums[0:1], sums[1:2] / total_count, sums[2:8]], axis=0)
    out_copies.append(pltpu.make_async_copy(sums_ref, sums_out, in_sem.at[0]))
    out_copies[-1].start()

    for copy in starts + tq_copies + sum_copies + list(line_copies.values()) + [count_x, count_c, emb_x, emb_core]:
        copy.wait_send()
    for p in range(8):
        core_copy(p).wait_send()
    for chunk in range(GRAD_CHUNKS):
        for t in range(6):
            quad_copy(jnp.int32(t), chunk).wait_send()
    for copy in out_copies + [blocks_out]:
        copy.wait()


def last_kernel(
    dims, blocks_ref, final_ref, sums_in, emb_ref, conv_ref,
    out_ref, loss_out, embg_out, convg_ref, biasg_out, scoreg_out,
    blocks_s, final_s, emb_s, conv_s, convg_s, in_sem, out_sem,
    sums_ref, loss_ref, embg_ref, biasg_ref, scoreg_ref,
):
    rows, length, width, vocab, size, fs = dims
    per_tap = width // 128
    copies = [
        pltpu.make_async_copy(emb_ref, emb_s, in_sem.at[0]),
        pltpu.make_async_copy(conv_ref, conv_s, in_sem.at[1]),
    ]
    for n in range(4):
        copies.append(
            pltpu.make_async_copy(final_ref.at[n // 2, n % 2], final_s.at[n // 2, n % 2], in_sem.at[2 + n])
        )
    blocks = [pltpu.make_async_copy(blocks_ref.at[r], blocks_s.at[r], in_sem.at[6 + r]) for r in range(rows)]
    copies.append(pltpu.make_async_copy(sums_in, sums_ref, in_sem.at[6 + rows]))
    for copy in copies + blocks:
        copy.start()
    outs = []
    have = 0
    copies[0].wait()
    copies[1].wait()
    emb_total = None
    for k in range(TAPS):
        while have * 8 < (k + 1) * per_tap:
            copies[2 + have].wait()
            have += 1
        grad = jnp.concatenate([final_s[static_place(k, j, per_tap)] for j in range(per_tap)], axis=1)
        convg_s[k] = jnp.dot(emb_s[...], grad, preferred_element_type=F32)
        outs.append(pltpu.make_async_copy(convg_s.at[k], convg_ref.at[k], out_sem.at[k]))
        outs[-1].start()
        term = lax.dot_general(conv_s[k], grad, (((1,), (1,)), ((), ())), preferred_element_type=F32)
        emb_total = term if emb_total is None else emb_total + term
        if k == TAPS // 2:
            bias_line = jnp.sum(grad.astype(F32), axis=0, keepdims=True)
        if k < rows:
            blocks[k].wait()
            outs.append(pltpu.make_async_copy(blocks_s.at[k], out_ref.at[k], out_sem.at[TAPS + k]))
            outs[-1].start()
    embg_ref[...] = emb_total
    copies[6].wait()
    f = lax.axis_index("fsdp")
    lane = lax.broadcasted_iota(jnp.int32, (128, width), 0)
    at = lax.broadcasted_iota(jnp.int32, (128, width), 1)
    pick = jnp.where((at == lane + f * size) & (lane < size), 1.0, 0.0).astype(BF16)
    lines = jnp.concatenate(
        list(split3(bias_line)) + list(split3(sums_ref[0:1])) + [jnp.zeros((10, width), F32)], axis=0
    ).astype(BF16)
    mine = lax.dot_general(lines, pick, (((1,), (1,)), ((), ())), preferred_element_type=F32)
    biasg_ref[...] = (mine[0:1] + mine[1:2] + mine[2:3])[:, :size]
    scoreg_ref[...] = (mine[3:4] + mine[4:5] + mine[5:6])[:, :size]
    loss_ref[...] = sums_ref[1:2, 0:1]
    for n, (source, target) in enumerate(
        [(embg_ref, embg_out), (biasg_ref, biasg_out), (scoreg_ref, scoreg_out), (loss_ref, loss_out)]
    ):
        outs.append(pltpu.make_async_copy(source, target, out_sem.at[TAPS + rows + n]))
        outs[-1].start()
    while have < 4:
        copies[2 + have].wait()
        have += 1
    for copy in outs:
        copy.wait()


def step_shards(byte_ids, doc_lengths, pad_mask, embedding, conv_weight, conv_bias, scorer, cotangent, aux_weight):
    rows, length = byte_ids.shape
    vocab, size = embedding.shape
    width = conv_weight.shape[2]
    half = length // 2
    fs = width // size
    dims = (rows, length, width, vocab, size, fs)
    hbm = pl.BlockSpec(memory_space=pl.ANY)
    dma = pltpu.SemaphoreType.DMA
    blocks, final, sums = pl.pallas_call(
        functools.partial(step_kernel, dims),
        out_shape=(
            jax.ShapeDtypeStruct((rows, half, width), BF16),
            jax.ShapeDtypeStruct((2, 2, 2, 4, vocab, 128), BF16),
            jax.ShapeDtypeStruct((8, width), F32),
        ),
        in_specs=[hbm] * 9,
        out_specs=(hbm, hbm, hbm),
        scratch_shapes=local_scratch(rows, length, width, vocab)
        + [
            pltpu.VMEM((rows, half, width), BF16),
            pltpu.VMEM((8, width), F32),
            pltpu.VMEM((TAPS, size, width), BF16),
            pltpu.VMEM((size, vocab), BF16),
            pltpu.VMEM((8, 128), F32),
            pltpu.VMEM((fs, 8, 128), F32),
            pltpu.VMEM((fs, size, 128), BF16),
            pltpu.VMEM((fs, size, vocab), BF16),
            pltpu.VMEM((8, vocab), F32),
            pltpu.VMEM((fs, 8, vocab), F32),
            pltpu.VMEM((4, 8, 128), F32),
            pltpu.VMEM((2, 2, 2, 4, 128, vocab), BF16),
            pltpu.VMEM((8, vocab, 256), F32),
            pltpu.VMEM((8, vocab, 256), F32),
            pltpu.VMEM((2, vocab, 256), F32),
            pltpu.VMEM((6, vocab, 256), BF16),
            pltpu.VMEM((6, vocab, 256), BF16),
            pltpu.VMEM((4, vocab, 128), BF16),
            pltpu.VMEM((4, vocab, 128), F32),
            pltpu.VMEM((3, vocab, 128), BF16),
            pltpu.VMEM((2, 2, 2, 4, vocab, 128), BF16),
            pltpu.VMEM((3, 8, width), F32),
            pltpu.VMEM((7, 8, width), F32),
            dma((4 + max(rows, 2),)),
            dma((4, fs - 1)),
            dma((4, fs - 1)),
            dma((8,)),
            dma((2, 11 * max(TABLE_CHUNKS, GRAD_CHUNKS))),
            dma((2, 11 * max(TABLE_CHUNKS, GRAD_CHUNKS))),
            dma((8,)),
            dma((8,)),
            dma((6 * GRAD_CHUNKS,)),
            dma((6 * GRAD_CHUNKS,)),
            dma((3 * GRAD_CHUNKS,)),
            dma((3 * GRAD_CHUNKS,)),
            dma((7,)),
            dma((7,)),
            pltpu.SMEM(doc_lengths.shape, jnp.int32),
            pltpu.SMEM((1, 1), F32),
            pltpu.VMEM((rows, length), jnp.int32),
            pltpu.VMEM((rows, length), jnp.int32),
            pltpu.VMEM((1, size), BF16),
            pltpu.VMEM((1, size), BF16),
            pltpu.VMEM((8, width), F32),
            dma((6,)),
        ],
        compiler_params=pltpu.CompilerParams(
            collective_id=0, has_side_effects=True, vmem_limit_bytes=62 * 1024 * 1024
        ),
        name="step",
    )(
        doc_lengths,
        aux_weight.reshape(1, 1),
        byte_ids,
        pad_mask,
        embedding.T,
        conv_weight,
        conv_bias.reshape(1, size),
        scorer.reshape(1, size),
        cotangent,
    )
    blocks, loss, emb_grad, conv_grad, bias_grad, score_grad = pl.pallas_call(
        functools.partial(last_kernel, dims),
        out_shape=(
            jax.ShapeDtypeStruct((rows, half, width), BF16),
            jax.ShapeDtypeStruct((1, 1), F32),
            jax.ShapeDtypeStruct((size, vocab), F32),
            jax.ShapeDtypeStruct((TAPS, size, width), F32),
            jax.ShapeDtypeStruct((1, size), F32),
            jax.ShapeDtypeStruct((1, size), F32),
        ),
        in_specs=[hbm] * 5,
        out_specs=(hbm,) * 6,
        scratch_shapes=[
            pltpu.VMEM((rows, half, width), BF16),
            pltpu.VMEM((2, 2, 2, 4, vocab, 128), BF16),
            pltpu.VMEM((size, vocab), BF16),
            pltpu.VMEM((TAPS, size, width), BF16),
            pltpu.VMEM((TAPS, size, width), F32),
            dma((7 + rows,)),
            dma((rows + TAPS + 4,)),
            pltpu.VMEM((8, width), F32),
            pltpu.VMEM((1, 1), F32),
            pltpu.VMEM((size, vocab), F32),
            pltpu.VMEM((1, size), F32),
            pltpu.VMEM((1, size), F32),
        ],
        compiler_params=pltpu.CompilerParams(vmem_limit_bytes=62 * 1024 * 1024),
        name="last",
    )(blocks, final, sums, embedding.T, conv_weight)
    return blocks, loss.reshape(()), emb_grad.T, conv_grad, bias_grad.reshape(size), score_grad.reshape(size)


def split3_rows(x):
    a = lax.reduce_precision(x, 8, 7)
    b = lax.reduce_precision(x - a, 8, 7)
    return jnp.concatenate([a, b, x - a - b], axis=0).astype(BF16)


def gathered_shards(byte_ids, doc_lengths, pad_mask, embedding, conv_weight, conv_bias, scorer, cotangent, aux_weight):
    emb = lax.all_gather(embedding, "fsdp", axis=1, tiled=True)
    conv = lax.all_gather(conv_weight, "fsdp", axis=1, tiled=True)
    bias = lax.all_gather(conv_bias, "fsdp", axis=0, tiled=True)
    score = lax.all_gather(scorer, "fsdp", axis=0, tiled=True)
    vocab, width = emb.shape
    count = lax.psum(jnp.sum(pad_mask.astype(F32)), ("fsdp", "dp"))
    table = jnp.einsum("kcd,vc->dkv", conv, emb, preferred_element_type=F32).reshape(width, TAPS * vocab)
    score32 = score.astype(F32)
    q_table = jnp.sum(table * score32[:, None], axis=0, keepdims=True)
    tq = jnp.concatenate([split3_rows(q_table), jnp.zeros((13, TAPS * vocab), BF16)], axis=0)
    bias32 = bias.astype(F32)
    small = jnp.stack([jnp.full((128,), count), jnp.full((128,), jnp.sum(bias32 * score32))])
    small = jnp.concatenate([small, jnp.zeros((6, 128), F32)], axis=0)
    blocks, grad, part = main_call(
        doc_lengths, aux_weight.reshape(1, 1), small, byte_ids, pad_mask, table.astype(BF16), tq, bias32[:, None], score[None, :], cotangent
    )
    grad = lax.psum(grad, ("fsdp", "dp")).reshape(TAPS, vocab, width)
    score_grad = lax.psum(part[0], ("fsdp", "dp"))
    loss = lax.psum(part[1, 0], ("fsdp", "dp")) / count
    size = embedding.shape[1]
    at = lax.axis_index("fsdp") * size
    bias_grad = lax.dynamic_slice_in_dim(jnp.sum(grad[TAPS // 2], axis=0), at, size, 0)
    score_grad = lax.dynamic_slice_in_dim(score_grad, at, size, 0)
    conv_grad = jnp.einsum("vc,kvd->kcd", embedding.astype(F32), grad, precision=lax.Precision.HIGHEST)
    emb_grad = jnp.einsum("kvd,kcd->vc", grad, conv_weight.astype(F32), precision=lax.Precision.HIGHEST)
    return blocks, loss, emb_grad, conv_grad, bias_grad, score_grad


def solution(mesh):
    small = mesh.shape["fsdp"] == 8 and mesh.shape["dp"] == 4
    return jax.shard_map(
        step_shards if small else gathered_shards,
        mesh=mesh,
        in_specs=(
            P(("fsdp", "dp"), None),
            P(("fsdp", "dp"), None),
            P(("fsdp", "dp"), None),
            P(None, "fsdp"),
            P(None, "fsdp", None),
            P("fsdp"),
            P("fsdp"),
            P(("fsdp", "dp"), None, None),
            P(),
        ),
        out_specs=(
            P(("fsdp", "dp"), None, None),
            P(),
            P(None, "fsdp"),
            P(None, "fsdp", None),
            P("fsdp"),
            P("fsdp"),
        ),
        check_vma=False,
    )
```

```python
import functools
import jax
import jax.numpy as jnp
from jax import lax
from jax.experimental import pallas as pl
from jax.experimental.pallas import tpu as pltpu
from jax.sharding import PartitionSpec as P

TAPS = 5
SIZES = 4
NEG = -1000000000.0
F32 = jnp.float32
BF16 = jnp.bfloat16
TILE = 256
EDGE = 16
TABLE_CHUNKS = 2
GRAD_CHUNKS = 2


def split2(x):
    high = x.astype(BF16).astype(F32)
    return high, x - high


def shift(x, offset):
    length = x.shape[1]
    return x if offset == 0 else pltpu.roll(x, (-offset) % length, 1)


def group_pair(x, step, lane_bit):
    size = x.shape[0]
    down = pltpu.roll(x, (size - step) % size, 0)
    up = pltpu.roll(x, step, 0)
    return jnp.where(lane_bit, up, down)


def group_all(x, op, bits):
    x = op(x, group_pair(x, 1, bits[0]))
    return op(x, group_pair(x, 2, bits[1]))


def spread(rows_list, length):
    return jnp.concatenate([jnp.broadcast_to(x, (SIZES, length)) for x in rows_list], axis=0)


def lane_rows(ref, at, r, length):
    return ref[at : at + 1, r * length : (r + 1) * length]


DELTA_EVEN = {-3: -2, -2: -1, -1: -1, 0: 0, 1: 0, 2: 1, 3: 1}
DELTA_ODD = {-3: -1, -2: -1, -1: 0, 0: 0, 1: 1, 2: 1, 3: 2}
OFFSETS = [o for o in range(1 - SIZES, SIZES) if o != 0]


def row_masks(rows, length, len_ref, ids_ref, mask_ref, taps_s):
    place1 = lax.broadcasted_iota(jnp.int32, (1, length), 1)
    seg_list, real_list = [], []
    for r in range(rows):
        end = len_ref[r, 0]
        segment = jnp.where(place1 >= end, 1.0, 0.0)
        for d in range(1, len_ref.shape[1]):
            end = end + len_ref[r, d]
            segment = segment + jnp.where(place1 >= end, 1.0, 0.0)
        seg_list.append(segment)
        real_list.append(mask_ref[r : r + 1, :].astype(F32))
        ids = ids_ref[r : r + 1, :].astype(F32)
        known = jnp.where(real_list[r] > 0.5, ids, -1.0)
        for k in range(TAPS):
            o = k - TAPS // 2
            inside = (place1 + o >= 0) & (place1 + o < length)
            keep = inside & (shift(segment, o) == segment)
            taps_s[k : k + 1, r * length : (r + 1) * length] = jnp.where(
                keep, shift(known, o), -1.0
            ).astype(jnp.int32)
    return seg_list, real_list


def fill_onehot(count, vocab, taps_s, onehot_s):
    symbol = lax.broadcasted_iota(jnp.int32, (vocab, TILE), 0)

    def step(t, carry):
        lanes = pl.ds(pl.multiple_of(t * TILE, TILE), TILE)
        for k in range(TAPS):
            here = taps_s[k : k + 1, lanes]
            onehot_s[k * vocab : (k + 1) * vocab, lanes] = jnp.where(symbol == here, 1.0, 0.0).astype(BF16)
        return carry

    lax.fori_loop(0, count, step, 0)


def members_of(rows, length, seg_list, real_list):
    shape = (rows * SIZES, length)
    place = lax.broadcasted_iota(jnp.int32, shape, 1)
    sub = lax.broadcasted_iota(jnp.int32, shape, 0)
    size = (sub & (SIZES - 1)) + 1
    third = jnp.floor((place.astype(F32) + 0.5) * (1.0 / 3.0)).astype(jnp.int32)
    within = jnp.where(
        size == 1, 0, jnp.where(size == 2, place & 1, jnp.where(size == 3, place - 3 * third, place & 3))
    )
    seg = spread(seg_list, length)
    real = spread(real_list, length)
    same = {}
    for o in range(1, SIZES):
        ahead = (within + o < size) & (place + o < length) & (shift(seg, o) == seg)
        behind = (within - o >= 0) & (shift(seg, -o) == seg)
        same[o] = jnp.where(ahead, 1.0, 0.0)
        same[-o] = jnp.where(behind, 1.0, 0.0)
    member = {o: same[o] * shift(real, o) for o in OFFSETS}
    members = real
    for o in OFFSETS:
        members = members + member[o]
    even = (place & 1) == 0
    pair = jnp.where(even | (shift(seg, -1) == seg), real, 0.0)
    partner = jnp.where(even, shift(pair, 1), shift(pair, -1))
    return dict(
        bits=((sub & 1) == 1, (sub & 2) == 2),
        first=size == 1,
        even=even,
        real=real,
        same=same,
        member=member,
        inverse=1.0 / jnp.maximum(members, 1.0),
        pair_weight=pair / jnp.maximum(pair + partner, 1.0),
    )


def block_scores(rows, length, m, q_s):
    q = spread([lane_rows(q_s, 0, r, length) for r in range(rows)], length)
    total = q * m["real"]
    for o in OFFSETS:
        total = total + m["member"][o] * shift(q, o)
    return total * m["inverse"]


def calibrate_row(r, length, scores, seg, real, similar_s, probs_s, between):
    s = scores[r * SIZES : (r + 1) * SIZES]
    a, rest = split2(s)
    b, c = split2(rest)
    key_seg = jnp.where(real > 0.5, seg, -1.0)
    zero = jnp.zeros((128 - 6 * SIZES - 1, length), F32)
    left = jnp.concatenate([a, a, b, b, a, c, key_seg, zero], axis=0).T
    right = jnp.concatenate([a, b, a, b, c, a, jnp.zeros_like(key_seg), zero], axis=0).astype(BF16)
    key_column = left[:, 6 * SIZES : 6 * SIZES + 1]
    left = left.astype(BF16)
    x = jnp.concatenate(
        [jnp.ones((1, length), F32), s, s[0:1] * s, s[1:2] * s[1:], s[2:3] * s[2:], s[3:4] * s[3:]]
        + [jnp.zeros((1, length), F32)],
        axis=0,
    )
    x_high, x_low = split2(x)
    features = jnp.concatenate([x_high, x_low], axis=0).astype(BF16)
    outs = []
    for t in range(length // TILE):
        lanes = slice(t * TILE, (t + 1) * TILE)
        query_seg = seg[:, lanes]
        top = None
        for j in range(length // 128):
            keys = slice(j * 128, (j + 1) * 128)
            sim = jnp.dot(left[keys], right[:, lanes], preferred_element_type=F32)
            allowed = key_column[keys] == query_seg
            if j * 128 // TILE == t:
                key_place = lax.broadcasted_iota(jnp.int32, (128, TILE), 0) + j * 128
                query_place = lax.broadcasted_iota(jnp.int32, (128, TILE), 1) + t * TILE
                allowed = allowed | (key_place == query_place)
            sim = jnp.where(allowed, sim, NEG)
            similar_s[keys, :] = sim
            here = jnp.max(sim, axis=0, keepdims=True)
            top = here if top is None else jnp.maximum(top, here)
        for j in range(length // 128):
            keys = slice(j * 128, (j + 1) * 128)
            probs_s[r, keys, lanes] = jnp.exp(similar_s[keys, :] - top).astype(BF16)
        outs.append(jnp.dot(features, probs_s[r, :, lanes], preferred_element_type=F32))
        between(r, t)
    moments = jnp.concatenate(outs, axis=1)
    moments = moments[0:16] + moments[16:32]
    norm = 1.0 / moments[0:1]
    return moments * norm, norm


def size_softmax(cal, bits):
    top = group_all(cal, jnp.maximum, bits)
    log_weight = (cal - top) - jnp.log(group_all(jnp.exp(cal - top), jnp.add, bits))
    weight = jnp.exp(log_weight)
    entropy = -group_all(weight * log_weight, jnp.add, bits)
    return weight, log_weight, entropy


def band_products(rows, length, cot_s, hidden_s, band_s, window, diagonal):
    for r in range(rows):
        for t in range(length // TILE):
            lanes = slice(r * length + t * TILE, r * length + (t + 1) * TILE)
            first = t * TILE // 2
            prod = jnp.dot(
                cot_s[r, first : first + window, :], hidden_s[:, lanes], preferred_element_type=F32
            )
            for d in range(-2, 3):
                band_s[d + 2 : d + 3, lanes] = jnp.sum(jnp.where(diagonal == d, prod, 0.0), axis=0, keepdims=True)


def calibrate_back(r, length, scores, cal_grad, inner, moments, norm, probs_s):
    part = slice(r * SIZES, (r + 1) * SIZES)
    s, g, ri = scores[part], cal_grad[part], inner[r * SIZES : r * SIZES + 1]
    at = {}
    n = 1 + SIZES
    for a in range(SIZES):
        for b in range(a, SIZES):
            at[a, b] = at[b, a] = n
            n += 1
    query = []
    for a in range(SIZES):
        total = -moments[1 + a : 2 + a] * ri
        for b in range(SIZES):
            total = total + moments[at[a, b] : at[a, b] + 1] * g[b : b + 1]
        query.append(total)
    y = jnp.concatenate([g - s * ri] + [s[a : a + 1] * g for a in range(SIZES)], axis=0) * norm
    y = jnp.concatenate([y, jnp.zeros((4, length), F32)], axis=0)
    y_high, y_low = split2(y)
    features = jnp.concatenate([y_high, y_low], axis=0).astype(BF16)
    outs = []
    for t in range(length // TILE):
        keys = slice(t * TILE, (t + 1) * TILE)
        outs.append(
            lax.dot_general(features, probs_s[r, keys, :], (((1,), (1,)), ((), ())), preferred_element_type=F32)
        )
    back = jnp.concatenate(outs, axis=1)
    back = back[0:24] + back[24:48]
    key = []
    for a in range(SIZES):
        total = back[a : a + 1]
        for b in range(SIZES):
            n = SIZES + a * SIZES + b
            total = total + s[b : b + 1] * back[n : n + 1]
        key.append(total + query[a])
    return jnp.concatenate(key, axis=0)


def middle(dims, m, scores, seg_list, real_list, scale, scorer, refs, between):
    rows, length, width, vocab = dims
    half = length // 2
    tiles = length // TILE
    window = TILE // 2 + 2 * EDGE
    hidden_s, cot_s, band_s, pooled_s, hgrad_s, probs_s, similar_s, blocks_ref, part_ref, matrix_s, late_hidden = refs
    bits, real, same, member, inverse, pair_weight = (
        m[n] for n in ("bits", "real", "same", "member", "inverse", "pair_weight")
    )
    kept = [
        calibrate_row(r, length, scores, seg_list[r], real_list[r], similar_s, probs_s, between) for r in range(rows)
    ]
    cal = jnp.concatenate([moments[1 : 1 + SIZES] for moments, norm in kept], axis=0)
    weight, log_weight, entropy = size_softmax(cal, bits)
    entropy_sum = jnp.sum(
        jnp.sum(jnp.where(m["first"], entropy * real, 0.0), axis=1, keepdims=True), axis=0, keepdims=True
    )
    part_ref[...] = jnp.zeros_like(part_ref)
    part_ref[1:2, :] = jnp.broadcast_to(entropy_sum, (1, width))
    for r in range(rows):
        pooled_s[r] = jnp.zeros_like(pooled_s[r])

    use = pair_weight * weight * inverse
    moved = {o: (use if o == 0 else same[o] * shift(use, o)) for o in range(1 - SIZES, SIZES)}
    mix = []
    for d in range(-2, 3):
        odd_sum = sum([moved[o] for o in moved if DELTA_ODD[o] == d], jnp.zeros_like(use))
        even_sum = sum([moved[o] for o in moved if DELTA_EVEN[o] == d], jnp.zeros_like(use))
        mix.append(group_all(jnp.where(m["even"], even_sum, odd_sum) * real, jnp.add, bits))

    kl = lax.broadcasted_iota(jnp.int32, (window, TILE), 0)
    diagonal = kl - (lax.broadcasted_iota(jnp.int32, (window, TILE), 1) // 2 + EDGE)
    for r in range(rows):
        at = r * SIZES
        for t in range(tiles):
            lanes = slice(t * TILE, (t + 1) * TILE)
            matrix = jnp.zeros((window, TILE), F32)
            for d in range(-2, 3):
                matrix = jnp.where(diagonal == d, mix[d + 2][at : at + 1, lanes], matrix)
            high, low = split2(matrix)
            matrix_s[r * tiles + t, 0:window] = high.astype(BF16)
            matrix_s[r * tiles + t, window : 2 * window] = low.astype(BF16)

    late_hidden()
    band_products(rows, length, cot_s, hidden_s, band_s, window, diagonal)
    even1 = (lax.broadcasted_iota(jnp.int32, (1, length), 1) & 1) == 0
    band = [[lane_rows(band_s, d + 2, r, length) for d in range(-2, 3)] for r in range(rows)]

    def product(o):
        return spread(
            [jnp.where(even1, band[r][DELTA_EVEN[o] + 2], band[r][DELTA_ODD[o] + 2]) for r in range(rows)], length
        )

    gathered = real * product(0)
    for o in OFFSETS:
        gathered = gathered + member[o] * shift(product(-o), o)
    weight_grad = pair_weight * inverse * gathered
    cal_grad = weight * (weight_grad - group_all(weight * weight_grad, jnp.add, bits))
    cal_grad = cal_grad - scale() * real * weight * (log_weight + entropy)
    inner = group_all(cal * cal_grad, jnp.add, bits)
    score_grad = jnp.concatenate(
        [calibrate_back(r, length, scores, cal_grad, inner, kept[r][0], kept[r][1], probs_s) for r in range(rows)],
        axis=0,
    )
    score_grad = score_grad * inverse
    q_grad = score_grad
    for o in OFFSETS:
        q_grad = q_grad + same[o] * shift(score_grad, o)
    q_grad = group_all(q_grad * real, jnp.add, bits)

    scorer16 = jnp.concatenate([scorer, scorer, jnp.zeros((EDGE - 2, width), BF16)], axis=0)
    for r in range(rows):
        at = r * SIZES
        q_high, q_low = split2(q_grad[at : at + 1])
        for t in range(tiles):
            lanes = slice(t * TILE, (t + 1) * TILE)
            all_lanes = slice(r * length + t * TILE, r * length + (t + 1) * TILE)
            first = t * TILE // 2
            matrix_s[r * tiles + t, 2 * window :] = jnp.concatenate(
                [q_high[:, lanes], q_low[:, lanes], jnp.zeros((EDGE - 2, TILE), F32)], axis=0
            ).astype(BF16)
            here = cot_s[r, first : first + window, :]
            given = jnp.concatenate([here, here, scorer16], axis=0)
            hgrad_s[all_lanes, :] = lax.dot_general(
                matrix_s[r * tiles + t], given, (((0,), (0,)), ((), ())), preferred_element_type=F32
            ).astype(BF16)

    def pool():
        for r in range(rows):
            for t in range(tiles):
                first = t * TILE // 2
                out = lax.dot_general(
                    matrix_s[r * tiles + t],
                    hidden_s[:, r * length + t * TILE : r * length + (t + 1) * TILE],
                    (((1,), (1,)), ((), ())),
                    preferred_element_type=F32,
                )
                pooled_s[r, first : first + window, :] += out[:window] + out[window : 2 * window]
                part_ref[0:1, :] += out[2 * window : 2 * window + 1] + out[2 * window + 1 : 2 * window + 2]
            blocks_ref[r] = pooled_s[r, EDGE : EDGE + half, :].astype(BF16)

    return pool


def fill_cotangent(rows, half, width, cot_ref, cot_s):
    cot_s[:, 0:EDGE, :] = jnp.zeros((rows, EDGE, width), BF16)
    cot_s[:, EDGE + half :, :] = jnp.zeros((rows, EDGE, width), BF16)
    for r in range(rows):
        cot_s[r, EDGE : EDGE + half, :] = cot_ref[r]


def fill_q(count, tq16, const, onehot_s, q_s):
    def step(t, carry):
        lanes = pl.ds(pl.multiple_of(t * TILE, TILE), TILE)
        got = jnp.dot(tq16, onehot_s[:, lanes], preferred_element_type=F32)
        q_s[0:1, lanes] = got[0:1] + got[1:2] + got[2:3] + const
        return carry

    lax.fori_loop(0, count, step, 0)


def fill_hidden(count, table, bias_column, onehot_s, hidden_s):
    def step(t, carry):
        lanes = pl.ds(pl.multiple_of(t * TILE, TILE), TILE)
        got = jnp.dot(table(), onehot_s[:, lanes], preferred_element_type=F32)
        hidden_s[:, lanes] = (got + bias_column).astype(BF16)
        return carry

    lax.fori_loop(0, count, step, 0)


def local_scratch(rows, length, width, vocab):
    half = length // 2
    return [
        pltpu.VMEM((8, rows * length), jnp.int32),
        pltpu.VMEM((TAPS * vocab, rows * length), BF16),
        pltpu.VMEM((width, rows * length), BF16),
        pltpu.VMEM((8, rows * length), F32),
        pltpu.VMEM((rows, length, length), BF16),
        pltpu.VMEM((length, TILE), F32),
        pltpu.VMEM((rows, half + 2 * EDGE, width), BF16),
        pltpu.VMEM((8, rows * length), F32),
        pltpu.VMEM((rows, half + 2 * EDGE, width), F32),
        pltpu.VMEM((rows * length, width), BF16),
        pltpu.VMEM((rows * (length // TILE), TILE + 5 * EDGE, TILE), BF16),
    ]


def main_kernel(
    dims, len_ref, aux_ref, small_ref, ids_ref, mask_ref, table_ref, tq_ref, bias_ref, scorer_ref, cot_ref,
    blocks_ref, grad_ref, part_ref,
    taps_s, onehot_s, hidden_s, q_s, probs_s, similar_s, cot_s, band_s, pooled_s, hgrad_s, matrix_s,
):
    rows, length, width, vocab = dims
    count = rows * (length // TILE)
    seg_list, real_list = row_masks(rows, length, len_ref, ids_ref, mask_ref, taps_s)
    fill_cotangent(rows, length // 2, width, cot_ref, cot_s)
    fill_onehot(count, vocab, taps_s, onehot_s)
    m = members_of(rows, length, seg_list, real_list)
    fill_q(count, tq_ref[...], small_ref[1:2, 0:1], onehot_s, q_s)
    scores = block_scores(rows, length, m, q_s)

    def late_hidden():
        fill_hidden(count, lambda: table_ref[...], bias_ref[...], onehot_s, hidden_s)

    def scale():
        return aux_ref[0, 0] / small_ref[0:1, 0:1]

    refs = (hidden_s, cot_s, band_s, pooled_s, hgrad_s, probs_s, similar_s, blocks_ref, part_ref, matrix_s, late_hidden)
    pool = middle(dims, m, scores, seg_list, real_list, scale, scorer_ref[...], refs, lambda r, t: None)
    pool()

    def grad_step(k, carry):
        symbols = pl.ds(pl.multiple_of(k * vocab, vocab), vocab)
        for c in range(width // TILE):
            cols = slice(c * TILE, (c + 1) * TILE)
            grad_ref[symbols, cols] = jnp.dot(
                onehot_s[symbols, :], hgrad_s[:, cols], preferred_element_type=F32
            )
        return carry

    lax.fori_loop(0, TAPS, grad_step, 0)


def main_call(lengths, aux, small, ids, mask, table, tq, bias, scorer, cot):
    rows, length = ids.shape
    width = cot.shape[2]
    vocab = table.shape[1] // TAPS
    dims = (rows, length, width, vocab)
    vmem = pl.BlockSpec(memory_space=pltpu.VMEM)
    smem = pl.BlockSpec(memory_space=pltpu.SMEM)
    half = length // 2
    return pl.pallas_call(
        functools.partial(main_kernel, dims),
        out_shape=(
            jax.ShapeDtypeStruct((rows, half, width), BF16),
            jax.ShapeDtypeStruct((TAPS * vocab, width), F32),
            jax.ShapeDtypeStruct((8, width), F32),
        ),
        in_specs=[smem, smem] + [vmem] * 8,
        out_specs=(vmem, vmem, vmem),
        scratch_shapes=local_scratch(rows, length, width, vocab),
        compiler_params=pltpu.CompilerParams(vmem_limit_bytes=60 * 1024 * 1024),
        name="latent",
    )(lengths, aux, small, ids, mask, table, tq, bias, scorer, cot)


MESH = pl.DeviceIdType.MESH
ALL = slice(None)


def split3(x):
    a = x.astype(BF16).astype(F32)
    b = (x - a).astype(BF16).astype(F32)
    return a, b, x - a - b


def remote(src, dst, send, recv, device):
    return pltpu.make_async_remote_copy(
        src_ref=src, dst_ref=dst, send_sem=send, recv_sem=recv, device_id=device, device_id_type=MESH
    )


def device_at(c, x, y, z):
    return (z * 2 + y, x * 2 + c)


class Gather:
    def __init__(self, buf, me, send, recv, chunks):
        self.buf, self.me, self.send, self.recv, self.chunks = buf, me, send, recv, chunks
        self.rows = buf.shape[4] // chunks
        self.copies = {}

    def part(self, c, x, y, z, chunk, half=None):
        if half is None:
            return self.buf.at[c, x, y, z, pl.ds(chunk * self.rows, self.rows)]
        return self.buf.at[c, x, y, z, pl.ds(chunk * self.rows + half * (self.rows // 2), self.rows // 2)]

    def go(self, chunk, n, ref, device):
        at = chunk * 11 + n
        copy = remote(ref, ref, self.send.at[at], self.recv.at[at], device)
        copy.start()
        self.copies[chunk, n] = copy

    def along_z(self, chunk):
        c, x, y, z = self.me
        for i in range(1, 4):
            self.go(chunk, i - 1, self.part(c, x, y, z, chunk), device_at(c, x, y, lax.rem(z + i, 4)))

    def across(self, chunk, step):
        c, x, y, z = self.me
        copies = self.copies
        core, over_x, over_y = device_at(1 - c, x, y, z), device_at(c, 1 - x, y, z), device_at(c, x, 1 - y, z)
        if step == 0:
            for n in range(3):
                copies[chunk, n].wait_recv()
            mine = self.part(c, x, y, ALL, chunk)
            self.go(chunk, 3, mine, over_x)
            self.go(chunk, 4, mine, over_y)
            self.go(chunk, 5, mine, core)
        elif step == 1:
            copies[chunk, 3].wait_recv()
            self.go(chunk, 6, self.part(c, 1 - x, y, ALL, chunk, 0), over_y)
            self.go(chunk, 7, self.part(c, 1 - x, y, ALL, chunk), core)
            copies[chunk, 4].wait_recv()
            self.go(chunk, 8, self.part(c, x, 1 - y, ALL, chunk, 1), over_x)
            self.go(chunk, 9, self.part(c, x, 1 - y, ALL, chunk), core)
        else:
            copies[chunk, 6].wait_recv()
            copies[chunk, 8].wait_recv()
            self.go(chunk, 10, self.part(c, 1 - x, 1 - y, ALL, chunk), core)

    def arrived(self, chunk):
        for n in (5, 7, 9, 10):
            self.copies[chunk, n].wait_recv()

    def drain(self):
        for copy in self.copies.values():
            copy.wait_send()


def place_of(slot, taps, per_tap):
    slot = jnp.minimum(slot, taps * per_tap - 1)
    tap = slot // per_tap
    return tap, slot - tap * per_tap


def static_place(tap, column, per_tap):
    slot = tap * per_tap + column
    return slot // 16, slot // 8 % 2, slot // 4 % 2, slot % 4


def step_kernel(
    dims,
    len_in, aux_in, ids_in, mask_in, emb_ref, conv_ref, bias_in, scorer_in, cot_ref,
    blocks_ref, final_ref, sums_out,
    taps_s, onehot_s, hidden_s, q_s, probs_s, similar_s, cot_s, band_s, pooled_s, hgrad_s, matrix_s,
    blocks_s, part_s, conv_s, emb_s,
    small_s, smalls_s, wcol_s, emball_s, tq_s, tqs_s, count_s, table_s,
    give_s, take_s, own_s, pass_s, came_s, zgive_s, zown_s, zcame_s, final_s, sums_s, sumr_s,
    local_sem, start_send, start_recv, half_sem, gather_send, gather_recv,
    core_send, core_recv, quad_send, quad_recv, line_send, line_recv, sum_send, sum_recv,
    len_ref, aux_ref, ids_ref, mask_ref, bias_ref, scorer_ref, sums_ref, in_sem,
):
    rows, length, width, vocab, size, fs = dims
    half = length // 2
    count = rows * (length // TILE)
    per_tap = width // 128
    f, d = lax.axis_index("fsdp"), lax.axis_index("dp")
    z, y = f // 2, lax.rem(f, 2)
    x, c = d // 2, lax.rem(d, 2)
    me = (c, x, y, z)
    core = device_at(1 - c, x, y, z)

    barrier = pltpu.get_barrier_semaphore()
    peers = [(lax.rem(f + i, fs), d) for i in range(1, fs)]
    others = [core, device_at(c, 1 - x, y, z), device_at(c, 1 - x, 1 - y, z)]
    for peer in peers + others:
        pl.semaphore_signal(barrier, inc=1, device_id=peer, device_id_type=MESH)

    inputs = [
        pltpu.make_async_copy(source, target, in_sem.at[n])
        for n, (source, target) in enumerate(
            [
                (len_in, len_ref),
                (ids_in, ids_ref),
                (mask_in, mask_ref),
                (bias_in, bias_ref),
                (scorer_in, scorer_ref),
                (aux_in, aux_ref),
            ]
        )
    ]
    for copy in inputs:
        copy.start()
    mid = vocab // 2
    my_half = pl.ds(pl.multiple_of(c * mid, mid), mid)
    my_rows = pl.ds(pl.multiple_of(x * (size // 2), size // 2), size // 2)
    my_tap, my_column = place_of(((c * 2 + x) * 2 + y) * 4 + z, TAPS, per_tap)
    local = [
        pltpu.make_async_copy(conv_ref, conv_s, local_sem.at[0]),
        pltpu.make_async_copy(emb_ref, emb_s, local_sem.at[1]),
        pltpu.make_async_copy(
            conv_ref.at[my_tap, :, pl.ds(pl.multiple_of(my_column * 128, 128), 128)], wcol_s.at[f], local_sem.at[2]
        ),
        pltpu.make_async_copy(emb_ref.at[my_rows, my_half], emball_s.at[f, my_rows, my_half], local_sem.at[3]),
    ]
    for r in range(rows):
        local.append(pltpu.make_async_copy(cot_ref.at[r], cot_s.at[r, pl.ds(EDGE, half)], local_sem.at[4 + r]))
    for copy in local:
        copy.start()
    for copy in inputs:
        copy.wait()
    real_here = jnp.sum(jnp.sum(mask_ref[...].astype(F32), axis=1, keepdims=True), axis=0, keepdims=True)
    small_s[...] = jnp.zeros_like(small_s)
    small_s[0:1, 0:size] = bias_ref[...].astype(F32)
    small_s[1:2, 0:size] = scorer_ref[...].astype(F32)
    small_s[2:3, :] = jnp.broadcast_to(real_here, (1, 128))
    smalls_s[f] = small_s[...]
    seg_list, real_list = row_masks(rows, length, len_ref, ids_ref, mask_ref, taps_s)

    pl.semaphore_wait(barrier, fs - 1 + 3)
    starts = []
    for i, peer in enumerate(peers):
        starts.append(remote(small_s, smalls_s.at[f], start_send.at[0, i], start_recv.at[0, i], peer))
        starts[-1].start()
    for i, peer in enumerate(peers):
        mine = emb_ref.at[my_rows, my_half]
        starts.append(
            remote(mine, emball_s.at[f, my_rows, my_half], start_send.at[1, i], start_recv.at[1, i], peer)
        )
        starts[-1].start()
    for i, peer in enumerate(peers):
        tap, column = place_of(((c * 2 + x) * 2 + lax.rem(peer[0], 2)) * 4 + peer[0] // 2, TAPS, per_tap)
        mine = conv_ref.at[tap, :, pl.ds(pl.multiple_of(column * 128, 128), 128)]
        starts.append(remote(mine, wcol_s.at[f], start_send.at[2, i], start_recv.at[2, i], peer))
        starts[-1].start()

    fill_onehot(count, vocab, taps_s, onehot_s)
    cot_s[:, 0:EDGE, :] = jnp.zeros((rows, EDGE, width), BF16)
    cot_s[:, EDGE + half :, :] = jnp.zeros((rows, EDGE, width), BF16)

    for i in range(fs - 1):
        starts[i].wait_recv()
    line = jnp.zeros((16, width), F32)
    real_sum = jnp.zeros((1, 1), F32)
    lane = lax.broadcasted_iota(jnp.int32, (128, width), 0)
    at = lax.broadcasted_iota(jnp.int32, (128, width), 1)
    for g in range(fs):
        pick = jnp.where((at == lane + g * size) & (lane < size), 1.0, 0.0).astype(BF16)
        both = jnp.concatenate([smalls_s[g], jnp.zeros((8, 128), F32)], axis=0)
        keep = lax.broadcasted_iota(jnp.int32, (16, 128), 0) < 2
        line = line + jnp.dot(jnp.where(keep, both, 0.0).astype(BF16), pick, preferred_element_type=F32)
        real_sum = real_sum + smalls_s[g][2:3, 0:1]
    count_s[0] = jnp.broadcast_to(real_sum, (8, 128))
    count_x = remote(
        count_s.at[0], count_s.at[1], half_sem.at[0], half_sem.at[1], device_at(c, 1 - x, y, z)
    )
    count_x.start()
    line16 = line.astype(BF16)
    bias_column = jnp.concatenate([line, jnp.zeros((112, width), F32)], axis=0).T[:, 0:1]
    const = jnp.sum(line[0:1] * line[1:2], axis=1, keepdims=True)
    scorer = line16[1:2]
    local[0].wait()
    local[1].wait()
    across = (((1,), (1,)), ((), ()))
    u = jnp.concatenate(
        [
            lax.dot_general(line16, conv_s[k], across, preferred_element_type=F32)[1:2]
            for k in range(TAPS)
        ],
        axis=0,
    )
    u = jnp.concatenate(list(split3(u)) + [jnp.zeros((1, size), F32)], axis=0).astype(BF16)
    tq = jnp.dot(u, emb_s[...], preferred_element_type=F32)
    tq_s[...] = jnp.zeros_like(tq_s)
    tq_s[0:TAPS, :] = tq[0:TAPS] + tq[TAPS : 2 * TAPS] + tq[2 * TAPS : 3 * TAPS]
    tqs_s[f] = tq_s[...]
    tq_copies = []
    for i, peer in enumerate(peers):
        copy = remote(tq_s, tqs_s.at[f], start_send.at[3, i], start_recv.at[3, i], peer)
        copy.start()
        tq_copies.append(copy)

    for copy in local[2:4]:
        copy.wait()
    for i in range(fs - 1):
        starts[fs - 1 + i].wait_recv()
    mine = emball_s.at[:, my_rows, my_half]
    emb_x = remote(mine, mine, half_sem.at[6], half_sem.at[7], device_at(c, 1 - x, y, z))
    emb_x.start()
    emb_x.wait_recv()
    mine = emball_s.at[:, :, my_half]
    emb_core = remote(mine, mine, half_sem.at[2], half_sem.at[3], core)
    emb_core.start()
    for i in range(fs - 1):
        starts[2 * (fs - 1) + i].wait_recv()
    emb_core.wait_recv()
    block = lax.dot_general(
        wcol_s[...].reshape(fs * size, 128),
        emball_s[...].reshape(fs * size, vocab),
        (((0,), (0,)), ((), ())),
        preferred_element_type=F32,
    )
    table_s[c, x, y, z] = block.astype(BF16)
    tables = Gather(table_s, me, gather_send.at[0], gather_recv.at[0], TABLE_CHUNKS)
    for chunk in range(TABLE_CHUNKS):
        tables.along_z(chunk)

    count_x.wait_recv()
    count_s[2] = count_s[0] + count_s[1]
    count_c = remote(count_s.at[2], count_s.at[3], half_sem.at[4], half_sem.at[5], core)
    count_c.start()

    m = members_of(rows, length, seg_list, real_list)
    for copy in tq_copies:
        copy.wait_recv()
    tq = tqs_s[0]
    for g in range(1, fs):
        tq = tq + tqs_s[g]
    tq16 = jnp.concatenate(
        [
            jnp.concatenate(list(split3(tq[k : k + 1])) + [jnp.zeros((13, vocab), F32)], axis=0)
            for k in range(TAPS)
        ],
        axis=1,
    ).astype(BF16)
    fill_q(count, tq16, const, onehot_s, q_s)
    scores = block_scores(rows, length, m, q_s)

    part = 128 // TABLE_CHUNKS

    def table_rows(chunk):
        return jnp.concatenate(
            [
                jnp.concatenate(
                    [
                        table_s[(*static_place(k, j, per_tap), slice(chunk * part, (chunk + 1) * part))]
                        for j in range(per_tap)
                    ],
                    axis=0,
                )
                for k in range(TAPS)
            ],
            axis=1,
        )

    def hidden_part(chunk, low, high):
        if low == 0 and chunk < TABLE_CHUNKS - 1:
            tables.arrived(chunk)
        bias_part = jnp.concatenate(
            [bias_column[j * 128 + chunk * part : j * 128 + (chunk + 1) * part] for j in range(per_tap)], axis=0
        )

        def step(t, carry):
            lanes = pl.ds(pl.multiple_of(t * TILE, TILE), TILE)
            got = jnp.dot(table_rows(chunk), onehot_s[:, lanes], preferred_element_type=F32)
            got = (got + bias_part).astype(BF16)
            for j in range(per_tap):
                hidden_s[j * 128 + chunk * part : j * 128 + (chunk + 1) * part, lanes] = got[
                    j * part : (j + 1) * part
                ]
            return carry

        for t in range(count * low // 4, count * high // 4):
            step(t, 0)

    order = [(0, 0), (1, 0), (0, 1), (1, 1), (0, 2), (0, 0, 2), (1, 2), (0, 2, 4), (1, 0, 4)]
    steps = [
        functools.partial(tables.across if len(n) == 2 else hidden_part, *n) for n in order
    ]
    turns = {(0, 1): 1, (0, 3): 1, (1, 1): 1, (1, 3): 1}

    def between(r, t):
        for _ in range(turns.get((r, t), 0)):
            steps.pop(0)()

    def late_hidden():
        while len(steps) > 1:
            steps.pop(0)()
        tables.arrived(TABLE_CHUNKS - 1)
        tables.drain()
        for copy in local[4:]:
            copy.wait()
        count_c.wait_recv()
        steps.pop(0)()

    def scale():
        return aux_ref[0, 0] / (count_s[2][0:1, 0:1] + count_s[3][0:1, 0:1])

    refs = (hidden_s, cot_s, band_s, pooled_s, hgrad_s, probs_s, similar_s, blocks_s, part_s, matrix_s, late_hidden)
    pool = middle(dims[:4], m, scores, seg_list, real_list, scale, scorer, refs, between)
    def product(slot):
        tap, column = place_of(jnp.minimum(slot, TAPS * per_tap - 2), TAPS, per_tap)
        symbols = pl.ds(pl.multiple_of(tap * vocab, vocab), vocab)
        lanes = pl.ds(pl.multiple_of(column * 128, 256), 256)
        return jnp.dot(onehot_s[symbols, :], hgrad_s[:, lanes], preferred_element_type=F32)

    def core_copy(p):
        return remote(give_s.at[p], take_s.at[p], core_send.at[p], core_recv.at[p], core)

    def quad_of(t):
        q = 3 - t // 2
        qx, qy = lax.rem(x + q // 2, 2), lax.rem(y + lax.rem(q, 2), 2)
        return qx, qy, qx * 4 + qy * 2 + lax.rem(t, 2)

    def give(t):
        p = quad_of(t)[2]
        give_s[p] = product((1 - c) * 16 + 2 * p)
        core_copy(p).start()

    def keep(t):
        p = quad_of(t)[2]
        got = product(c * 16 + 2 * p)
        core_copy(p).wait_recv()
        return got + take_s[p]

    gap = vocab // GRAD_CHUNKS

    def quad_copy(t, chunk):
        qx, qy, _ = quad_of(t)
        at = chunk * 6 + t
        ref = t, pl.ds(chunk * gap, gap)
        return remote(pass_s.at[ref], came_s.at[ref], quad_send.at[at], quad_recv.at[at], device_at(c, qx, qy, z))

    def pass_on(t):
        pass_s[t] = keep(t).astype(BF16)
        for chunk in range(GRAD_CHUNKS):
            quad_copy(t, chunk).start()

    def forward(t, carry):
        pass_on(t)
        give(t + 2)
        return carry

    give(jnp.int32(0))
    give(jnp.int32(1))
    lax.fori_loop(0, 6, forward, 0)
    own_s[0] = keep(jnp.int32(6))
    own_s[1] = keep(jnp.int32(7))

    pool()
    blocks_out = pltpu.make_async_copy(blocks_s, blocks_ref, local_sem.at[0])
    blocks_out.start()
    sums_s[0] = part_s[...]
    sum_copies = [remote(sums_s.at[0], sumr_s.at[0], sum_send.at[0], sum_recv.at[0], core)]
    sum_copies[0].start()

    def sums_quad():
        sum_copies[0].wait_recv()
        sums_s[1] = sums_s[0] + sumr_s[0]
        quad = [device_at(c, lax.rem(x + q // 2, 2), lax.rem(y + q % 2, 2), z) for q in range(4)]
        for q in range(1, 4):
            sum_copies.append(remote(sums_s.at[1], sumr_s.at[q], sum_send.at[q], sum_recv.at[q], quad[q]))
            sum_copies[-1].start()

    def sums_line():
        for q in range(1, 4):
            sum_copies[q].wait_recv()
        sums_s[2] = (sums_s[1] + sumr_s[1]) + (sumr_s[2] + sumr_s[3])
        for i in range(1, 4):
            to = device_at(c, x, y, lax.rem(z + i, 4))
            sum_copies.append(remote(sums_s.at[2], sumr_s.at[3 + i], sum_send.at[3 + i], sum_recv.at[3 + i], to))
            sum_copies[-1].start()

    grads = Gather(final_s, me, gather_send.at[1], gather_recv.at[1], GRAD_CHUNKS)
    line_copies = {}

    def to_line(chunk):
        part = slice(chunk * gap, (chunk + 1) * gap)
        for t in range(6):
            quad_copy(jnp.int32(t), chunk).wait_recv()
        for t in range(2):
            total = own_s[t, part]
            for q in range(1, 4):
                total = total + came_s[6 - 2 * q + t, part].astype(F32)
            for j in range(2):
                zown_s[2 * t + j, part] = total[:, j * 128 : (j + 1) * 128]
                zgive_s[2 * t + j, part] = total[:, j * 128 : (j + 1) * 128].astype(BF16)
        for i in range(1, 4):
            to = lax.rem(z + i, 4)
            at = chunk * 3 + i - 1
            part = pl.ds(chunk * gap, gap)
            copy = remote(
                zgive_s.at[to, part],
                zcame_s.at[i - 1, part],
                line_send.at[at],
                line_recv.at[at],
                device_at(c, x, y, to),
            )
            copy.start()
            line_copies[chunk, i] = copy

    def from_line(chunk):
        part = slice(chunk * gap, (chunk + 1) * gap)
        total = zown_s[z, part]
        for i in range(1, 4):
            line_copies[chunk, i].wait_recv()
            total = total + zcame_s[i - 1, part].astype(F32)
        final_s[c, x, y, z, part] = total.astype(BF16)
        grads.along_z(chunk)

    def put(chunk):
        part = pl.ds(chunk * gap, gap)
        ref = ALL, ALL, ALL, ALL, part
        out_copies.append(pltpu.make_async_copy(final_s.at[ref], final_ref.at[ref], local_sem.at[1 + chunk]))
        out_copies[-1].start()

    out_copies = []
    to_line(0)
    to_line(1)
    from_line(0)
    from_line(1)
    sums_quad()
    grads.across(0, 0)
    sums_line()
    grads.across(1, 0)
    grads.across(0, 1)
    grads.across(1, 1)
    grads.across(0, 2)
    grads.across(1, 2)
    grads.arrived(0)
    put(0)
    grads.arrived(1)
    put(1)
    grads.drain()

    for i in range(4, 7):
        sum_copies[i].wait_recv()
    sums = (sums_s[2] + sumr_s[4]) + (sumr_s[5] + sumr_s[6])
    total_count = count_s[2][0:1, 0:1] + count_s[3][0:1, 0:1]
    sums_ref[...] = jnp.concatenate([sums[0:1], sums[1:2] / total_count, sums[2:8]], axis=0)
    out_copies.append(pltpu.make_async_copy(sums_ref, sums_out, in_sem.at[0]))
    out_copies[-1].start()

    for copy in starts + tq_copies + sum_copies + list(line_copies.values()) + [count_x, count_c, emb_x, emb_core]:
        copy.wait_send()
    for p in range(8):
        core_copy(p).wait_send()
    for chunk in range(GRAD_CHUNKS):
        for t in range(6):
            quad_copy(jnp.int32(t), chunk).wait_send()
    for copy in out_copies + [blocks_out]:
        copy.wait()


def last_kernel(
    dims, blocks_ref, final_ref, sums_in, emb_ref, conv_ref,
    out_ref, loss_out, embg_out, convg_ref, biasg_out, scoreg_out,
    blocks_s, final_s, emb_s, conv_s, convg_s, in_sem, out_sem,
    sums_ref, loss_ref, embg_ref, biasg_ref, scoreg_ref,
):
    rows, length, width, vocab, size, fs = dims
    per_tap = width // 128
    copies = [
        pltpu.make_async_copy(emb_ref, emb_s, in_sem.at[0]),
        pltpu.make_async_copy(conv_ref, conv_s, in_sem.at[1]),
    ]
    for n in range(4):
        copies.append(
            pltpu.make_async_copy(final_ref.at[n // 2, n % 2], final_s.at[n // 2, n % 2], in_sem.at[2 + n])
        )
    blocks = [pltpu.make_async_copy(blocks_ref.at[r], blocks_s.at[r], in_sem.at[6 + r]) for r in range(rows)]
    copies.append(pltpu.make_async_copy(sums_in, sums_ref, in_sem.at[6 + rows]))
    for copy in copies + blocks:
        copy.start()
    outs = []
    have = 0
    copies[0].wait()
    copies[1].wait()
    emb_total = None
    for k in range(TAPS):
        while have * 8 < (k + 1) * per_tap:
            copies[2 + have].wait()
            have += 1
        grad = jnp.concatenate([final_s[static_place(k, j, per_tap)] for j in range(per_tap)], axis=1)
        convg_s[k] = jnp.dot(emb_s[...], grad, preferred_element_type=F32)
        outs.append(pltpu.make_async_copy(convg_s.at[k], convg_ref.at[k], out_sem.at[k]))
        outs[-1].start()
        term = lax.dot_general(conv_s[k], grad, (((1,), (1,)), ((), ())), preferred_element_type=F32)
        emb_total = term if emb_total is None else emb_total + term
        if k == TAPS // 2:
            bias_line = jnp.sum(grad.astype(F32), axis=0, keepdims=True)
        if k < rows:
            blocks[k].wait()
            outs.append(pltpu.make_async_copy(blocks_s.at[k], out_ref.at[k], out_sem.at[TAPS + k]))
            outs[-1].start()
    embg_ref[...] = emb_total
    copies[6].wait()
    f = lax.axis_index("fsdp")
    lane = lax.broadcasted_iota(jnp.int32, (128, width), 0)
    at = lax.broadcasted_iota(jnp.int32, (128, width), 1)
    pick = jnp.where((at == lane + f * size) & (lane < size), 1.0, 0.0).astype(BF16)
    lines = jnp.concatenate(
        list(split3(bias_line)) + list(split3(sums_ref[0:1])) + [jnp.zeros((10, width), F32)], axis=0
    ).astype(BF16)
    mine = lax.dot_general(lines, pick, (((1,), (1,)), ((), ())), preferred_element_type=F32)
    biasg_ref[...] = (mine[0:1] + mine[1:2] + mine[2:3])[:, :size]
    scoreg_ref[...] = (mine[3:4] + mine[4:5] + mine[5:6])[:, :size]
    loss_ref[...] = sums_ref[1:2, 0:1]
    for n, (source, target) in enumerate(
        [(embg_ref, embg_out), (biasg_ref, biasg_out), (scoreg_ref, scoreg_out), (loss_ref, loss_out)]
    ):
        outs.append(pltpu.make_async_copy(source, target, out_sem.at[TAPS + rows + n]))
        outs[-1].start()
    while have < 4:
        copies[2 + have].wait()
        have += 1
    for copy in outs:
        copy.wait()


def step_shards(byte_ids, doc_lengths, pad_mask, embedding, conv_weight, conv_bias, scorer, cotangent, aux_weight):
    rows, length = byte_ids.shape
    vocab, size = embedding.shape
    width = conv_weight.shape[2]
    half = length // 2
    fs = width // size
    dims = (rows, length, width, vocab, size, fs)
    hbm = pl.BlockSpec(memory_space=pl.ANY)
    dma = pltpu.SemaphoreType.DMA
    blocks, final, sums = pl.pallas_call(
        functools.partial(step_kernel, dims),
        out_shape=(
            jax.ShapeDtypeStruct((rows, half, width), BF16),
            jax.ShapeDtypeStruct((2, 2, 2, 4, vocab, 128), BF16),
            jax.ShapeDtypeStruct((8, width), F32),
        ),
        in_specs=[hbm] * 9,
        out_specs=(hbm, hbm, hbm),
        scratch_shapes=local_scratch(rows, length, width, vocab)
        + [
            pltpu.VMEM((rows, half, width), BF16),
            pltpu.VMEM((8, width), F32),
            pltpu.VMEM((TAPS, size, width), BF16),
            pltpu.VMEM((size, vocab), BF16),
            pltpu.VMEM((8, 128), F32),
            pltpu.VMEM((fs, 8, 128), F32),
            pltpu.VMEM((fs, size, 128), BF16),
            pltpu.VMEM((fs, size, vocab), BF16),
            pltpu.VMEM((8, vocab), F32),
            pltpu.VMEM((fs, 8, vocab), F32),
            pltpu.VMEM((4, 8, 128), F32),
            pltpu.VMEM((2, 2, 2, 4, 128, vocab), BF16),
            pltpu.VMEM((8, vocab, 256), F32),
            pltpu.VMEM((8, vocab, 256), F32),
            pltpu.VMEM((2, vocab, 256), F32),
            pltpu.VMEM((6, vocab, 256), BF16),
            pltpu.VMEM((6, vocab, 256), BF16),
            pltpu.VMEM((4, vocab, 128), BF16),
            pltpu.VMEM((4, vocab, 128), F32),
            pltpu.VMEM((3, vocab, 128), BF16),
            pltpu.VMEM((2, 2, 2, 4, vocab, 128), BF16),
            pltpu.VMEM((3, 8, width), F32),
            pltpu.VMEM((7, 8, width), F32),
            dma((4 + max(rows, 2),)),
            dma((4, fs - 1)),
            dma((4, fs - 1)),
            dma((8,)),
            dma((2, 11 * max(TABLE_CHUNKS, GRAD_CHUNKS))),
            dma((2, 11 * max(TABLE_CHUNKS, GRAD_CHUNKS))),
            dma((8,)),
            dma((8,)),
            dma((6 * GRAD_CHUNKS,)),
            dma((6 * GRAD_CHUNKS,)),
            dma((3 * GRAD_CHUNKS,)),
            dma((3 * GRAD_CHUNKS,)),
            dma((7,)),
            dma((7,)),
            pltpu.SMEM(doc_lengths.shape, jnp.int32),
            pltpu.SMEM((1, 1), F32),
            pltpu.VMEM((rows, length), jnp.int32),
            pltpu.VMEM((rows, length), jnp.int32),
            pltpu.VMEM((1, size), BF16),
            pltpu.VMEM((1, size), BF16),
            pltpu.VMEM((8, width), F32),
            dma((6,)),
        ],
        compiler_params=pltpu.CompilerParams(
            collective_id=0, has_side_effects=True, vmem_limit_bytes=62 * 1024 * 1024
        ),
        name="step",
    )(
        doc_lengths,
        aux_weight.reshape(1, 1),
        byte_ids,
        pad_mask,
        embedding.T,
        conv_weight,
        conv_bias.reshape(1, size),
        scorer.reshape(1, size),
        cotangent,
    )
    blocks, loss, emb_grad, conv_grad, bias_grad, score_grad = pl.pallas_call(
        functools.partial(last_kernel, dims),
        out_shape=(
            jax.ShapeDtypeStruct((rows, half, width), BF16),
            jax.ShapeDtypeStruct((1, 1), F32),
            jax.ShapeDtypeStruct((size, vocab), F32),
            jax.ShapeDtypeStruct((TAPS, size, width), F32),
            jax.ShapeDtypeStruct((1, size), F32),
            jax.ShapeDtypeStruct((1, size), F32),
        ),
        in_specs=[hbm] * 5,
        out_specs=(hbm,) * 6,
        scratch_shapes=[
            pltpu.VMEM((rows, half, width), BF16),
            pltpu.VMEM((2, 2, 2, 4, vocab, 128), BF16),
            pltpu.VMEM((size, vocab), BF16),
            pltpu.VMEM((TAPS, size, width), BF16),
            pltpu.VMEM((TAPS, size, width), F32),
            dma((7 + rows,)),
            dma((rows + TAPS + 4,)),
            pltpu.VMEM((8, width), F32),
            pltpu.VMEM((1, 1), F32),
            pltpu.VMEM((size, vocab), F32),
            pltpu.VMEM((1, size), F32),
            pltpu.VMEM((1, size), F32),
        ],
        compiler_params=pltpu.CompilerParams(vmem_limit_bytes=62 * 1024 * 1024),
        name="last",
    )(blocks, final, sums, embedding.T, conv_weight)
    return blocks, loss.reshape(()), emb_grad.T, conv_grad, bias_grad.reshape(size), score_grad.reshape(size)


def split3_rows(x):
    a = lax.reduce_precision(x, 8, 7)
    b = lax.reduce_precision(x - a, 8, 7)
    return jnp.concatenate([a, b, x - a - b], axis=0).astype(BF16)


def gathered_shards(byte_ids, doc_lengths, pad_mask, embedding, conv_weight, conv_bias, scorer, cotangent, aux_weight):
    emb = lax.all_gather(embedding, "fsdp", axis=1, tiled=True)
    conv = lax.all_gather(conv_weight, "fsdp", axis=1, tiled=True)
    bias = lax.all_gather(conv_bias, "fsdp", axis=0, tiled=True)
    score = lax.all_gather(scorer, "fsdp", axis=0, tiled=True)
    vocab, width = emb.shape
    count = lax.psum(jnp.sum(pad_mask.astype(F32)), ("fsdp", "dp"))
    table = jnp.einsum("kcd,vc->dkv", conv, emb, preferred_element_type=F32).reshape(width, TAPS * vocab)
    score32 = score.astype(F32)
    q_table = jnp.sum(table * score32[:, None], axis=0, keepdims=True)
    tq = jnp.concatenate([split3_rows(q_table), jnp.zeros((13, TAPS * vocab), BF16)], axis=0)
    bias32 = bias.astype(F32)
    small = jnp.stack([jnp.full((128,), count), jnp.full((128,), jnp.sum(bias32 * score32))])
    small = jnp.concatenate([small, jnp.zeros((6, 128), F32)], axis=0)
    blocks, grad, part = main_call(
        doc_lengths, aux_weight.reshape(1, 1), small, byte_ids, pad_mask, table.astype(BF16), tq, bias32[:, None], score[None, :], cotangent
    )
    grad = lax.psum(grad, ("fsdp", "dp")).reshape(TAPS, vocab, width)
    score_grad = lax.psum(part[0], ("fsdp", "dp"))
    loss = lax.psum(part[1, 0], ("fsdp", "dp")) / count
    size = embedding.shape[1]
    at = lax.axis_index("fsdp") * size
    bias_grad = lax.dynamic_slice_in_dim(jnp.sum(grad[TAPS // 2], axis=0), at, size, 0)
    score_grad = lax.dynamic_slice_in_dim(score_grad, at, size, 0)
    conv_grad = jnp.einsum("vc,kvd->kcd", embedding.astype(F32), grad, precision=lax.Precision.HIGHEST)
    emb_grad = jnp.einsum("kvd,kcd->vc", grad, conv_weight.astype(F32), precision=lax.Precision.HIGHEST)
    return blocks, loss, emb_grad, conv_grad, bias_grad, score_grad


def solution(mesh):
    small = mesh.shape["fsdp"] == 8 and mesh.shape["dp"] == 4
    return jax.shard_map(
        step_shards if small else gathered_shards,
        mesh=mesh,
        in_specs=(
            P(("fsdp", "dp"), None),
            P(("fsdp", "dp"), None),
            P(("fsdp", "dp"), None),
            P(None, "fsdp"),
            P(None, "fsdp", None),
            P("fsdp"),
            P("fsdp"),
            P(("fsdp", "dp"), None, None),
            P(),
        ),
        out_specs=(
            P(("fsdp", "dp"), None, None),
            P(),
            P(None, "fsdp"),
            P(None, "fsdp", None),
            P("fsdp"),
            P("fsdp"),
        ),
        check_vma=False,
    )
```

```python
import functools
import jax
import jax.numpy as jnp
from jax import lax
from jax.experimental import pallas as pl
from jax.experimental.pallas import tpu as pltpu
from jax.sharding import PartitionSpec as P

TAPS = 5
SIZES = 4
NEG = -1000000000.0
F32 = jnp.float32
BF16 = jnp.bfloat16
TILE = 256
EDGE = 16
TABLE_CHUNKS = 2
GRAD_CHUNKS = 2


def split2(x):
    high = x.astype(BF16).astype(F32)
    return high, x - high


def shift(x, offset):
    length = x.shape[1]
    return x if offset == 0 else pltpu.roll(x, (-offset) % length, 1)


def group_pair(x, step, lane_bit):
    size = x.shape[0]
    down = pltpu.roll(x, (size - step) % size, 0)
    up = pltpu.roll(x, step, 0)
    return jnp.where(lane_bit, up, down)


def group_all(x, op, bits):
    x = op(x, group_pair(x, 1, bits[0]))
    return op(x, group_pair(x, 2, bits[1]))


def spread(rows_list, length):
    return jnp.concatenate([jnp.broadcast_to(x, (SIZES, length)) for x in rows_list], axis=0)


def lane_rows(ref, at, r, length):
    return ref[at : at + 1, r * length : (r + 1) * length]


DELTA_EVEN = {-3: -2, -2: -1, -1: -1, 0: 0, 1: 0, 2: 1, 3: 1}
DELTA_ODD = {-3: -1, -2: -1, -1: 0, 0: 0, 1: 1, 2: 1, 3: 2}
OFFSETS = [o for o in range(1 - SIZES, SIZES) if o != 0]


def row_masks(rows, length, len_ref, ids_ref, mask_ref, taps_s):
    place1 = lax.broadcasted_iota(jnp.int32, (1, length), 1)
    seg_list, real_list = [], []
    for r in range(rows):
        end = len_ref[r, 0]
        segment = jnp.where(place1 >= end, 1.0, 0.0)
        for d in range(1, len_ref.shape[1]):
            end = end + len_ref[r, d]
            segment = segment + jnp.where(place1 >= end, 1.0, 0.0)
        seg_list.append(segment)
        real_list.append(mask_ref[r : r + 1, :].astype(F32))
        ids = ids_ref[r : r + 1, :].astype(F32)
        known = jnp.where(real_list[r] > 0.5, ids, -1.0)
        for k in range(TAPS):
            o = k - TAPS // 2
            inside = (place1 + o >= 0) & (place1 + o < length)
            keep = inside & (shift(segment, o) == segment)
            taps_s[k : k + 1, r * length : (r + 1) * length] = jnp.where(
                keep, shift(known, o), -1.0
            ).astype(jnp.int32)
    return seg_list, real_list


def fill_onehot(count, vocab, taps_s, onehot_s):
    symbol = lax.broadcasted_iota(jnp.int32, (vocab, TILE), 0)

    def step(t, carry):
        lanes = pl.ds(pl.multiple_of(t * TILE, TILE), TILE)
        for k in range(TAPS):
            here = taps_s[k : k + 1, lanes]
            onehot_s[k * vocab : (k + 1) * vocab, lanes] = jnp.where(symbol == here, 1.0, 0.0).astype(BF16)
        return carry

    lax.fori_loop(0, count, step, 0)


def members_of(rows, length, seg_list, real_list):
    shape = (rows * SIZES, length)
    place = lax.broadcasted_iota(jnp.int32, shape, 1)
    sub = lax.broadcasted_iota(jnp.int32, shape, 0)
    size = (sub & (SIZES - 1)) + 1
    third = jnp.floor((place.astype(F32) + 0.5) * (1.0 / 3.0)).astype(jnp.int32)
    within = jnp.where(
        size == 1, 0, jnp.where(size == 2, place & 1, jnp.where(size == 3, place - 3 * third, place & 3))
    )
    seg = spread(seg_list, length)
    real = spread(real_list, length)
    same = {}
    for o in range(1, SIZES):
        ahead = (within + o < size) & (place + o < length) & (shift(seg, o) == seg)
        behind = (within - o >= 0) & (shift(seg, -o) == seg)
        same[o] = jnp.where(ahead, 1.0, 0.0)
        same[-o] = jnp.where(behind, 1.0, 0.0)
    member = {o: same[o] * shift(real, o) for o in OFFSETS}
    members = real
    for o in OFFSETS:
        members = members + member[o]
    even = (place & 1) == 0
    pair = jnp.where(even | (shift(seg, -1) == seg), real, 0.0)
    partner = jnp.where(even, shift(pair, 1), shift(pair, -1))
    return dict(
        bits=((sub & 1) == 1, (sub & 2) == 2),
        first=size == 1,
        even=even,
        real=real,
        same=same,
        member=member,
        inverse=1.0 / jnp.maximum(members, 1.0),
        pair_weight=pair / jnp.maximum(pair + partner, 1.0),
    )


def block_scores(rows, length, m, q_s):
    q = spread([lane_rows(q_s, 0, r, length) for r in range(rows)], length)
    total = q * m["real"]
    for o in OFFSETS:
        total = total + m["member"][o] * shift(q, o)
    return total * m["inverse"]


def near_keys(t, length):
    return [
        j
        for j in range(length // 128)
        if max(j * 128 - (t * TILE + TILE - 1), t * TILE - (j * 128 + 127)) < length // 2
    ]


def calibrate_row(r, length, scores, seg, real, similar_s, probs_s, between):
    s = scores[r * SIZES : (r + 1) * SIZES]
    a, rest = split2(s)
    b, c = split2(rest)
    key_seg = jnp.where(real > 0.5, seg, -1.0)
    zero = jnp.zeros((128 - 6 * SIZES - 1, length), F32)
    left = jnp.concatenate([a, a, b, b, a, c, key_seg, zero], axis=0).T
    right = jnp.concatenate([a, b, a, b, c, a, jnp.zeros_like(key_seg), zero], axis=0).astype(BF16)
    key_column = left[:, 6 * SIZES : 6 * SIZES + 1]
    left = left.astype(BF16)
    x = jnp.concatenate(
        [jnp.ones((1, length), F32), s, s[0:1] * s, s[1:2] * s[1:], s[2:3] * s[2:], s[3:4] * s[3:]]
        + [jnp.zeros((1, length), F32)],
        axis=0,
    )
    x_high, x_low = split2(x)
    features = jnp.concatenate([x_high, x_low], axis=0).astype(BF16)
    outs = []
    for t in range(length // TILE):
        lanes = slice(t * TILE, (t + 1) * TILE)
        query_seg = seg[:, lanes]
        top = None
        near = near_keys(t, length)
        for j in near:
            keys = slice(j * 128, (j + 1) * 128)
            sim = jnp.dot(left[keys], right[:, lanes], preferred_element_type=F32)
            allowed = key_column[keys] == query_seg
            if j * 128 // TILE == t:
                key_place = lax.broadcasted_iota(jnp.int32, (128, TILE), 0) + j * 128
                query_place = lax.broadcasted_iota(jnp.int32, (128, TILE), 1) + t * TILE
                allowed = allowed | (key_place == query_place)
            sim = jnp.where(allowed, sim, NEG)
            similar_s[keys, :] = sim
            here = jnp.max(sim, axis=0, keepdims=True)
            top = here if top is None else jnp.maximum(top, here)
        for j in near:
            keys = slice(j * 128, (j + 1) * 128)
            probs_s[r, keys, lanes] = jnp.exp(similar_s[keys, :] - top).astype(BF16)
        keys = slice(near[0] * 128, (near[-1] + 1) * 128)
        outs.append(jnp.dot(features[:, keys], probs_s[r, keys, lanes], preferred_element_type=F32))
        between(r, t)
    moments = jnp.concatenate(outs, axis=1)
    moments = moments[0:16] + moments[16:32]
    norm = 1.0 / moments[0:1]
    return moments * norm, norm


def size_softmax(cal, bits):
    top = group_all(cal, jnp.maximum, bits)
    log_weight = (cal - top) - jnp.log(group_all(jnp.exp(cal - top), jnp.add, bits))
    weight = jnp.exp(log_weight)
    entropy = -group_all(weight * log_weight, jnp.add, bits)
    return weight, log_weight, entropy


def band_products(rows, length, cot_s, hidden_s, band_s, window, diagonal):
    for r in range(rows):
        for t in range(length // TILE):
            lanes = slice(r * length + t * TILE, r * length + (t + 1) * TILE)
            first = t * TILE // 2
            prod = jnp.dot(
                cot_s[r, first : first + window, :], hidden_s[:, lanes], preferred_element_type=F32
            )
            for d in range(-2, 3):
                band_s[d + 2 : d + 3, lanes] = jnp.sum(jnp.where(diagonal == d, prod, 0.0), axis=0, keepdims=True)


def calibrate_back(r, length, scores, cal_grad, inner, moments, norm, probs_s):
    part = slice(r * SIZES, (r + 1) * SIZES)
    s, g, ri = scores[part], cal_grad[part], inner[r * SIZES : r * SIZES + 1]
    at = {}
    n = 1 + SIZES
    for a in range(SIZES):
        for b in range(a, SIZES):
            at[a, b] = at[b, a] = n
            n += 1
    query = []
    for a in range(SIZES):
        total = -moments[1 + a : 2 + a] * ri
        for b in range(SIZES):
            total = total + moments[at[a, b] : at[a, b] + 1] * g[b : b + 1]
        query.append(total)
    y = jnp.concatenate([g - s * ri] + [s[a : a + 1] * g for a in range(SIZES)], axis=0) * norm
    y = jnp.concatenate([y, jnp.zeros((4, length), F32)], axis=0)
    y_high, y_low = split2(y)
    features = jnp.concatenate([y_high, y_low], axis=0).astype(BF16)
    outs = []
    for t in range(length // TILE):
        keys = slice(t * TILE, (t + 1) * TILE)
        outs.append(
            lax.dot_general(
                features[:, max(t - 2, 0) * TILE : (t + 3) * TILE],
                probs_s[r, keys, max(t - 2, 0) * TILE : min(t + 3, length // TILE) * TILE],
                (((1,), (1,)), ((), ())),
                preferred_element_type=F32,
            )
        )
    back = jnp.concatenate(outs, axis=1)
    back = back[0:24] + back[24:48]
    key = []
    for a in range(SIZES):
        total = back[a : a + 1]
        for b in range(SIZES):
            n = SIZES + a * SIZES + b
            total = total + s[b : b + 1] * back[n : n + 1]
        key.append(total + query[a])
    return jnp.concatenate(key, axis=0)


def middle(dims, m, scores, seg_list, real_list, scale, scorer, refs, between):
    rows, length, width, vocab = dims
    half = length // 2
    tiles = length // TILE
    window = TILE // 2 + 2 * EDGE
    hidden_s, cot_s, band_s, pooled_s, hgrad_s, probs_s, similar_s, blocks_ref, part_ref, matrix_s, late_hidden = refs
    bits, real, same, member, inverse, pair_weight = (
        m[n] for n in ("bits", "real", "same", "member", "inverse", "pair_weight")
    )
    kept = [
        calibrate_row(r, length, scores, seg_list[r], real_list[r], similar_s, probs_s, between) for r in range(rows)
    ]
    cal = jnp.concatenate([moments[1 : 1 + SIZES] for moments, norm in kept], axis=0)
    weight, log_weight, entropy = size_softmax(cal, bits)
    entropy_sum = jnp.sum(
        jnp.sum(jnp.where(m["first"], entropy * real, 0.0), axis=1, keepdims=True), axis=0, keepdims=True
    )
    part_ref[...] = jnp.zeros_like(part_ref)
    part_ref[1:2, :] = jnp.broadcast_to(entropy_sum, (1, width))
    for r in range(rows):
        pooled_s[r] = jnp.zeros_like(pooled_s[r])

    use = pair_weight * weight * inverse
    moved = {o: (use if o == 0 else same[o] * shift(use, o)) for o in range(1 - SIZES, SIZES)}
    mix = []
    for d in range(-2, 3):
        odd_sum = sum([moved[o] for o in moved if DELTA_ODD[o] == d], jnp.zeros_like(use))
        even_sum = sum([moved[o] for o in moved if DELTA_EVEN[o] == d], jnp.zeros_like(use))
        mix.append(group_all(jnp.where(m["even"], even_sum, odd_sum) * real, jnp.add, bits))

    kl = lax.broadcasted_iota(jnp.int32, (window, TILE), 0)
    diagonal = kl - (lax.broadcasted_iota(jnp.int32, (window, TILE), 1) // 2 + EDGE)
    for r in range(rows):
        at = r * SIZES
        for t in range(tiles):
            lanes = slice(t * TILE, (t + 1) * TILE)
            matrix = jnp.zeros((window, TILE), F32)
            for d in range(-2, 3):
                matrix = jnp.where(diagonal == d, mix[d + 2][at : at + 1, lanes], matrix)
            high, low = split2(matrix)
            matrix_s[r * tiles + t, 0:window] = high.astype(BF16)
            matrix_s[r * tiles + t, window : 2 * window] = low.astype(BF16)

    late_hidden()
    band_products(rows, length, cot_s, hidden_s, band_s, window, diagonal)
    even1 = (lax.broadcasted_iota(jnp.int32, (1, length), 1) & 1) == 0
    band = [[lane_rows(band_s, d + 2, r, length) for d in range(-2, 3)] for r in range(rows)]

    def product(o):
        return spread(
            [jnp.where(even1, band[r][DELTA_EVEN[o] + 2], band[r][DELTA_ODD[o] + 2]) for r in range(rows)], length
        )

    gathered = real * product(0)
    for o in OFFSETS:
        gathered = gathered + member[o] * shift(product(-o), o)
    weight_grad = pair_weight * inverse * gathered
    cal_grad = weight * (weight_grad - group_all(weight * weight_grad, jnp.add, bits))
    cal_grad = cal_grad - scale() * real * weight * (log_weight + entropy)
    inner = group_all(cal * cal_grad, jnp.add, bits)
    score_grad = jnp.concatenate(
        [calibrate_back(r, length, scores, cal_grad, inner, kept[r][0], kept[r][1], probs_s) for r in range(rows)],
        axis=0,
    )
    score_grad = score_grad * inverse
    q_grad = score_grad
    for o in OFFSETS:
        q_grad = q_grad + same[o] * shift(score_grad, o)
    q_grad = group_all(q_grad * real, jnp.add, bits)

    scorer16 = jnp.concatenate([scorer, scorer, jnp.zeros((EDGE - 2, width), BF16)], axis=0)
    for r in range(rows):
        at = r * SIZES
        q_high, q_low = split2(q_grad[at : at + 1])
        for t in range(tiles):
            lanes = slice(t * TILE, (t + 1) * TILE)
            all_lanes = slice(r * length + t * TILE, r * length + (t + 1) * TILE)
            first = t * TILE // 2
            matrix_s[r * tiles + t, 2 * window :] = jnp.concatenate(
                [q_high[:, lanes], q_low[:, lanes], jnp.zeros((EDGE - 2, TILE), F32)], axis=0
            ).astype(BF16)
            here = cot_s[r, first : first + window, :]
            given = jnp.concatenate([here, here, scorer16], axis=0)
            hgrad_s[all_lanes, :] = lax.dot_general(
                matrix_s[r * tiles + t], given, (((0,), (0,)), ((), ())), preferred_element_type=F32
            ).astype(BF16)

    def pool():
        for r in range(rows):
            for t in range(tiles):
                first = t * TILE // 2
                out = lax.dot_general(
                    matrix_s[r * tiles + t],
                    hidden_s[:, r * length + t * TILE : r * length + (t + 1) * TILE],
                    (((1,), (1,)), ((), ())),
                    preferred_element_type=F32,
                )
                pooled_s[r, first : first + window, :] += out[:window] + out[window : 2 * window]
                part_ref[0:1, :] += out[2 * window : 2 * window + 1] + out[2 * window + 1 : 2 * window + 2]
            blocks_ref[r] = pooled_s[r, EDGE : EDGE + half, :].astype(BF16)

    return pool


def fill_cotangent(rows, half, width, cot_ref, cot_s):
    cot_s[:, 0:EDGE, :] = jnp.zeros((rows, EDGE, width), BF16)
    cot_s[:, EDGE + half :, :] = jnp.zeros((rows, EDGE, width), BF16)
    for r in range(rows):
        cot_s[r, EDGE : EDGE + half, :] = cot_ref[r]


def fill_q(count, tq16, const, onehot_s, q_s):
    def step(t, carry):
        lanes = pl.ds(pl.multiple_of(t * TILE, TILE), TILE)
        got = jnp.dot(tq16, onehot_s[:, lanes], preferred_element_type=F32)
        q_s[0:1, lanes] = got[0:1] + got[1:2] + got[2:3] + const
        return carry

    lax.fori_loop(0, count, step, 0)


def fill_hidden(count, table, bias_column, onehot_s, hidden_s):
    def step(t, carry):
        lanes = pl.ds(pl.multiple_of(t * TILE, TILE), TILE)
        got = jnp.dot(table(), onehot_s[:, lanes], preferred_element_type=F32)
        hidden_s[:, lanes] = (got + bias_column).astype(BF16)
        return carry

    lax.fori_loop(0, count, step, 0)


def local_scratch(rows, length, width, vocab):
    half = length // 2
    return [
        pltpu.VMEM((8, rows * length), jnp.int32),
        pltpu.VMEM((TAPS * vocab, rows * length), BF16),
        pltpu.VMEM((width, rows * length), BF16),
        pltpu.VMEM((8, rows * length), F32),
        pltpu.VMEM((rows, length, length), BF16),
        pltpu.VMEM((length, TILE), F32),
        pltpu.VMEM((rows, half + 2 * EDGE, width), BF16),
        pltpu.VMEM((8, rows * length), F32),
        pltpu.VMEM((rows, half + 2 * EDGE, width), F32),
        pltpu.VMEM((rows * length, width), BF16),
        pltpu.VMEM((rows * (length // TILE), TILE + 5 * EDGE, TILE), BF16),
    ]


def main_kernel(
    dims, len_ref, aux_ref, small_ref, ids_ref, mask_ref, table_ref, tq_ref, bias_ref, scorer_ref, cot_ref,
    blocks_ref, grad_ref, part_ref,
    taps_s, onehot_s, hidden_s, q_s, probs_s, similar_s, cot_s, band_s, pooled_s, hgrad_s, matrix_s,
):
    rows, length, width, vocab = dims
    count = rows * (length // TILE)
    seg_list, real_list = row_masks(rows, length, len_ref, ids_ref, mask_ref, taps_s)
    fill_cotangent(rows, length // 2, width, cot_ref, cot_s)
    fill_onehot(count, vocab, taps_s, onehot_s)
    m = members_of(rows, length, seg_list, real_list)
    fill_q(count, tq_ref[...], small_ref[1:2, 0:1], onehot_s, q_s)
    scores = block_scores(rows, length, m, q_s)

    def late_hidden():
        fill_hidden(count, lambda: table_ref[...], bias_ref[...], onehot_s, hidden_s)

    def scale():
        return aux_ref[0, 0] / small_ref[0:1, 0:1]

    refs = (hidden_s, cot_s, band_s, pooled_s, hgrad_s, probs_s, similar_s, blocks_ref, part_ref, matrix_s, late_hidden)
    pool = middle(dims, m, scores, seg_list, real_list, scale, scorer_ref[...], refs, lambda r, t: None)
    pool()

    def grad_step(k, carry):
        symbols = pl.ds(pl.multiple_of(k * vocab, vocab), vocab)
        for c in range(width // TILE):
            cols = slice(c * TILE, (c + 1) * TILE)
            grad_ref[symbols, cols] = jnp.dot(
                onehot_s[symbols, :], hgrad_s[:, cols], preferred_element_type=F32
            )
        return carry

    lax.fori_loop(0, TAPS, grad_step, 0)


def main_call(lengths, aux, small, ids, mask, table, tq, bias, scorer, cot):
    rows, length = ids.shape
    width = cot.shape[2]
    vocab = table.shape[1] // TAPS
    dims = (rows, length, width, vocab)
    vmem = pl.BlockSpec(memory_space=pltpu.VMEM)
    smem = pl.BlockSpec(memory_space=pltpu.SMEM)
    half = length // 2
    return pl.pallas_call(
        functools.partial(main_kernel, dims),
        out_shape=(
            jax.ShapeDtypeStruct((rows, half, width), BF16),
            jax.ShapeDtypeStruct((TAPS * vocab, width), F32),
            jax.ShapeDtypeStruct((8, width), F32),
        ),
        in_specs=[smem, smem] + [vmem] * 8,
        out_specs=(vmem, vmem, vmem),
        scratch_shapes=local_scratch(rows, length, width, vocab),
        compiler_params=pltpu.CompilerParams(vmem_limit_bytes=60 * 1024 * 1024),
        name="latent",
    )(lengths, aux, small, ids, mask, table, tq, bias, scorer, cot)


MESH = pl.DeviceIdType.MESH
ALL = slice(None)


def split3(x):
    a = x.astype(BF16).astype(F32)
    b = (x - a).astype(BF16).astype(F32)
    return a, b, x - a - b


def remote(src, dst, send, recv, device):
    return pltpu.make_async_remote_copy(
        src_ref=src, dst_ref=dst, send_sem=send, recv_sem=recv, device_id=device, device_id_type=MESH
    )


def device_at(c, x, y, z):
    return (z * 2 + y, x * 2 + c)


class Gather:
    def __init__(self, buf, me, send, recv, chunks):
        self.buf, self.me, self.send, self.recv, self.chunks = buf, me, send, recv, chunks
        self.rows = buf.shape[4] // chunks
        self.copies = {}

    def part(self, c, x, y, z, chunk, half=None):
        if half is None:
            return self.buf.at[c, x, y, z, pl.ds(chunk * self.rows, self.rows)]
        return self.buf.at[c, x, y, z, pl.ds(chunk * self.rows + half * (self.rows // 2), self.rows // 2)]

    def go(self, chunk, n, ref, device):
        at = chunk * 11 + n
        copy = remote(ref, ref, self.send.at[at], self.recv.at[at], device)
        copy.start()
        self.copies[chunk, n] = copy

    def along_z(self, chunk):
        c, x, y, z = self.me
        for i in range(1, 4):
            self.go(chunk, i - 1, self.part(c, x, y, z, chunk), device_at(c, x, y, lax.rem(z + i, 4)))

    def across(self, chunk, step):
        c, x, y, z = self.me
        copies = self.copies
        core, over_x, over_y = device_at(1 - c, x, y, z), device_at(c, 1 - x, y, z), device_at(c, x, 1 - y, z)
        if step == 0:
            for n in range(3):
                copies[chunk, n].wait_recv()
            mine = self.part(c, x, y, ALL, chunk)
            self.go(chunk, 3, mine, over_x)
            self.go(chunk, 4, mine, over_y)
            self.go(chunk, 5, mine, core)
        elif step == 1:
            copies[chunk, 3].wait_recv()
            self.go(chunk, 6, self.part(c, 1 - x, y, ALL, chunk, 0), over_y)
            self.go(chunk, 7, self.part(c, 1 - x, y, ALL, chunk), core)
            copies[chunk, 4].wait_recv()
            self.go(chunk, 8, self.part(c, x, 1 - y, ALL, chunk, 1), over_x)
            self.go(chunk, 9, self.part(c, x, 1 - y, ALL, chunk), core)
        else:
            copies[chunk, 6].wait_recv()
            copies[chunk, 8].wait_recv()
            self.go(chunk, 10, self.part(c, 1 - x, 1 - y, ALL, chunk), core)

    def arrived(self, chunk):
        for n in (5, 7, 9, 10):
            self.copies[chunk, n].wait_recv()

    def drain(self):
        for copy in self.copies.values():
            copy.wait_send()


def place_of(slot, taps, per_tap):
    slot = jnp.minimum(slot, taps * per_tap - 1)
    tap = slot // per_tap
    return tap, slot - tap * per_tap


def static_place(tap, column, per_tap):
    slot = tap * per_tap + column
    return slot // 16, slot // 8 % 2, slot // 4 % 2, slot % 4


def step_kernel(
    dims,
    len_in, aux_in, ids_in, mask_in, emb_ref, conv_ref, bias_in, scorer_in, cot_ref,
    blocks_ref, final_ref, sums_out,
    taps_s, onehot_s, hidden_s, q_s, probs_s, similar_s, cot_s, band_s, pooled_s, hgrad_s, matrix_s,
    blocks_s, part_s, conv_s, emb_s,
    small_s, smalls_s, wcol_s, emball_s, tq_s, tqs_s, count_s, table_s,
    give_s, take_s, own_s, hold_s, pass_s, came_s, zgive_s, zown_s, zcame_s, final_s, sums_s, sumr_s,
    local_sem, start_send, start_recv, half_sem, gather_send, gather_recv,
    core_send, core_recv, quad_send, quad_recv, line_send, line_recv, sum_send, sum_recv,
    len_ref, aux_ref, ids_ref, mask_ref, bias_ref, scorer_ref, sums_ref, in_sem,
):
    rows, length, width, vocab, size, fs = dims
    half = length // 2
    count = rows * (length // TILE)
    per_tap = width // 128
    f, d = lax.axis_index("fsdp"), lax.axis_index("dp")
    z, y = f // 2, lax.rem(f, 2)
    x, c = d // 2, lax.rem(d, 2)
    me = (c, x, y, z)
    core = device_at(1 - c, x, y, z)

    barrier = pltpu.get_barrier_semaphore()
    peers = [(lax.rem(f + i, fs), d) for i in range(1, fs)]
    others = [core, device_at(c, 1 - x, y, z), device_at(c, 1 - x, 1 - y, z)]
    for peer in peers + others:
        pl.semaphore_signal(barrier, inc=1, device_id=peer, device_id_type=MESH)

    inputs = [
        pltpu.make_async_copy(source, target, in_sem.at[n])
        for n, (source, target) in enumerate(
            [
                (len_in, len_ref),
                (ids_in, ids_ref),
                (mask_in, mask_ref),
                (bias_in, bias_ref),
                (scorer_in, scorer_ref),
                (aux_in, aux_ref),
            ]
        )
    ]
    for copy in inputs:
        copy.start()
    mid = vocab // 2
    my_half = pl.ds(pl.multiple_of(c * mid, mid), mid)
    my_rows = pl.ds(pl.multiple_of(x * (size // 2), size // 2), size // 2)
    my_tap, my_column = place_of(((c * 2 + x) * 2 + y) * 4 + z, TAPS, per_tap)
    local = [
        pltpu.make_async_copy(conv_ref, conv_s, local_sem.at[0]),
        pltpu.make_async_copy(emb_ref, emb_s, local_sem.at[1]),
        pltpu.make_async_copy(
            conv_ref.at[my_tap, :, pl.ds(pl.multiple_of(my_column * 128, 128), 128)], wcol_s.at[f], local_sem.at[2]
        ),
        pltpu.make_async_copy(emb_ref.at[my_rows, my_half], emball_s.at[f, my_rows, my_half], local_sem.at[3]),
    ]
    for r in range(rows):
        local.append(pltpu.make_async_copy(cot_ref.at[r], cot_s.at[r, pl.ds(EDGE, half)], local_sem.at[4 + r]))
    for copy in local:
        copy.start()
    for copy in inputs:
        copy.wait()
    real_here = jnp.sum(jnp.sum(mask_ref[...].astype(F32), axis=1, keepdims=True), axis=0, keepdims=True)
    small_s[...] = jnp.zeros_like(small_s)
    small_s[0:1, 0:size] = bias_ref[...].astype(F32)
    small_s[1:2, 0:size] = scorer_ref[...].astype(F32)
    small_s[2:3, :] = jnp.broadcast_to(real_here, (1, 128))
    smalls_s[f] = small_s[...]
    seg_list, real_list = row_masks(rows, length, len_ref, ids_ref, mask_ref, taps_s)

    pl.semaphore_wait(barrier, fs - 1 + 3)
    starts = []
    for i, peer in enumerate(peers):
        starts.append(remote(small_s, smalls_s.at[f], start_send.at[0, i], start_recv.at[0, i], peer))
        starts[-1].start()
    for i, peer in enumerate(peers):
        mine = emb_ref.at[my_rows, my_half]
        starts.append(
            remote(mine, emball_s.at[f, my_rows, my_half], start_send.at[1, i], start_recv.at[1, i], peer)
        )
        starts[-1].start()
    for i, peer in enumerate(peers):
        tap, column = place_of(((c * 2 + x) * 2 + lax.rem(peer[0], 2)) * 4 + peer[0] // 2, TAPS, per_tap)
        mine = conv_ref.at[tap, :, pl.ds(pl.multiple_of(column * 128, 128), 128)]
        starts.append(remote(mine, wcol_s.at[f], start_send.at[2, i], start_recv.at[2, i], peer))
        starts[-1].start()

    fill_onehot(count, vocab, taps_s, onehot_s)
    cot_s[:, 0:EDGE, :] = jnp.zeros((rows, EDGE, width), BF16)
    cot_s[:, EDGE + half :, :] = jnp.zeros((rows, EDGE, width), BF16)

    for copy in local[2:4]:
        copy.wait()
    for i in range(fs - 1):
        starts[fs - 1 + i].wait_recv()
    mine = emball_s.at[:, my_rows, my_half]
    emb_x = remote(mine, mine, half_sem.at[6], half_sem.at[7], device_at(c, 1 - x, y, z))
    emb_x.start()

    for i in range(fs - 1):
        starts[i].wait_recv()
    line = jnp.zeros((16, width), F32)
    real_sum = jnp.zeros((1, 1), F32)
    lane = lax.broadcasted_iota(jnp.int32, (128, width), 0)
    at = lax.broadcasted_iota(jnp.int32, (128, width), 1)
    for g in range(fs):
        pick = jnp.where((at == lane + g * size) & (lane < size), 1.0, 0.0).astype(BF16)
        both = jnp.concatenate([smalls_s[g], jnp.zeros((8, 128), F32)], axis=0)
        keep = lax.broadcasted_iota(jnp.int32, (16, 128), 0) < 2
        line = line + jnp.dot(jnp.where(keep, both, 0.0).astype(BF16), pick, preferred_element_type=F32)
        real_sum = real_sum + smalls_s[g][2:3, 0:1]
    count_s[0] = jnp.broadcast_to(real_sum, (8, 128))
    count_x = remote(
        count_s.at[0], count_s.at[1], half_sem.at[0], half_sem.at[1], device_at(c, 1 - x, y, z)
    )
    count_x.start()
    line16 = line.astype(BF16)
    bias_column = jnp.concatenate([line, jnp.zeros((112, width), F32)], axis=0).T[:, 0:1]
    const = jnp.sum(line[0:1] * line[1:2], axis=1, keepdims=True)
    scorer = line16[1:2]
    local[0].wait()
    local[1].wait()
    across = (((1,), (1,)), ((), ()))
    u = jnp.concatenate(
        [
            lax.dot_general(line16, conv_s[k], across, preferred_element_type=F32)[1:2]
            for k in range(TAPS)
        ],
        axis=0,
    )
    u = jnp.concatenate(list(split3(u)) + [jnp.zeros((1, size), F32)], axis=0).astype(BF16)
    tq = jnp.dot(u, emb_s[...], preferred_element_type=F32)
    tq_s[...] = jnp.zeros_like(tq_s)
    tq_s[0:TAPS, :] = tq[0:TAPS] + tq[TAPS : 2 * TAPS] + tq[2 * TAPS : 3 * TAPS]
    tqs_s[f] = tq_s[...]
    tq_copies = []
    for i, peer in enumerate(peers):
        copy = remote(tq_s, tqs_s.at[f], start_send.at[3, i], start_recv.at[3, i], peer)
        copy.start()
        tq_copies.append(copy)

    emb_x.wait_recv()
    mine = emball_s.at[:, :, my_half]
    emb_core = remote(mine, mine, half_sem.at[2], half_sem.at[3], core)
    emb_core.start()
    for i in range(fs - 1):
        starts[2 * (fs - 1) + i].wait_recv()
    emb_core.wait_recv()
    block = lax.dot_general(
        wcol_s[...].reshape(fs * size, 128),
        emball_s[...].reshape(fs * size, vocab),
        (((0,), (0,)), ((), ())),
        preferred_element_type=F32,
    )
    table_s[c, x, y, z] = block.astype(BF16)
    tables = Gather(table_s, me, gather_send.at[0], gather_recv.at[0], TABLE_CHUNKS)
    for chunk in range(TABLE_CHUNKS):
        tables.along_z(chunk)

    count_x.wait_recv()
    count_s[2] = count_s[0] + count_s[1]
    count_c = remote(count_s.at[2], count_s.at[3], half_sem.at[4], half_sem.at[5], core)
    count_c.start()

    m = members_of(rows, length, seg_list, real_list)
    for copy in tq_copies:
        copy.wait_recv()
    tq = tqs_s[0]
    for g in range(1, fs):
        tq = tq + tqs_s[g]
    tq16 = jnp.concatenate(
        [
            jnp.concatenate(list(split3(tq[k : k + 1])) + [jnp.zeros((13, vocab), F32)], axis=0)
            for k in range(TAPS)
        ],
        axis=1,
    ).astype(BF16)
    fill_q(count, tq16, const, onehot_s, q_s)
    scores = block_scores(rows, length, m, q_s)

    part = 128 // TABLE_CHUNKS

    def table_rows(chunk):
        return jnp.concatenate(
            [
                jnp.concatenate(
                    [
                        table_s[(*static_place(k, j, per_tap), slice(chunk * part, (chunk + 1) * part))]
                        for j in range(per_tap)
                    ],
                    axis=0,
                )
                for k in range(TAPS)
            ],
            axis=1,
        )

    def hidden_part(chunk, low, high):
        if low == 0 and chunk < TABLE_CHUNKS - 1:
            tables.arrived(chunk)
        bias_part = jnp.concatenate(
            [bias_column[j * 128 + chunk * part : j * 128 + (chunk + 1) * part] for j in range(per_tap)], axis=0
        )

        def step(t, carry):
            lanes = pl.ds(pl.multiple_of(t * TILE, TILE), TILE)
            got = jnp.dot(table_rows(chunk), onehot_s[:, lanes], preferred_element_type=F32)
            got = (got + bias_part).astype(BF16)
            for j in range(per_tap):
                hidden_s[j * 128 + chunk * part : j * 128 + (chunk + 1) * part, lanes] = got[
                    j * part : (j + 1) * part
                ]
            return carry

        for t in range(count * low // 4, count * high // 4):
            step(t, 0)

    order = [(0, 0), (1, 0), (0, 1), (1, 1), (0, 2), (0, 0, 2), (1, 2), (0, 2, 4), (1, 0, 4)]
    steps = [
        functools.partial(tables.across if len(n) == 2 else hidden_part, *n) for n in order
    ]
    turns = {(0, 1): 1, (0, 3): 1, (1, 1): 1, (1, 3): 1}

    def between(r, t):
        for _ in range(turns.get((r, t), 0)):
            steps.pop(0)()

    def late_hidden():
        while len(steps) > 1:
            steps.pop(0)()
        tables.arrived(TABLE_CHUNKS - 1)
        tables.drain()
        for copy in local[4:]:
            copy.wait()
        count_c.wait_recv()
        steps.pop(0)()

    def scale():
        return aux_ref[0, 0] / (count_s[2][0:1, 0:1] + count_s[3][0:1, 0:1])

    refs = (hidden_s, cot_s, band_s, pooled_s, hgrad_s, probs_s, similar_s, blocks_s, part_s, matrix_s, late_hidden)
    pool = middle(dims[:4], m, scores, seg_list, real_list, scale, scorer, refs, between)
    def product(slot):
        tap, column = place_of(jnp.minimum(slot, TAPS * per_tap - 2), TAPS, per_tap)
        symbols = pl.ds(pl.multiple_of(tap * vocab, vocab), vocab)
        lanes = pl.ds(pl.multiple_of(column * 128, 256), 256)
        return jnp.dot(onehot_s[symbols, :], hgrad_s[:, lanes], preferred_element_type=F32)

    def core_copy(p):
        return remote(give_s.at[p], take_s.at[p], core_send.at[p], core_recv.at[p], core)

    def pair_of(q, n):
        return lax.rem(x + q // 2, 2) * 4 + lax.rem(y + q % 2, 2) * 2 + n

    def give(q, n):
        p = pair_of(q, n)
        give_s[p] = product((1 - c) * 16 + 2 * p)
        core_copy(p).start()

    def keep(q, n):
        p = pair_of(q, n)
        got = product(c * 16 + 2 * p)
        core_copy(p).wait_recv()
        return got + take_s[p]

    gap = vocab // 2
    over_x, over_y = device_at(c, 1 - x, y, z), device_at(c, x, 1 - y, z)

    def quad_copy(q, n, part):
        at = (3 - q) * 2 + n
        ref = at, pl.ds(part * gap, gap)
        to = over_x if q == 2 or (q == 3 and part == 0) else over_y
        return remote(pass_s.at[ref], came_s.at[ref], quad_send.at[at * 2 + part], quad_recv.at[at * 2 + part], to)

    parts = [slice(0, gap), slice(gap, 2 * gap)]
    def across(n):
        pass_s[n] = keep(3, n).astype(BF16)
        quad_copy(3, n, 0).start()
        quad_copy(3, n, 1).start()

    def beside(q, n):
        got = keep(q, n)
        plain = 2 - q
        pass_s[(3 - q) * 2 + n, parts[plain]] = got[parts[plain]].astype(BF16)
        quad_copy(q, n, plain).start()
        hold_s[2 - q, n] = got[parts[1 - plain]]

    def mixed(q, n):
        part = q - 1
        quad_copy(3, n, part).wait_recv()
        pass_s[(3 - q) * 2 + n, parts[part]] = (
            hold_s[2 - q, n] + came_s[n, parts[part]].astype(F32)
        ).astype(BF16)
        quad_copy(q, n, part).start()

    give(3, 0)
    give(3, 1)
    give(2, 0)
    give(1, 0)
    across(0)
    across(1)
    beside(2, 0)
    beside(1, 0)
    give(2, 1)
    give(1, 1)
    mixed(1, 0)
    mixed(2, 0)
    give(0, 0)
    beside(2, 1)
    beside(1, 1)
    mixed(1, 1)
    mixed(2, 1)
    give(0, 1)
    own_s[0] = keep(0, 0)
    own_s[1] = keep(0, 1)

    pool()
    blocks_out = pltpu.make_async_copy(blocks_s, blocks_ref, local_sem.at[0])
    blocks_out.start()
    sums_s[0] = part_s[...]
    sum_copies = [remote(sums_s.at[0], sumr_s.at[0], sum_send.at[0], sum_recv.at[0], core)]
    sum_copies[0].start()

    def sums_quad():
        sum_copies[0].wait_recv()
        sums_s[1] = sums_s[0] + sumr_s[0]
        quad = [device_at(c, lax.rem(x + q // 2, 2), lax.rem(y + q % 2, 2), z) for q in range(4)]
        for q in range(1, 4):
            sum_copies.append(remote(sums_s.at[1], sumr_s.at[q], sum_send.at[q], sum_recv.at[q], quad[q]))
            sum_copies[-1].start()

    def sums_line():
        for q in range(1, 4):
            sum_copies[q].wait_recv()
        sums_s[2] = (sums_s[1] + sumr_s[1]) + (sumr_s[2] + sumr_s[3])
        for i in range(1, 4):
            to = device_at(c, x, y, lax.rem(z + i, 4))
            sum_copies.append(remote(sums_s.at[2], sumr_s.at[3 + i], sum_send.at[3 + i], sum_recv.at[3 + i], to))
            sum_copies[-1].start()

    grads = Gather(final_s, me, gather_send.at[1], gather_recv.at[1], GRAD_CHUNKS)
    line_copies = {}

    def to_line(chunk):
        part = slice(chunk * gap, (chunk + 1) * gap)
        for q in (2, 1):
            for n in range(2):
                quad_copy(q, n, chunk).wait_recv()
        for t in range(2):
            total = own_s[t, part] + (came_s[2 + t, part].astype(F32) + came_s[4 + t, part].astype(F32))
            for j in range(2):
                zown_s[2 * t + j, part] = total[:, j * 128 : (j + 1) * 128]
                zgive_s[2 * t + j, part] = total[:, j * 128 : (j + 1) * 128].astype(BF16)
        for i in range(1, 4):
            to = lax.rem(z + i, 4)
            at = chunk * 3 + i - 1
            part = pl.ds(chunk * gap, gap)
            copy = remote(
                zgive_s.at[to, part],
                zcame_s.at[i - 1, part],
                line_send.at[at],
                line_recv.at[at],
                device_at(c, x, y, to),
            )
            copy.start()
            line_copies[chunk, i] = copy

    def from_line(chunk):
        part = slice(chunk * gap, (chunk + 1) * gap)
        total = zown_s[z, part]
        for i in range(1, 4):
            line_copies[chunk, i].wait_recv()
            total = total + zcame_s[i - 1, part].astype(F32)
        final_s[c, x, y, z, part] = total.astype(BF16)
        grads.along_z(chunk)

    def put(chunk):
        part = pl.ds(chunk * gap, gap)
        ref = ALL, ALL, ALL, ALL, part
        out_copies.append(pltpu.make_async_copy(final_s.at[ref], final_ref.at[ref], local_sem.at[1 + chunk]))
        out_copies[-1].start()

    out_copies = []
    to_line(0)
    to_line(1)
    from_line(0)
    from_line(1)
    sums_quad()
    grads.across(0, 0)
    sums_line()
    grads.across(1, 0)
    grads.across(0, 1)
    grads.across(1, 1)
    grads.across(0, 2)
    grads.across(1, 2)
    grads.arrived(0)
    put(0)
    grads.arrived(1)
    put(1)
    grads.drain()

    for i in range(4, 7):
        sum_copies[i].wait_recv()
    sums = (sums_s[2] + sumr_s[4]) + (sumr_s[5] + sumr_s[6])
    total_count = count_s[2][0:1, 0:1] + count_s[3][0:1, 0:1]
    sums_ref[...] = jnp.concatenate([sums[0:1], sums[1:2] / total_count, sums[2:8]], axis=0)
    out_copies.append(pltpu.make_async_copy(sums_ref, sums_out, in_sem.at[0]))
    out_copies[-1].start()

    for copy in starts + tq_copies + sum_copies + list(line_copies.values()) + [count_x, count_c, emb_x, emb_core]:
        copy.wait_send()
    for p in range(8):
        core_copy(p).wait_send()
    for chunk in range(GRAD_CHUNKS):
        for q in (3, 2, 1):
            for n in range(2):
                quad_copy(q, n, chunk).wait_send()
    for copy in out_copies + [blocks_out]:
        copy.wait()


def last_kernel(
    dims, blocks_ref, final_ref, sums_in, emb_ref, conv_ref,
    out_ref, loss_out, embg_out, convg_ref, biasg_out, scoreg_out,
    blocks_s, final_s, emb_s, conv_s, convg_s, in_sem, out_sem,
    sums_ref, loss_ref, embg_ref, biasg_ref, scoreg_ref,
):
    rows, length, width, vocab, size, fs = dims
    per_tap = width // 128
    copies = [
        pltpu.make_async_copy(emb_ref, emb_s, in_sem.at[0]),
        pltpu.make_async_copy(conv_ref, conv_s, in_sem.at[1]),
    ]
    for n in range(4):
        copies.append(
            pltpu.make_async_copy(final_ref.at[n // 2, n % 2], final_s.at[n // 2, n % 2], in_sem.at[2 + n])
        )
    blocks = [pltpu.make_async_copy(blocks_ref.at[r], blocks_s.at[r], in_sem.at[6 + r]) for r in range(rows)]
    copies.append(pltpu.make_async_copy(sums_in, sums_ref, in_sem.at[6 + rows]))
    for copy in copies + blocks:
        copy.start()
    outs = []
    have = 0
    copies[0].wait()
    copies[1].wait()
    emb_total = None
    for k in range(TAPS):
        while have * 8 < (k + 1) * per_tap:
            copies[2 + have].wait()
            have += 1
        grad = jnp.concatenate([final_s[static_place(k, j, per_tap)] for j in range(per_tap)], axis=1)
        convg_s[k] = jnp.dot(emb_s[...], grad, preferred_element_type=F32)
        outs.append(pltpu.make_async_copy(convg_s.at[k], convg_ref.at[k], out_sem.at[k]))
        outs[-1].start()
        term = lax.dot_general(conv_s[k], grad, (((1,), (1,)), ((), ())), preferred_element_type=F32)
        emb_total = term if emb_total is None else emb_total + term
        if k == TAPS // 2:
            bias_line = jnp.sum(grad.astype(F32), axis=0, keepdims=True)
        if k < rows:
            blocks[k].wait()
            outs.append(pltpu.make_async_copy(blocks_s.at[k], out_ref.at[k], out_sem.at[TAPS + k]))
            outs[-1].start()
    embg_ref[...] = emb_total
    copies[6].wait()
    f = lax.axis_index("fsdp")
    lane = lax.broadcasted_iota(jnp.int32, (128, width), 0)
    at = lax.broadcasted_iota(jnp.int32, (128, width), 1)
    pick = jnp.where((at == lane + f * size) & (lane < size), 1.0, 0.0).astype(BF16)
    lines = jnp.concatenate(
        list(split3(bias_line)) + list(split3(sums_ref[0:1])) + [jnp.zeros((10, width), F32)], axis=0
    ).astype(BF16)
    mine = lax.dot_general(lines, pick, (((1,), (1,)), ((), ())), preferred_element_type=F32)
    biasg_ref[...] = (mine[0:1] + mine[1:2] + mine[2:3])[:, :size]
    scoreg_ref[...] = (mine[3:4] + mine[4:5] + mine[5:6])[:, :size]
    loss_ref[...] = sums_ref[1:2, 0:1]
    for n, (source, target) in enumerate(
        [(embg_ref, embg_out), (biasg_ref, biasg_out), (scoreg_ref, scoreg_out), (loss_ref, loss_out)]
    ):
        outs.append(pltpu.make_async_copy(source, target, out_sem.at[TAPS + rows + n]))
        outs[-1].start()
    while have < 4:
        copies[2 + have].wait()
        have += 1
    for copy in outs:
        copy.wait()


def step_shards(byte_ids, doc_lengths, pad_mask, embedding, conv_weight, conv_bias, scorer, cotangent, aux_weight):
    rows, length = byte_ids.shape
    vocab, size = embedding.shape
    width = conv_weight.shape[2]
    half = length // 2
    fs = width // size
    dims = (rows, length, width, vocab, size, fs)
    hbm = pl.BlockSpec(memory_space=pl.ANY)
    dma = pltpu.SemaphoreType.DMA
    blocks, final, sums = pl.pallas_call(
        functools.partial(step_kernel, dims),
        out_shape=(
            jax.ShapeDtypeStruct((rows, half, width), BF16),
            jax.ShapeDtypeStruct((2, 2, 2, 4, vocab, 128), BF16),
            jax.ShapeDtypeStruct((8, width), F32),
        ),
        in_specs=[hbm] * 9,
        out_specs=(hbm, hbm, hbm),
        scratch_shapes=local_scratch(rows, length, width, vocab)
        + [
            pltpu.VMEM((rows, half, width), BF16),
            pltpu.VMEM((8, width), F32),
            pltpu.VMEM((TAPS, size, width), BF16),
            pltpu.VMEM((size, vocab), BF16),
            pltpu.VMEM((8, 128), F32),
            pltpu.VMEM((fs, 8, 128), F32),
            pltpu.VMEM((fs, size, 128), BF16),
            pltpu.VMEM((fs, size, vocab), BF16),
            pltpu.VMEM((8, vocab), F32),
            pltpu.VMEM((fs, 8, vocab), F32),
            pltpu.VMEM((4, 8, 128), F32),
            pltpu.VMEM((2, 2, 2, 4, 128, vocab), BF16),
            pltpu.VMEM((8, vocab, 256), F32),
            pltpu.VMEM((8, vocab, 256), F32),
            pltpu.VMEM((2, vocab, 256), F32),
            pltpu.VMEM((2, 2, vocab // 2, 256), F32),
            pltpu.VMEM((6, vocab, 256), BF16),
            pltpu.VMEM((6, vocab, 256), BF16),
            pltpu.VMEM((4, vocab, 128), BF16),
            pltpu.VMEM((4, vocab, 128), F32),
            pltpu.VMEM((3, vocab, 128), BF16),
            pltpu.VMEM((2, 2, 2, 4, vocab, 128), BF16),
            pltpu.VMEM((3, 8, width), F32),
            pltpu.VMEM((7, 8, width), F32),
            dma((4 + max(rows, 2),)),
            dma((4, fs - 1)),
            dma((4, fs - 1)),
            dma((8,)),
            dma((2, 11 * max(TABLE_CHUNKS, GRAD_CHUNKS))),
            dma((2, 11 * max(TABLE_CHUNKS, GRAD_CHUNKS))),
            dma((8,)),
            dma((8,)),
            dma((12,)),
            dma((12,)),
            dma((3 * GRAD_CHUNKS,)),
            dma((3 * GRAD_CHUNKS,)),
            dma((7,)),
            dma((7,)),
            pltpu.SMEM(doc_lengths.shape, jnp.int32),
            pltpu.SMEM((1, 1), F32),
            pltpu.VMEM((rows, length), jnp.int32),
            pltpu.VMEM((rows, length), jnp.int32),
            pltpu.VMEM((1, size), BF16),
            pltpu.VMEM((1, size), BF16),
            pltpu.VMEM((8, width), F32),
            dma((6,)),
        ],
        compiler_params=pltpu.CompilerParams(
            collective_id=0, has_side_effects=True, vmem_limit_bytes=62 * 1024 * 1024
        ),
        name="step",
    )(
        doc_lengths,
        aux_weight.reshape(1, 1),
        byte_ids,
        pad_mask,
        embedding.T,
        conv_weight,
        conv_bias.reshape(1, size),
        scorer.reshape(1, size),
        cotangent,
    )
    blocks, loss, emb_grad, conv_grad, bias_grad, score_grad = pl.pallas_call(
        functools.partial(last_kernel, dims),
        out_shape=(
            jax.ShapeDtypeStruct((rows, half, width), BF16),
            jax.ShapeDtypeStruct((1, 1), F32),
            jax.ShapeDtypeStruct((size, vocab), F32),
            jax.ShapeDtypeStruct((TAPS, size, width), F32),
            jax.ShapeDtypeStruct((1, size), F32),
            jax.ShapeDtypeStruct((1, size), F32),
        ),
        in_specs=[hbm] * 5,
        out_specs=(hbm,) * 6,
        scratch_shapes=[
            pltpu.VMEM((rows, half, width), BF16),
            pltpu.VMEM((2, 2, 2, 4, vocab, 128), BF16),
            pltpu.VMEM((size, vocab), BF16),
            pltpu.VMEM((TAPS, size, width), BF16),
            pltpu.VMEM((TAPS, size, width), F32),
            dma((7 + rows,)),
            dma((rows + TAPS + 4,)),
            pltpu.VMEM((8, width), F32),
            pltpu.VMEM((1, 1), F32),
            pltpu.VMEM((size, vocab), F32),
            pltpu.VMEM((1, size), F32),
            pltpu.VMEM((1, size), F32),
        ],
        compiler_params=pltpu.CompilerParams(vmem_limit_bytes=62 * 1024 * 1024),
        name="last",
    )(blocks, final, sums, embedding.T, conv_weight)
    return blocks, loss.reshape(()), emb_grad.T, conv_grad, bias_grad.reshape(size), score_grad.reshape(size)


def split3_rows(x):
    a = lax.reduce_precision(x, 8, 7)
    b = lax.reduce_precision(x - a, 8, 7)
    return jnp.concatenate([a, b, x - a - b], axis=0).astype(BF16)


def gathered_shards(byte_ids, doc_lengths, pad_mask, embedding, conv_weight, conv_bias, scorer, cotangent, aux_weight):
    emb = lax.all_gather(embedding, "fsdp", axis=1, tiled=True)
    conv = lax.all_gather(conv_weight, "fsdp", axis=1, tiled=True)
    bias = lax.all_gather(conv_bias, "fsdp", axis=0, tiled=True)
    score = lax.all_gather(scorer, "fsdp", axis=0, tiled=True)
    vocab, width = emb.shape
    count = lax.psum(jnp.sum(pad_mask.astype(F32)), ("fsdp", "dp"))
    table = jnp.einsum("kcd,vc->dkv", conv, emb, preferred_element_type=F32).reshape(width, TAPS * vocab)
    score32 = score.astype(F32)
    q_table = jnp.sum(table * score32[:, None], axis=0, keepdims=True)
    tq = jnp.concatenate([split3_rows(q_table), jnp.zeros((13, TAPS * vocab), BF16)], axis=0)
    bias32 = bias.astype(F32)
    small = jnp.stack([jnp.full((128,), count), jnp.full((128,), jnp.sum(bias32 * score32))])
    small = jnp.concatenate([small, jnp.zeros((6, 128), F32)], axis=0)
    blocks, grad, part = main_call(
        doc_lengths, aux_weight.reshape(1, 1), small, byte_ids, pad_mask, table.astype(BF16), tq, bias32[:, None], score[None, :], cotangent
    )
    grad = lax.psum(grad, ("fsdp", "dp")).reshape(TAPS, vocab, width)
    score_grad = lax.psum(part[0], ("fsdp", "dp"))
    loss = lax.psum(part[1, 0], ("fsdp", "dp")) / count
    size = embedding.shape[1]
    at = lax.axis_index("fsdp") * size
    bias_grad = lax.dynamic_slice_in_dim(jnp.sum(grad[TAPS // 2], axis=0), at, size, 0)
    score_grad = lax.dynamic_slice_in_dim(score_grad, at, size, 0)
    conv_grad = jnp.einsum("vc,kvd->kcd", embedding.astype(F32), grad, precision=lax.Precision.HIGHEST)
    emb_grad = jnp.einsum("kvd,kcd->vc", grad, conv_weight.astype(F32), precision=lax.Precision.HIGHEST)
    return blocks, loss, emb_grad, conv_grad, bias_grad, score_grad


def solution(mesh):
    small = mesh.shape["fsdp"] == 8 and mesh.shape["dp"] == 4
    return jax.shard_map(
        step_shards if small else gathered_shards,
        mesh=mesh,
        in_specs=(
            P(("fsdp", "dp"), None),
            P(("fsdp", "dp"), None),
            P(("fsdp", "dp"), None),
            P(None, "fsdp"),
            P(None, "fsdp", None),
            P("fsdp"),
            P("fsdp"),
            P(("fsdp", "dp"), None, None),
            P(),
        ),
        out_specs=(
            P(("fsdp", "dp"), None, None),
            P(),
            P(None, "fsdp"),
            P(None, "fsdp", None),
            P("fsdp"),
            P("fsdp"),
        ),
        check_vma=False,
    )
```

```python
import functools
import jax
import jax.numpy as jnp
from jax import lax
from jax.experimental import pallas as pl
from jax.experimental.pallas import tpu as pltpu
from jax.sharding import PartitionSpec as P

TAPS = 5
SIZES = 4
NEG = -1000000000.0
F32 = jnp.float32
BF16 = jnp.bfloat16
TILE = 256
EDGE = 16
TABLE_CHUNKS = 2
GRAD_CHUNKS = 2


def split2(x):
    high = x.astype(BF16).astype(F32)
    return high, x - high


def shift(x, offset):
    length = x.shape[1]
    return x if offset == 0 else pltpu.roll(x, (-offset) % length, 1)


def group_pair(x, step, lane_bit):
    size = x.shape[0]
    down = pltpu.roll(x, (size - step) % size, 0)
    up = pltpu.roll(x, step, 0)
    return jnp.where(lane_bit, up, down)


def group_all(x, op, bits):
    x = op(x, group_pair(x, 1, bits[0]))
    return op(x, group_pair(x, 2, bits[1]))


def spread(rows_list, length):
    return jnp.concatenate([jnp.broadcast_to(x, (SIZES, length)) for x in rows_list], axis=0)


def lane_rows(ref, at, r, length):
    return ref[at : at + 1, r * length : (r + 1) * length]


DELTA_EVEN = {-3: -2, -2: -1, -1: -1, 0: 0, 1: 0, 2: 1, 3: 1}
DELTA_ODD = {-3: -1, -2: -1, -1: 0, 0: 0, 1: 1, 2: 1, 3: 2}
OFFSETS = [o for o in range(1 - SIZES, SIZES) if o != 0]


def row_masks(rows, length, len_ref, ids_ref, mask_ref, taps_s):
    place1 = lax.broadcasted_iota(jnp.int32, (1, length), 1)
    seg_list, real_list = [], []
    for r in range(rows):
        end = len_ref[r, 0]
        segment = jnp.where(place1 >= end, 1.0, 0.0)
        for d in range(1, len_ref.shape[1]):
            end = end + len_ref[r, d]
            segment = segment + jnp.where(place1 >= end, 1.0, 0.0)
        seg_list.append(segment)
        real_list.append(mask_ref[r : r + 1, :].astype(F32))
        ids = ids_ref[r : r + 1, :].astype(F32)
        known = jnp.where(real_list[r] > 0.5, ids, -1.0)
        for k in range(TAPS):
            o = k - TAPS // 2
            inside = (place1 + o >= 0) & (place1 + o < length)
            keep = inside & (shift(segment, o) == segment)
            taps_s[k : k + 1, r * length : (r + 1) * length] = jnp.where(
                keep, shift(known, o), -1.0
            ).astype(jnp.int32)
    return seg_list, real_list


def fill_onehot(count, vocab, taps_s, onehot_s):
    symbol = lax.broadcasted_iota(jnp.int32, (vocab, TILE), 0)

    def step(t, carry):
        lanes = pl.ds(pl.multiple_of(t * TILE, TILE), TILE)
        for k in range(TAPS):
            here = taps_s[k : k + 1, lanes]
            onehot_s[k * vocab : (k + 1) * vocab, lanes] = jnp.where(symbol == here, 1.0, 0.0).astype(BF16)
        return carry

    lax.fori_loop(0, count, step, 0)


def members_of(rows, length, seg_list, real_list):
    shape = (rows * SIZES, length)
    place = lax.broadcasted_iota(jnp.int32, shape, 1)
    sub = lax.broadcasted_iota(jnp.int32, shape, 0)
    size = (sub & (SIZES - 1)) + 1
    third = jnp.floor((place.astype(F32) + 0.5) * (1.0 / 3.0)).astype(jnp.int32)
    within = jnp.where(
        size == 1, 0, jnp.where(size == 2, place & 1, jnp.where(size == 3, place - 3 * third, place & 3))
    )
    seg = spread(seg_list, length)
    real = spread(real_list, length)
    same = {}
    for o in range(1, SIZES):
        ahead = (within + o < size) & (place + o < length) & (shift(seg, o) == seg)
        behind = (within - o >= 0) & (shift(seg, -o) == seg)
        same[o] = jnp.where(ahead, 1.0, 0.0)
        same[-o] = jnp.where(behind, 1.0, 0.0)
    member = {o: same[o] * shift(real, o) for o in OFFSETS}
    members = real
    for o in OFFSETS:
        members = members + member[o]
    even = (place & 1) == 0
    pair = jnp.where(even | (shift(seg, -1) == seg), real, 0.0)
    partner = jnp.where(even, shift(pair, 1), shift(pair, -1))
    return dict(
        bits=((sub & 1) == 1, (sub & 2) == 2),
        first=size == 1,
        even=even,
        real=real,
        same=same,
        member=member,
        inverse=1.0 / jnp.maximum(members, 1.0),
        pair_weight=pair / jnp.maximum(pair + partner, 1.0),
    )


def block_scores(rows, length, m, q_s):
    q = spread([lane_rows(q_s, 0, r, length) for r in range(rows)], length)
    total = q * m["real"]
    for o in OFFSETS:
        total = total + m["member"][o] * shift(q, o)
    return total * m["inverse"]


def near_keys(t, length):
    return [
        j
        for j in range(length // 128)
        if max(j * 128 - (t * TILE + TILE - 1), t * TILE - (j * 128 + 127)) < length // 2
    ]


def calibrate_row(r, length, scores, seg, real, similar_s, probs_s, between):
    s = scores[r * SIZES : (r + 1) * SIZES]
    a, rest = split2(s)
    b, c = split2(rest)
    key_seg = jnp.where(real > 0.5, seg, -1.0)
    zero = jnp.zeros((128 - 6 * SIZES - 1, length), F32)
    left = jnp.concatenate([a, a, b, b, a, c, key_seg, zero], axis=0).T
    right = jnp.concatenate([a, b, a, b, c, a, jnp.zeros_like(key_seg), zero], axis=0).astype(BF16)
    key_column = left[:, 6 * SIZES : 6 * SIZES + 1]
    left = left.astype(BF16)
    x = jnp.concatenate(
        [jnp.ones((1, length), F32), s, s[0:1] * s, s[1:2] * s[1:], s[2:3] * s[2:], s[3:4] * s[3:]]
        + [jnp.zeros((1, length), F32)],
        axis=0,
    )
    x_high, x_low = split2(x)
    features = jnp.concatenate([x_high, x_low], axis=0).astype(BF16)
    outs = []
    for t in range(length // TILE):
        lanes = slice(t * TILE, (t + 1) * TILE)
        query_seg = seg[:, lanes]
        top = None
        near = near_keys(t, length)
        for j in near:
            keys = slice(j * 128, (j + 1) * 128)
            sim = jnp.dot(left[keys], right[:, lanes], preferred_element_type=F32)
            allowed = key_column[keys] == query_seg
            if j * 128 // TILE == t:
                key_place = lax.broadcasted_iota(jnp.int32, (128, TILE), 0) + j * 128
                query_place = lax.broadcasted_iota(jnp.int32, (128, TILE), 1) + t * TILE
                allowed = allowed | (key_place == query_place)
            sim = jnp.where(allowed, sim, NEG)
            similar_s[keys, :] = sim
            here = jnp.max(sim, axis=0, keepdims=True)
            top = here if top is None else jnp.maximum(top, here)
        for j in near:
            keys = slice(j * 128, (j + 1) * 128)
            probs_s[r, keys, lanes] = jnp.exp(similar_s[keys, :] - top).astype(BF16)
        keys = slice(near[0] * 128, (near[-1] + 1) * 128)
        outs.append(jnp.dot(features[:, keys], probs_s[r, keys, lanes], preferred_element_type=F32))
        between(r, t)
    moments = jnp.concatenate(outs, axis=1)
    moments = moments[0:16] + moments[16:32]
    norm = 1.0 / moments[0:1]
    return moments * norm, norm


def size_softmax(cal, bits):
    top = group_all(cal, jnp.maximum, bits)
    log_weight = (cal - top) - jnp.log(group_all(jnp.exp(cal - top), jnp.add, bits))
    weight = jnp.exp(log_weight)
    entropy = -group_all(weight * log_weight, jnp.add, bits)
    return weight, log_weight, entropy


def band_products(rows, length, cot_s, hidden_s, band_s, window, diagonal):
    for r in range(rows):
        for t in range(length // TILE):
            lanes = slice(r * length + t * TILE, r * length + (t + 1) * TILE)
            first = t * TILE // 2
            prod = jnp.dot(
                cot_s[r, first : first + window, :], hidden_s[:, lanes], preferred_element_type=F32
            )
            for d in range(-2, 3):
                band_s[d + 2 : d + 3, lanes] = jnp.sum(jnp.where(diagonal == d, prod, 0.0), axis=0, keepdims=True)


def calibrate_back(r, length, scores, cal_grad, inner, moments, norm, probs_s):
    part = slice(r * SIZES, (r + 1) * SIZES)
    s, g, ri = scores[part], cal_grad[part], inner[r * SIZES : r * SIZES + 1]
    at = {}
    n = 1 + SIZES
    for a in range(SIZES):
        for b in range(a, SIZES):
            at[a, b] = at[b, a] = n
            n += 1
    query = []
    for a in range(SIZES):
        total = -moments[1 + a : 2 + a] * ri
        for b in range(SIZES):
            total = total + moments[at[a, b] : at[a, b] + 1] * g[b : b + 1]
        query.append(total)
    y = jnp.concatenate([g - s * ri] + [s[a : a + 1] * g for a in range(SIZES)], axis=0) * norm
    y = jnp.concatenate([y, jnp.zeros((4, length), F32)], axis=0)
    y_high, y_low = split2(y)
    features = jnp.concatenate([y_high, y_low], axis=0).astype(BF16)
    outs = []
    for t in range(length // TILE):
        keys = slice(t * TILE, (t + 1) * TILE)
        outs.append(
            lax.dot_general(
                features[:, max(t - 2, 0) * TILE : (t + 3) * TILE],
                probs_s[r, keys, max(t - 2, 0) * TILE : min(t + 3, length // TILE) * TILE],
                (((1,), (1,)), ((), ())),
                preferred_element_type=F32,
            )
        )
    back = jnp.concatenate(outs, axis=1)
    back = back[0:24] + back[24:48]
    key = []
    for a in range(SIZES):
        total = back[a : a + 1]
        for b in range(SIZES):
            n = SIZES + a * SIZES + b
            total = total + s[b : b + 1] * back[n : n + 1]
        key.append(total + query[a])
    return jnp.concatenate(key, axis=0)


def middle(dims, m, scores, seg_list, real_list, scale, scorer, refs, between):
    rows, length, width, vocab = dims
    half = length // 2
    tiles = length // TILE
    window = TILE // 2 + 2 * EDGE
    hidden_s, cot_s, band_s, pooled_s, hgrad_s, probs_s, similar_s, blocks_ref, part_ref, matrix_s, late_hidden = refs
    bits, real, same, member, inverse, pair_weight = (
        m[n] for n in ("bits", "real", "same", "member", "inverse", "pair_weight")
    )
    kept = [
        calibrate_row(r, length, scores, seg_list[r], real_list[r], similar_s, probs_s, between) for r in range(rows)
    ]
    cal = jnp.concatenate([moments[1 : 1 + SIZES] for moments, norm in kept], axis=0)
    weight, log_weight, entropy = size_softmax(cal, bits)
    entropy_sum = jnp.sum(
        jnp.sum(jnp.where(m["first"], entropy * real, 0.0), axis=1, keepdims=True), axis=0, keepdims=True
    )
    part_ref[...] = jnp.zeros_like(part_ref)
    part_ref[1:2, :] = jnp.broadcast_to(entropy_sum, (1, width))
    for r in range(rows):
        pooled_s[r] = jnp.zeros_like(pooled_s[r])

    use = pair_weight * weight * inverse
    moved = {o: (use if o == 0 else same[o] * shift(use, o)) for o in range(1 - SIZES, SIZES)}
    mix = []
    for d in range(-2, 3):
        odd_sum = sum([moved[o] for o in moved if DELTA_ODD[o] == d], jnp.zeros_like(use))
        even_sum = sum([moved[o] for o in moved if DELTA_EVEN[o] == d], jnp.zeros_like(use))
        mix.append(group_all(jnp.where(m["even"], even_sum, odd_sum) * real, jnp.add, bits))

    kl = lax.broadcasted_iota(jnp.int32, (window, TILE), 0)
    diagonal = kl - (lax.broadcasted_iota(jnp.int32, (window, TILE), 1) // 2 + EDGE)
    for r in range(rows):
        at = r * SIZES
        for t in range(tiles):
            lanes = slice(t * TILE, (t + 1) * TILE)
            matrix = jnp.zeros((window, TILE), F32)
            for d in range(-2, 3):
                matrix = jnp.where(diagonal == d, mix[d + 2][at : at + 1, lanes], matrix)
            high, low = split2(matrix)
            matrix_s[r * tiles + t, 0:window] = high.astype(BF16)
            matrix_s[r * tiles + t, window : 2 * window] = low.astype(BF16)

    late_hidden()
    band_products(rows, length, cot_s, hidden_s, band_s, window, diagonal)
    even1 = (lax.broadcasted_iota(jnp.int32, (1, length), 1) & 1) == 0
    band = [[lane_rows(band_s, d + 2, r, length) for d in range(-2, 3)] for r in range(rows)]

    def product(o):
        return spread(
            [jnp.where(even1, band[r][DELTA_EVEN[o] + 2], band[r][DELTA_ODD[o] + 2]) for r in range(rows)], length
        )

    gathered = real * product(0)
    for o in OFFSETS:
        gathered = gathered + member[o] * shift(product(-o), o)
    weight_grad = pair_weight * inverse * gathered
    cal_grad = weight * (weight_grad - group_all(weight * weight_grad, jnp.add, bits))
    cal_grad = cal_grad - scale() * real * weight * (log_weight + entropy)
    inner = group_all(cal * cal_grad, jnp.add, bits)
    score_grad = jnp.concatenate(
        [calibrate_back(r, length, scores, cal_grad, inner, kept[r][0], kept[r][1], probs_s) for r in range(rows)],
        axis=0,
    )
    score_grad = score_grad * inverse
    q_grad = score_grad
    for o in OFFSETS:
        q_grad = q_grad + same[o] * shift(score_grad, o)
    q_grad = group_all(q_grad * real, jnp.add, bits)

    scorer16 = jnp.concatenate([scorer, scorer, jnp.zeros((EDGE - 2, width), BF16)], axis=0)
    for r in range(rows):
        at = r * SIZES
        q_high, q_low = split2(q_grad[at : at + 1])
        for t in range(tiles):
            lanes = slice(t * TILE, (t + 1) * TILE)
            all_lanes = slice(r * length + t * TILE, r * length + (t + 1) * TILE)
            first = t * TILE // 2
            matrix_s[r * tiles + t, 2 * window :] = jnp.concatenate(
                [q_high[:, lanes], q_low[:, lanes], jnp.zeros((EDGE - 2, TILE), F32)], axis=0
            ).astype(BF16)
            here = cot_s[r, first : first + window, :]
            given = jnp.concatenate([here, here, scorer16], axis=0)
            hgrad_s[all_lanes, :] = lax.dot_general(
                matrix_s[r * tiles + t], given, (((0,), (0,)), ((), ())), preferred_element_type=F32
            ).astype(BF16)

    def pool():
        for r in range(rows):
            for t in range(tiles):
                first = t * TILE // 2
                out = lax.dot_general(
                    matrix_s[r * tiles + t],
                    hidden_s[:, r * length + t * TILE : r * length + (t + 1) * TILE],
                    (((1,), (1,)), ((), ())),
                    preferred_element_type=F32,
                )
                pooled_s[r, first : first + window, :] += out[:window] + out[window : 2 * window]
                part_ref[0:1, :] += out[2 * window : 2 * window + 1] + out[2 * window + 1 : 2 * window + 2]
            blocks_ref[r] = pooled_s[r, EDGE : EDGE + half, :].astype(BF16)

    return pool


def fill_cotangent(rows, half, width, cot_ref, cot_s):
    cot_s[:, 0:EDGE, :] = jnp.zeros((rows, EDGE, width), BF16)
    cot_s[:, EDGE + half :, :] = jnp.zeros((rows, EDGE, width), BF16)
    for r in range(rows):
        cot_s[r, EDGE : EDGE + half, :] = cot_ref[r]


def fill_q(count, tq16, const, onehot_s, q_s):
    def step(t, carry):
        lanes = pl.ds(pl.multiple_of(t * TILE, TILE), TILE)
        got = jnp.dot(tq16, onehot_s[:, lanes], preferred_element_type=F32)
        q_s[0:1, lanes] = got[0:1] + got[1:2] + got[2:3] + const
        return carry

    lax.fori_loop(0, count, step, 0)


def fill_hidden(count, table, bias_column, onehot_s, hidden_s):
    def step(t, carry):
        lanes = pl.ds(pl.multiple_of(t * TILE, TILE), TILE)
        got = jnp.dot(table(), onehot_s[:, lanes], preferred_element_type=F32)
        hidden_s[:, lanes] = (got + bias_column).astype(BF16)
        return carry

    lax.fori_loop(0, count, step, 0)


def local_scratch(rows, length, width, vocab):
    half = length // 2
    return [
        pltpu.VMEM((8, rows * length), jnp.int32),
        pltpu.VMEM((TAPS * vocab, rows * length), BF16),
        pltpu.VMEM((width, rows * length), BF16),
        pltpu.VMEM((8, rows * length), F32),
        pltpu.VMEM((rows, length, length), BF16),
        pltpu.VMEM((length, TILE), F32),
        pltpu.VMEM((rows, half + 2 * EDGE, width), BF16),
        pltpu.VMEM((8, rows * length), F32),
        pltpu.VMEM((rows, half + 2 * EDGE, width), F32),
        pltpu.VMEM((rows * length, width), BF16),
        pltpu.VMEM((rows * (length // TILE), TILE + 5 * EDGE, TILE), BF16),
    ]


def main_kernel(
    dims, len_ref, aux_ref, small_ref, ids_ref, mask_ref, table_ref, tq_ref, bias_ref, scorer_ref, cot_ref,
    blocks_ref, grad_ref, part_ref,
    taps_s, onehot_s, hidden_s, q_s, probs_s, similar_s, cot_s, band_s, pooled_s, hgrad_s, matrix_s,
):
    rows, length, width, vocab = dims
    count = rows * (length // TILE)
    seg_list, real_list = row_masks(rows, length, len_ref, ids_ref, mask_ref, taps_s)
    fill_cotangent(rows, length // 2, width, cot_ref, cot_s)
    fill_onehot(count, vocab, taps_s, onehot_s)
    m = members_of(rows, length, seg_list, real_list)
    fill_q(count, tq_ref[...], small_ref[1:2, 0:1], onehot_s, q_s)
    scores = block_scores(rows, length, m, q_s)

    def late_hidden():
        fill_hidden(count, lambda: table_ref[...], bias_ref[...], onehot_s, hidden_s)

    def scale():
        return aux_ref[0, 0] / small_ref[0:1, 0:1]

    refs = (hidden_s, cot_s, band_s, pooled_s, hgrad_s, probs_s, similar_s, blocks_ref, part_ref, matrix_s, late_hidden)
    pool = middle(dims, m, scores, seg_list, real_list, scale, scorer_ref[...], refs, lambda r, t: None)
    pool()

    def grad_step(k, carry):
        symbols = pl.ds(pl.multiple_of(k * vocab, vocab), vocab)
        for c in range(width // TILE):
            cols = slice(c * TILE, (c + 1) * TILE)
            grad_ref[symbols, cols] = jnp.dot(
                onehot_s[symbols, :], hgrad_s[:, cols], preferred_element_type=F32
            )
        return carry

    lax.fori_loop(0, TAPS, grad_step, 0)


def main_call(lengths, aux, small, ids, mask, table, tq, bias, scorer, cot):
    rows, length = ids.shape
    width = cot.shape[2]
    vocab = table.shape[1] // TAPS
    dims = (rows, length, width, vocab)
    vmem = pl.BlockSpec(memory_space=pltpu.VMEM)
    smem = pl.BlockSpec(memory_space=pltpu.SMEM)
    half = length // 2
    return pl.pallas_call(
        functools.partial(main_kernel, dims),
        out_shape=(
            jax.ShapeDtypeStruct((rows, half, width), BF16),
            jax.ShapeDtypeStruct((TAPS * vocab, width), F32),
            jax.ShapeDtypeStruct((8, width), F32),
        ),
        in_specs=[smem, smem] + [vmem] * 8,
        out_specs=(vmem, vmem, vmem),
        scratch_shapes=local_scratch(rows, length, width, vocab),
        compiler_params=pltpu.CompilerParams(vmem_limit_bytes=60 * 1024 * 1024),
        name="latent",
    )(lengths, aux, small, ids, mask, table, tq, bias, scorer, cot)


MESH = pl.DeviceIdType.MESH
ALL = slice(None)


def split3(x):
    a = x.astype(BF16).astype(F32)
    b = (x - a).astype(BF16).astype(F32)
    return a, b, x - a - b


def remote(src, dst, send, recv, device):
    return pltpu.make_async_remote_copy(
        src_ref=src, dst_ref=dst, send_sem=send, recv_sem=recv, device_id=device, device_id_type=MESH
    )


def device_at(c, x, y, z):
    return (z * 2 + y, x * 2 + c)


class Gather:
    def __init__(self, buf, me, send, recv, chunks):
        self.buf, self.me, self.send, self.recv, self.chunks = buf, me, send, recv, chunks
        self.rows = buf.shape[4] // chunks
        self.copies = {}

    def part(self, c, x, y, z, chunk, half=None):
        if half is None:
            return self.buf.at[c, x, y, z, pl.ds(chunk * self.rows, self.rows)]
        return self.buf.at[c, x, y, z, pl.ds(chunk * self.rows + half * (self.rows // 2), self.rows // 2)]

    def go(self, chunk, n, ref, device):
        at = chunk * 11 + n
        copy = remote(ref, ref, self.send.at[at], self.recv.at[at], device)
        copy.start()
        self.copies[chunk, n] = copy

    def along_z(self, chunk):
        c, x, y, z = self.me
        for i in range(1, 4):
            self.go(chunk, i - 1, self.part(c, x, y, z, chunk), device_at(c, x, y, lax.rem(z + i, 4)))

    def across(self, chunk, step):
        c, x, y, z = self.me
        copies = self.copies
        core, over_x, over_y = device_at(1 - c, x, y, z), device_at(c, 1 - x, y, z), device_at(c, x, 1 - y, z)
        if step == 0:
            for n in range(3):
                copies[chunk, n].wait_recv()
            mine = self.part(c, x, y, ALL, chunk)
            self.go(chunk, 3, mine, over_x)
            self.go(chunk, 4, mine, over_y)
            self.go(chunk, 5, mine, core)
        elif step == 1:
            copies[chunk, 3].wait_recv()
            self.go(chunk, 6, self.part(c, 1 - x, y, ALL, chunk, 0), over_y)
            self.go(chunk, 7, self.part(c, 1 - x, y, ALL, chunk), core)
            copies[chunk, 4].wait_recv()
            self.go(chunk, 8, self.part(c, x, 1 - y, ALL, chunk, 1), over_x)
            self.go(chunk, 9, self.part(c, x, 1 - y, ALL, chunk), core)
        else:
            copies[chunk, 6].wait_recv()
            copies[chunk, 8].wait_recv()
            self.go(chunk, 10, self.part(c, 1 - x, 1 - y, ALL, chunk), core)

    def arrived(self, chunk):
        for n in (5, 7, 9, 10):
            self.copies[chunk, n].wait_recv()

    def drain(self):
        for copy in self.copies.values():
            copy.wait_send()


def place_of(slot, taps, per_tap):
    slot = jnp.minimum(slot, taps * per_tap - 1)
    tap = slot // per_tap
    return tap, slot - tap * per_tap


def static_place(tap, column, per_tap):
    slot = tap * per_tap + column
    return slot // 16, slot // 8 % 2, slot // 4 % 2, slot % 4


def step_kernel(
    dims,
    len_in, aux_in, ids_in, mask_in, emb_ref, conv_ref, bias_in, scorer_in, cot_ref,
    blocks_ref, final_ref, sums_out,
    taps_s, onehot_s, hidden_s, q_s, probs_s, similar_s, cot_s, band_s, pooled_s, hgrad_s, matrix_s,
    blocks_s, part_s, conv_s, emb_s,
    small_s, smalls_s, wcol_s, emball_s, tq_s, tqs_s, count_s, table_s,
    give_s, take_s, own_s, hold_s, pass_s, came_s, zgive_s, zown_s, zcame_s, final_s, sums_s, sumr_s,
    local_sem, start_send, start_recv, half_sem, gather_send, gather_recv,
    core_send, core_recv, quad_send, quad_recv, line_send, line_recv, sum_send, sum_recv,
    len_ref, aux_ref, ids_ref, mask_ref, bias_ref, scorer_ref, sums_ref, in_sem,
):
    rows, length, width, vocab, size, fs = dims
    half = length // 2
    count = rows * (length // TILE)
    per_tap = width // 128
    f, d = lax.axis_index("fsdp"), lax.axis_index("dp")
    z, y = f // 2, lax.rem(f, 2)
    x, c = d // 2, lax.rem(d, 2)
    me = (c, x, y, z)
    core = device_at(1 - c, x, y, z)

    barrier = pltpu.get_barrier_semaphore()
    peers = [(lax.rem(f + i, fs), d) for i in range(1, fs)]
    others = [core, device_at(c, 1 - x, y, z), device_at(c, 1 - x, 1 - y, z)]
    for peer in peers + others:
        pl.semaphore_signal(barrier, inc=1, device_id=peer, device_id_type=MESH)

    inputs = [
        pltpu.make_async_copy(source, target, in_sem.at[n])
        for n, (source, target) in enumerate(
            [
                (len_in, len_ref),
                (ids_in, ids_ref),
                (mask_in, mask_ref),
                (bias_in, bias_ref),
                (scorer_in, scorer_ref),
                (aux_in, aux_ref),
            ]
        )
    ]
    for copy in inputs:
        copy.start()
    mid = vocab // 2
    my_half = pl.ds(pl.multiple_of(c * mid, mid), mid)
    my_rows = pl.ds(pl.multiple_of(x * (size // 2), size // 2), size // 2)
    my_tap, my_column = place_of(((c * 2 + x) * 2 + y) * 4 + z, TAPS, per_tap)
    local = [
        pltpu.make_async_copy(conv_ref, conv_s, local_sem.at[0]),
        pltpu.make_async_copy(emb_ref, emb_s, local_sem.at[1]),
        pltpu.make_async_copy(
            conv_ref.at[my_tap, :, pl.ds(pl.multiple_of(my_column * 128, 128), 128)], wcol_s.at[f], local_sem.at[2]
        ),
        pltpu.make_async_copy(emb_ref.at[my_rows, my_half], emball_s.at[f, my_rows, my_half], local_sem.at[3]),
    ]
    for r in range(rows):
        local.append(pltpu.make_async_copy(cot_ref.at[r], cot_s.at[r, pl.ds(EDGE, half)], local_sem.at[4 + r]))
    for copy in local:
        copy.start()
    for copy in inputs:
        copy.wait()
    real_here = jnp.sum(jnp.sum(mask_ref[...].astype(F32), axis=1, keepdims=True), axis=0, keepdims=True)
    small_s[...] = jnp.zeros_like(small_s)
    small_s[0:1, 0:size] = bias_ref[...].astype(F32)
    small_s[1:2, 0:size] = scorer_ref[...].astype(F32)
    small_s[2:3, :] = jnp.broadcast_to(real_here, (1, 128))
    smalls_s[f] = small_s[...]
    seg_list, real_list = row_masks(rows, length, len_ref, ids_ref, mask_ref, taps_s)

    pl.semaphore_wait(barrier, fs - 1 + 3)
    starts = []
    for i, peer in enumerate(peers):
        starts.append(remote(small_s, smalls_s.at[f], start_send.at[0, i], start_recv.at[0, i], peer))
        starts[-1].start()
    for i, peer in enumerate(peers):
        mine = emb_ref.at[my_rows, my_half]
        starts.append(
            remote(mine, emball_s.at[f, my_rows, my_half], start_send.at[1, i], start_recv.at[1, i], peer)
        )
        starts[-1].start()
    for i, peer in enumerate(peers):
        tap, column = place_of(((c * 2 + x) * 2 + lax.rem(peer[0], 2)) * 4 + peer[0] // 2, TAPS, per_tap)
        mine = conv_ref.at[tap, :, pl.ds(pl.multiple_of(column * 128, 128), 128)]
        starts.append(remote(mine, wcol_s.at[f], start_send.at[2, i], start_recv.at[2, i], peer))
        starts[-1].start()

    fill_onehot(count, vocab, taps_s, onehot_s)
    cot_s[:, 0:EDGE, :] = jnp.zeros((rows, EDGE, width), BF16)
    cot_s[:, EDGE + half :, :] = jnp.zeros((rows, EDGE, width), BF16)

    for copy in local[2:4]:
        copy.wait()
    for i in range(fs - 1):
        starts[fs - 1 + i].wait_recv()
    mine = emball_s.at[:, my_rows, my_half]
    emb_x = remote(mine, mine, half_sem.at[6], half_sem.at[7], device_at(c, 1 - x, y, z))
    emb_x.start()

    for i in range(fs - 1):
        starts[i].wait_recv()
    line = jnp.zeros((16, width), F32)
    real_sum = jnp.zeros((1, 1), F32)
    lane = lax.broadcasted_iota(jnp.int32, (128, width), 0)
    at = lax.broadcasted_iota(jnp.int32, (128, width), 1)
    for g in range(fs):
        pick = jnp.where((at == lane + g * size) & (lane < size), 1.0, 0.0).astype(BF16)
        both = jnp.concatenate([smalls_s[g], jnp.zeros((8, 128), F32)], axis=0)
        keep = lax.broadcasted_iota(jnp.int32, (16, 128), 0) < 2
        line = line + jnp.dot(jnp.where(keep, both, 0.0).astype(BF16), pick, preferred_element_type=F32)
        real_sum = real_sum + smalls_s[g][2:3, 0:1]
    count_s[0] = jnp.broadcast_to(real_sum, (8, 128))
    count_x = remote(
        count_s.at[0], count_s.at[1], half_sem.at[0], half_sem.at[1], device_at(c, 1 - x, y, z)
    )
    count_x.start()
    line16 = line.astype(BF16)
    bias_column = jnp.concatenate([line, jnp.zeros((112, width), F32)], axis=0).T[:, 0:1]
    const = jnp.sum(line[0:1] * line[1:2], axis=1, keepdims=True)
    scorer = line16[1:2]
    local[0].wait()
    local[1].wait()
    across = (((1,), (1,)), ((), ()))
    u = jnp.concatenate(
        [
            lax.dot_general(line16, conv_s[k], across, preferred_element_type=F32)[1:2]
            for k in range(TAPS)
        ],
        axis=0,
    )
    u = jnp.concatenate(list(split3(u)) + [jnp.zeros((1, size), F32)], axis=0).astype(BF16)
    tq = jnp.dot(u, emb_s[...], preferred_element_type=F32)
    tq_s[...] = jnp.zeros_like(tq_s)
    tq_s[0:TAPS, :] = tq[0:TAPS] + tq[TAPS : 2 * TAPS] + tq[2 * TAPS : 3 * TAPS]
    tqs_s[f] = tq_s[...]
    tq_copies = []
    for i, peer in enumerate(peers):
        copy = remote(tq_s, tqs_s.at[f], start_send.at[3, i], start_recv.at[3, i], peer)
        copy.start()
        tq_copies.append(copy)

    emb_x.wait_recv()
    mine = emball_s.at[:, :, my_half]
    emb_core = remote(mine, mine, half_sem.at[2], half_sem.at[3], core)
    emb_core.start()
    for i in range(fs - 1):
        starts[2 * (fs - 1) + i].wait_recv()
    emb_core.wait_recv()
    block = lax.dot_general(
        wcol_s[...].reshape(fs * size, 128),
        emball_s[...].reshape(fs * size, vocab),
        (((0,), (0,)), ((), ())),
        preferred_element_type=F32,
    )
    table_s[c, x, y, z] = block.astype(BF16)
    tables = Gather(table_s, me, gather_send.at[0], gather_recv.at[0], TABLE_CHUNKS)
    for chunk in range(TABLE_CHUNKS):
        tables.along_z(chunk)

    count_x.wait_recv()
    count_s[2] = count_s[0] + count_s[1]
    count_c = remote(count_s.at[2], count_s.at[3], half_sem.at[4], half_sem.at[5], core)
    count_c.start()

    m = members_of(rows, length, seg_list, real_list)
    for copy in tq_copies:
        copy.wait_recv()
    tq = tqs_s[0]
    for g in range(1, fs):
        tq = tq + tqs_s[g]
    tq16 = jnp.concatenate(
        [
            jnp.concatenate(list(split3(tq[k : k + 1])) + [jnp.zeros((13, vocab), F32)], axis=0)
            for k in range(TAPS)
        ],
        axis=1,
    ).astype(BF16)
    fill_q(count, tq16, const, onehot_s, q_s)
    scores = block_scores(rows, length, m, q_s)

    part = 128 // TABLE_CHUNKS

    def table_rows(chunk):
        return jnp.concatenate(
            [
                jnp.concatenate(
                    [
                        table_s[(*static_place(k, j, per_tap), slice(chunk * part, (chunk + 1) * part))]
                        for j in range(per_tap)
                    ],
                    axis=0,
                )
                for k in range(TAPS)
            ],
            axis=1,
        )

    def hidden_part(chunk, low, high):
        if low == 0 and chunk < TABLE_CHUNKS - 1:
            tables.arrived(chunk)
        bias_part = jnp.concatenate(
            [bias_column[j * 128 + chunk * part : j * 128 + (chunk + 1) * part] for j in range(per_tap)], axis=0
        )

        def step(t, carry):
            lanes = pl.ds(pl.multiple_of(t * TILE, TILE), TILE)
            got = jnp.dot(table_rows(chunk), onehot_s[:, lanes], preferred_element_type=F32)
            got = (got + bias_part).astype(BF16)
            for j in range(per_tap):
                hidden_s[j * 128 + chunk * part : j * 128 + (chunk + 1) * part, lanes] = got[
                    j * part : (j + 1) * part
                ]
            return carry

        for t in range(count * low // 4, count * high // 4):
            step(t, 0)

    order = [(0, 0), (1, 0), (0, 1), (1, 1), (0, 2), (0, 0, 2), (1, 2), (0, 2, 4), (1, 0, 4)]
    steps = [
        functools.partial(tables.across if len(n) == 2 else hidden_part, *n) for n in order
    ]
    turns = {(0, 1): 1, (0, 3): 1, (1, 1): 1, (1, 3): 1}

    def between(r, t):
        for _ in range(turns.get((r, t), 0)):
            steps.pop(0)()

    def late_hidden():
        while len(steps) > 1:
            steps.pop(0)()
        tables.arrived(TABLE_CHUNKS - 1)
        tables.drain()
        for copy in local[4:]:
            copy.wait()
        count_c.wait_recv()
        steps.pop(0)()

    def scale():
        return aux_ref[0, 0] / (count_s[2][0:1, 0:1] + count_s[3][0:1, 0:1])

    refs = (hidden_s, cot_s, band_s, pooled_s, hgrad_s, probs_s, similar_s, blocks_s, part_s, matrix_s, late_hidden)
    pool = middle(dims[:4], m, scores, seg_list, real_list, scale, scorer, refs, between)
    def product(slot):
        tap, column = place_of(jnp.minimum(slot, TAPS * per_tap - 2), TAPS, per_tap)
        symbols = pl.ds(pl.multiple_of(tap * vocab, vocab), vocab)
        lanes = pl.ds(pl.multiple_of(column * 128, 256), 256)
        return jnp.dot(onehot_s[symbols, :], hgrad_s[:, lanes], preferred_element_type=F32)

    def core_copy(p):
        return remote(give_s.at[p], take_s.at[p], core_send.at[p], core_recv.at[p], core)

    def pair_of(q, n):
        return lax.rem(x + q // 2, 2) * 4 + lax.rem(y + q % 2, 2) * 2 + n

    def give(q, n):
        p = pair_of(q, n)
        give_s[p] = product((1 - c) * 16 + 2 * p)
        core_copy(p).start()

    def keep(q, n):
        p = pair_of(q, n)
        got = product(c * 16 + 2 * p)
        core_copy(p).wait_recv()
        return got + take_s[p]

    gap = vocab // 2
    over_x, over_y = device_at(c, 1 - x, y, z), device_at(c, x, 1 - y, z)

    def quad_copy(q, n, part):
        at = (3 - q) * 2 + n
        ref = at, pl.ds(part * gap, gap)
        to = over_x if q == 2 or (q == 3 and part == 0) else over_y
        return remote(pass_s.at[ref], came_s.at[ref], quad_send.at[at * 2 + part], quad_recv.at[at * 2 + part], to)

    parts = [slice(0, gap), slice(gap, 2 * gap)]
    def across(n):
        pass_s[n] = keep(3, n).astype(BF16)
        quad_copy(3, n, 0).start()
        quad_copy(3, n, 1).start()

    def beside(q, n):
        got = keep(q, n)
        plain = 2 - q
        pass_s[(3 - q) * 2 + n, parts[plain]] = got[parts[plain]].astype(BF16)
        quad_copy(q, n, plain).start()
        hold_s[2 - q, n] = got[parts[1 - plain]]

    def mixed(q, n):
        part = q - 1
        quad_copy(3, n, part).wait_recv()
        pass_s[(3 - q) * 2 + n, parts[part]] = (
            hold_s[2 - q, n] + came_s[n, parts[part]].astype(F32)
        ).astype(BF16)
        quad_copy(q, n, part).start()

    give(3, 0)
    give(3, 1)
    give(2, 0)
    give(1, 0)
    across(0)
    across(1)
    beside(2, 0)
    beside(1, 0)
    give(2, 1)
    give(1, 1)
    mixed(1, 0)
    mixed(2, 0)
    give(0, 0)
    beside(2, 1)
    beside(1, 1)
    mixed(1, 1)
    mixed(2, 1)
    give(0, 1)
    own_s[0] = keep(0, 0)
    own_s[1] = keep(0, 1)

    pool()
    blocks_out = pltpu.make_async_copy(blocks_s, blocks_ref, local_sem.at[4])
    blocks_out.start()
    sums_s[0] = part_s[...]
    sum_copies = [remote(sums_s.at[0], sumr_s.at[0], sum_send.at[0], sum_recv.at[0], core)]
    sum_copies[0].start()

    def sums_quad():
        sum_copies[0].wait_recv()
        sums_s[1] = sums_s[0] + sumr_s[0]
        quad = [device_at(c, lax.rem(x + q // 2, 2), lax.rem(y + q % 2, 2), z) for q in range(4)]
        for q in range(1, 4):
            sum_copies.append(remote(sums_s.at[1], sumr_s.at[q], sum_send.at[q], sum_recv.at[q], quad[q]))
            sum_copies[-1].start()

    def sums_line():
        for q in range(1, 4):
            sum_copies[q].wait_recv()
        sums_s[2] = (sums_s[1] + sumr_s[1]) + (sumr_s[2] + sumr_s[3])
        for i in range(1, 4):
            to = device_at(c, x, y, lax.rem(z + i, 4))
            sum_copies.append(remote(sums_s.at[2], sumr_s.at[3 + i], sum_send.at[3 + i], sum_recv.at[3 + i], to))
            sum_copies[-1].start()

    grads = Gather(final_s, me, gather_send.at[1], gather_recv.at[1], GRAD_CHUNKS)
    line_copies = {}

    def to_line(chunk):
        part = slice(chunk * gap, (chunk + 1) * gap)
        for q in (2, 1):
            for n in range(2):
                quad_copy(q, n, chunk).wait_recv()
        for t in range(2):
            total = own_s[t, part] + (came_s[2 + t, part].astype(F32) + came_s[4 + t, part].astype(F32))
            for j in range(2):
                zown_s[2 * t + j, part] = total[:, j * 128 : (j + 1) * 128]
                zgive_s[2 * t + j, part] = total[:, j * 128 : (j + 1) * 128].astype(BF16)
        for i in range(1, 4):
            to = lax.rem(z + i, 4)
            at = chunk * 3 + i - 1
            part = pl.ds(chunk * gap, gap)
            copy = remote(
                zgive_s.at[to, part],
                zcame_s.at[i - 1, part],
                line_send.at[at],
                line_recv.at[at],
                device_at(c, x, y, to),
            )
            copy.start()
            line_copies[chunk, i] = copy

    def from_line(chunk):
        part = slice(chunk * gap, (chunk + 1) * gap)
        total = zown_s[z, part]
        for i in range(1, 4):
            line_copies[chunk, i].wait_recv()
            total = total + zcame_s[i - 1, part].astype(F32)
        final_s[c, x, y, z, part] = total.astype(BF16)
        grads.along_z(chunk)

    def put(chunk, side):
        part = pl.ds(chunk * gap, gap)
        ref = side, ALL, ALL, ALL, part
        at = local_sem.at[2 * chunk + (0 if side is c else 1)]
        out_copies.append(pltpu.make_async_copy(final_s.at[ref], final_ref.at[ref], at))
        out_copies[-1].start()

    out_copies = []
    to_line(0)
    to_line(1)
    from_line(0)
    from_line(1)
    sums_quad()
    grads.across(0, 0)
    sums_line()
    grads.across(1, 0)
    grads.across(0, 1)
    grads.across(1, 1)
    grads.across(0, 2)
    put(0, c)
    grads.across(1, 2)
    put(1, c)
    grads.arrived(0)
    put(0, 1 - c)
    grads.arrived(1)
    put(1, 1 - c)
    grads.drain()

    for i in range(4, 7):
        sum_copies[i].wait_recv()
    sums = (sums_s[2] + sumr_s[4]) + (sumr_s[5] + sumr_s[6])
    total_count = count_s[2][0:1, 0:1] + count_s[3][0:1, 0:1]
    sums_ref[...] = jnp.concatenate([sums[0:1], sums[1:2] / total_count, sums[2:8]], axis=0)
    out_copies.append(pltpu.make_async_copy(sums_ref, sums_out, in_sem.at[0]))
    out_copies[-1].start()

    for copy in starts + tq_copies + sum_copies + list(line_copies.values()) + [count_x, count_c, emb_x, emb_core]:
        copy.wait_send()
    for p in range(8):
        core_copy(p).wait_send()
    for chunk in range(GRAD_CHUNKS):
        for q in (3, 2, 1):
            for n in range(2):
                quad_copy(q, n, chunk).wait_send()
    for copy in out_copies + [blocks_out]:
        copy.wait()


def last_kernel(
    dims, blocks_ref, final_ref, sums_in, emb_ref, conv_ref,
    out_ref, loss_out, embg_out, convg_ref, biasg_out, scoreg_out,
    blocks_s, final_s, emb_s, conv_s, convg_s, in_sem, out_sem,
    sums_ref, loss_ref, embg_ref, biasg_ref, scoreg_ref,
):
    rows, length, width, vocab, size, fs = dims
    per_tap = width // 128
    copies = [
        pltpu.make_async_copy(emb_ref, emb_s, in_sem.at[0]),
        pltpu.make_async_copy(conv_ref, conv_s, in_sem.at[1]),
    ]
    for n in range(4):
        copies.append(
            pltpu.make_async_copy(final_ref.at[n // 2, n % 2], final_s.at[n // 2, n % 2], in_sem.at[2 + n])
        )
    blocks = [pltpu.make_async_copy(blocks_ref.at[r], blocks_s.at[r], in_sem.at[6 + r]) for r in range(rows)]
    copies.append(pltpu.make_async_copy(sums_in, sums_ref, in_sem.at[6 + rows]))
    for copy in copies + blocks:
        copy.start()
    outs = []
    have = 0
    copies[0].wait()
    copies[1].wait()
    emb_total = None
    for k in range(TAPS):
        while have * 8 < (k + 1) * per_tap:
            copies[2 + have].wait()
            have += 1
        grad = jnp.concatenate([final_s[static_place(k, j, per_tap)] for j in range(per_tap)], axis=1)
        convg_s[k] = jnp.dot(emb_s[...], grad, preferred_element_type=F32)
        outs.append(pltpu.make_async_copy(convg_s.at[k], convg_ref.at[k], out_sem.at[k]))
        outs[-1].start()
        term = lax.dot_general(conv_s[k], grad, (((1,), (1,)), ((), ())), preferred_element_type=F32)
        emb_total = term if emb_total is None else emb_total + term
        if k == TAPS // 2:
            bias_line = jnp.sum(grad.astype(F32), axis=0, keepdims=True)
        if k < rows:
            blocks[k].wait()
            outs.append(pltpu.make_async_copy(blocks_s.at[k], out_ref.at[k], out_sem.at[TAPS + k]))
            outs[-1].start()
    embg_ref[...] = emb_total
    copies[6].wait()
    f = lax.axis_index("fsdp")
    lane = lax.broadcasted_iota(jnp.int32, (128, width), 0)
    at = lax.broadcasted_iota(jnp.int32, (128, width), 1)
    pick = jnp.where((at == lane + f * size) & (lane < size), 1.0, 0.0).astype(BF16)
    lines = jnp.concatenate(
        list(split3(bias_line)) + list(split3(sums_ref[0:1])) + [jnp.zeros((10, width), F32)], axis=0
    ).astype(BF16)
    mine = lax.dot_general(lines, pick, (((1,), (1,)), ((), ())), preferred_element_type=F32)
    biasg_ref[...] = (mine[0:1] + mine[1:2] + mine[2:3])[:, :size]
    scoreg_ref[...] = (mine[3:4] + mine[4:5] + mine[5:6])[:, :size]
    loss_ref[...] = sums_ref[1:2, 0:1]
    for n, (source, target) in enumerate(
        [(embg_ref, embg_out), (biasg_ref, biasg_out), (scoreg_ref, scoreg_out), (loss_ref, loss_out)]
    ):
        outs.append(pltpu.make_async_copy(source, target, out_sem.at[TAPS + rows + n]))
        outs[-1].start()
    while have < 4:
        copies[2 + have].wait()
        have += 1
    for copy in outs:
        copy.wait()


def step_shards(byte_ids, doc_lengths, pad_mask, embedding, conv_weight, conv_bias, scorer, cotangent, aux_weight):
    rows, length = byte_ids.shape
    vocab, size = embedding.shape
    width = conv_weight.shape[2]
    half = length // 2
    fs = width // size
    dims = (rows, length, width, vocab, size, fs)
    hbm = pl.BlockSpec(memory_space=pl.ANY)
    dma = pltpu.SemaphoreType.DMA
    blocks, final, sums = pl.pallas_call(
        functools.partial(step_kernel, dims),
        out_shape=(
            jax.ShapeDtypeStruct((rows, half, width), BF16),
            jax.ShapeDtypeStruct((2, 2, 2, 4, vocab, 128), BF16),
            jax.ShapeDtypeStruct((8, width), F32),
        ),
        in_specs=[hbm] * 9,
        out_specs=(hbm, hbm, hbm),
        scratch_shapes=local_scratch(rows, length, width, vocab)
        + [
            pltpu.VMEM((rows, half, width), BF16),
            pltpu.VMEM((8, width), F32),
            pltpu.VMEM((TAPS, size, width), BF16),
            pltpu.VMEM((size, vocab), BF16),
            pltpu.VMEM((8, 128), F32),
            pltpu.VMEM((fs, 8, 128), F32),
            pltpu.VMEM((fs, size, 128), BF16),
            pltpu.VMEM((fs, size, vocab), BF16),
            pltpu.VMEM((8, vocab), F32),
            pltpu.VMEM((fs, 8, vocab), F32),
            pltpu.VMEM((4, 8, 128), F32),
            pltpu.VMEM((2, 2, 2, 4, 128, vocab), BF16),
            pltpu.VMEM((8, vocab, 256), F32),
            pltpu.VMEM((8, vocab, 256), F32),
            pltpu.VMEM((2, vocab, 256), F32),
            pltpu.VMEM((2, 2, vocab // 2, 256), F32),
            pltpu.VMEM((6, vocab, 256), BF16),
            pltpu.VMEM((6, vocab, 256), BF16),
            pltpu.VMEM((4, vocab, 128), BF16),
            pltpu.VMEM((4, vocab, 128), F32),
            pltpu.VMEM((3, vocab, 128), BF16),
            pltpu.VMEM((2, 2, 2, 4, vocab, 128), BF16),
            pltpu.VMEM((3, 8, width), F32),
            pltpu.VMEM((7, 8, width), F32),
            dma((4 + max(rows, 2),)),
            dma((4, fs - 1)),
            dma((4, fs - 1)),
            dma((8,)),
            dma((2, 11 * max(TABLE_CHUNKS, GRAD_CHUNKS))),
            dma((2, 11 * max(TABLE_CHUNKS, GRAD_CHUNKS))),
            dma((8,)),
            dma((8,)),
            dma((12,)),
            dma((12,)),
            dma((3 * GRAD_CHUNKS,)),
            dma((3 * GRAD_CHUNKS,)),
            dma((7,)),
            dma((7,)),
            pltpu.SMEM(doc_lengths.shape, jnp.int32),
            pltpu.SMEM((1, 1), F32),
            pltpu.VMEM((rows, length), jnp.int32),
            pltpu.VMEM((rows, length), jnp.int32),
            pltpu.VMEM((1, size), BF16),
            pltpu.VMEM((1, size), BF16),
            pltpu.VMEM((8, width), F32),
            dma((6,)),
        ],
        compiler_params=pltpu.CompilerParams(
            collective_id=0, has_side_effects=True, vmem_limit_bytes=62 * 1024 * 1024
        ),
        name="step",
    )(
        doc_lengths,
        aux_weight.reshape(1, 1),
        byte_ids,
        pad_mask,
        embedding.T,
        conv_weight,
        conv_bias.reshape(1, size),
        scorer.reshape(1, size),
        cotangent,
    )
    blocks, loss, emb_grad, conv_grad, bias_grad, score_grad = pl.pallas_call(
        functools.partial(last_kernel, dims),
        out_shape=(
            jax.ShapeDtypeStruct((rows, half, width), BF16),
            jax.ShapeDtypeStruct((1, 1), F32),
            jax.ShapeDtypeStruct((size, vocab), F32),
            jax.ShapeDtypeStruct((TAPS, size, width), F32),
            jax.ShapeDtypeStruct((1, size), F32),
            jax.ShapeDtypeStruct((1, size), F32),
        ),
        in_specs=[hbm] * 5,
        out_specs=(hbm,) * 6,
        scratch_shapes=[
            pltpu.VMEM((rows, half, width), BF16),
            pltpu.VMEM((2, 2, 2, 4, vocab, 128), BF16),
            pltpu.VMEM((size, vocab), BF16),
            pltpu.VMEM((TAPS, size, width), BF16),
            pltpu.VMEM((TAPS, size, width), F32),
            dma((7 + rows,)),
            dma((rows + TAPS + 4,)),
            pltpu.VMEM((8, width), F32),
            pltpu.VMEM((1, 1), F32),
            pltpu.VMEM((size, vocab), F32),
            pltpu.VMEM((1, size), F32),
            pltpu.VMEM((1, size), F32),
        ],
        compiler_params=pltpu.CompilerParams(vmem_limit_bytes=62 * 1024 * 1024),
        name="last",
    )(blocks, final, sums, embedding.T, conv_weight)
    return blocks, loss.reshape(()), emb_grad.T, conv_grad, bias_grad.reshape(size), score_grad.reshape(size)


def split3_rows(x):
    a = lax.reduce_precision(x, 8, 7)
    b = lax.reduce_precision(x - a, 8, 7)
    return jnp.concatenate([a, b, x - a - b], axis=0).astype(BF16)


def gathered_shards(byte_ids, doc_lengths, pad_mask, embedding, conv_weight, conv_bias, scorer, cotangent, aux_weight):
    emb = lax.all_gather(embedding, "fsdp", axis=1, tiled=True)
    conv = lax.all_gather(conv_weight, "fsdp", axis=1, tiled=True)
    bias = lax.all_gather(conv_bias, "fsdp", axis=0, tiled=True)
    score = lax.all_gather(scorer, "fsdp", axis=0, tiled=True)
    vocab, width = emb.shape
    count = lax.psum(jnp.sum(pad_mask.astype(F32)), ("fsdp", "dp"))
    table = jnp.einsum("kcd,vc->dkv", conv, emb, preferred_element_type=F32).reshape(width, TAPS * vocab)
    score32 = score.astype(F32)
    q_table = jnp.sum(table * score32[:, None], axis=0, keepdims=True)
    tq = jnp.concatenate([split3_rows(q_table), jnp.zeros((13, TAPS * vocab), BF16)], axis=0)
    bias32 = bias.astype(F32)
    small = jnp.stack([jnp.full((128,), count), jnp.full((128,), jnp.sum(bias32 * score32))])
    small = jnp.concatenate([small, jnp.zeros((6, 128), F32)], axis=0)
    blocks, grad, part = main_call(
        doc_lengths, aux_weight.reshape(1, 1), small, byte_ids, pad_mask, table.astype(BF16), tq, bias32[:, None], score[None, :], cotangent
    )
    grad = lax.psum(grad, ("fsdp", "dp")).reshape(TAPS, vocab, width)
    score_grad = lax.psum(part[0], ("fsdp", "dp"))
    loss = lax.psum(part[1, 0], ("fsdp", "dp")) / count
    size = embedding.shape[1]
    at = lax.axis_index("fsdp") * size
    bias_grad = lax.dynamic_slice_in_dim(jnp.sum(grad[TAPS // 2], axis=0), at, size, 0)
    score_grad = lax.dynamic_slice_in_dim(score_grad, at, size, 0)
    conv_grad = jnp.einsum("vc,kvd->kcd", embedding.astype(F32), grad, precision=lax.Precision.HIGHEST)
    emb_grad = jnp.einsum("kvd,kcd->vc", grad, conv_weight.astype(F32), precision=lax.Precision.HIGHEST)
    return blocks, loss, emb_grad, conv_grad, bias_grad, score_grad


def solution(mesh):
    small = mesh.shape["fsdp"] == 8 and mesh.shape["dp"] == 4
    return jax.shard_map(
        step_shards if small else gathered_shards,
        mesh=mesh,
        in_specs=(
            P(("fsdp", "dp"), None),
            P(("fsdp", "dp"), None),
            P(("fsdp", "dp"), None),
            P(None, "fsdp"),
            P(None, "fsdp", None),
            P("fsdp"),
            P("fsdp"),
            P(("fsdp", "dp"), None, None),
            P(),
        ),
        out_specs=(
            P(("fsdp", "dp"), None, None),
            P(),
            P(None, "fsdp"),
            P(None, "fsdp", None),
            P("fsdp"),
            P("fsdp"),
        ),
        check_vma=False,
    )
```
